1024 devices in a mesh: face: 32 (over z_lo, y, core), tile: 32 (over x, z_hi).
Axes of the slice: x: 8, y: 8, z: 8 (z_hi: 4, z_lo: 2; z = z_hi * 2 + z_lo), core: 2. Of those that a mesh axis runs over, the one named last changes fastest.
Arguments:
- adjoint_end: float32 [2, 36, 512, 4096], P(None, None, 'face', 'tile'), may hold values from -6 to 6
- stored_rows: bfloat16 [32, 3072, 2, 36, 128], P('face', 'tile'), may hold values from -2.5 to 2.5
- stored_owner: int32 [32, 3072], P('face', 'tile'), may hold values from 0 to 31, as said below
- stored_unit: int32 [32, 3072], P('face', 'tile'), may hold values from 0 to 47
- stored_valid: int32 [32, 3072], P('face', 'tile'), may hold values from 0 to 1
- edge_match: int32 [32, 32], P('face', 'tile'), may hold values from 0 to 31, as said below
- edge_turn: int32 [32, 32], P('face', 'tile'), may hold values from 0 to 1
Outputs:
- adjoint_start: float32 [2, 36, 512, 4096], P(None, None, 'face', 'tile')
The draws below stay inside these ranges and needn't reach their ends.
Inputs may be any that keep to these rules, and one draw needn't show every extreme that they name: `stored_owner`: in each face row the valid slots of all holders name every unit of every owner exactly once; one holder has at most 3 valid slots for one owner, and every owner's own holder has exactly 3 for it. For each tile index, edge_match over the face rows is a permutation.
All inputs are finite; a program needn't handle non-finite values.
Results may differ from the reference program's by a relative error of at most 0.0003.
Values may be sent and summed in bfloat16 or wider, within the bound.
No kernel may reach another device: no remote copies, remote signals or barrier semaphores. Data moves between devices by JAX's collectives and lax.ppermute only.
A program may use at most 32 MiB of HBM per device.

```python
import jax
import jax.numpy as jnp
from jax import lax

LEVELS = 36
TILE_ROWS = 16
TILE_COLS = 128
STEPS = 3
UNITS = 48
CAPACITY = 3
SLOTS = 96
NX = 512
NY = 4096
N_FACE = 32
N_TILE = 32


def checkpoint_layout(key):
    base_key = jax.random.fold_in(key, 11)
    owner_keys = jax.random.split(jax.random.fold_in(base_key, 1), N_FACE * N_TILE)

    def owner_layout(owner_key):
        spread = jax.random.permutation(owner_key, (N_TILE - 1) * CAPACITY)[:UNITS - CAPACITY].astype(jnp.int32) + CAPACITY
        places = jnp.concatenate([jnp.arange(CAPACITY, dtype=jnp.int32), spread])
        return jnp.full((SLOTS,), -1, jnp.int32).at[places].set(jnp.arange(UNITS, dtype=jnp.int32))
    unit_at = jax.vmap(owner_layout)(owner_keys).reshape(N_FACE, N_TILE, SLOTS)
    holder = jnp.arange(N_TILE, dtype=jnp.int32)[:, None]
    virtual = jnp.arange(SLOTS, dtype=jnp.int32)[None, :]
    owner_of = (holder - virtual // CAPACITY) % N_TILE
    held_unit = unit_at[:, owner_of, jnp.broadcast_to(virtual, owner_of.shape)]
    shuffle_keys = jax.random.split(jax.random.fold_in(base_key, 2), N_FACE * N_TILE)

    def shuffle_one(shuffle_key):
        return jax.random.permutation(shuffle_key, SLOTS)
    slot_order = jax.vmap(shuffle_one)(shuffle_keys).reshape(N_FACE, N_TILE, SLOTS).astype(jnp.int32)
    owner_tile = jnp.take_along_axis(jnp.broadcast_to(owner_of[None], (N_FACE, N_TILE, SLOTS)), slot_order, axis=2)
    unit_ids = jnp.take_along_axis(held_unit, slot_order, axis=2)
    live_slot = (unit_ids >= 0).astype(jnp.int32)
    filler = jax.random.randint(jax.random.fold_in(base_key, 3), unit_ids.shape, 0, UNITS, dtype=jnp.int32)
    unit_ids = jnp.where(live_slot == 1, unit_ids, filler)
    flat = (N_FACE, N_TILE * SLOTS)
    return (owner_tile.reshape(flat), unit_ids.reshape(flat), live_slot.reshape(flat))


def draw_stored_owner(key, part):
    return checkpoint_layout(key)[0]


def draw_stored_unit(key, part):
    return checkpoint_layout(key)[1]


def draw_stored_valid(key, part):
    return checkpoint_layout(key)[2]


def draw_edge_match(key, part):
    column_keys = jax.random.split(jax.random.fold_in(key, 23), N_TILE)

    def column_perm(column_key):
        return jax.random.permutation(column_key, N_FACE)
    return jnp.transpose(jax.vmap(column_perm)(column_keys)).astype(jnp.int32)


def plant(entries, own_key, least, high):
    longest = entries.shape.index(max(entries.shape))
    spots = []
    for shift in (0, 1):
        where = [jax.random.randint(jax.random.fold_in(own_key, axis), (), 0, length) for axis, length in enumerate(entries.shape)]
        where[longest] = (where[longest] + shift) % entries.shape[longest]
        spots.append(tuple(where))
    return entries.at[spots[0]].set(least).at[spots[1]].set(high)


def shard_levels(rng, dims, cuts, smallest, largest):
    def one(axis_at, shards_of):
        draws = jax.random.uniform(jax.random.fold_in(jax.random.fold_in(rng, 6), axis_at), (shards_of,), jnp.float32, smallest / len(cuts), largest / len(cuts))
        return jnp.repeat(jnp.exp(draws), dims[axis_at] // shards_of).reshape((-1,) + (1,) * (len(dims) - axis_at - 1))

    loudness = one(*cuts[0])
    for cut in cuts[1:]:
        loudness = loudness * one(*cut)
    return loudness


def normal_values(own_key, shape, width, most, pieces=(), held_as=jnp.bfloat16):
    drawn = jax.random.normal(own_key, shape, jnp.float32) * width
    if len(pieces) > 0:
        drawn = shard_levels(own_key, shape, pieces, -0.22, 0.18) * drawn
    return jnp.clip(drawn, min=-most, max=most).astype(held_as)


def setup_inputs(seed: int = 0) -> dict:
    keys = jax.random.split(jax.random.key(seed), 8)
    return {
        "adjoint_end": normal_values(keys[0], (2, LEVELS, NX, NY), 1.0, 6.0, ((2, 32), (3, 32)), jnp.float32),
        "stored_rows": normal_values(keys[1], (N_FACE, N_TILE * SLOTS, 2, LEVELS, TILE_COLS), 0.8, 2.5, ((0, 32), (1, 32))),
        "stored_owner": draw_stored_owner(jax.random.fold_in(keys[7], 71), 0),
        "stored_unit": draw_stored_unit(jax.random.fold_in(keys[7], 71), 0),
        "stored_valid": draw_stored_valid(jax.random.fold_in(keys[7], 71), 0),
        "edge_match": draw_edge_match(jax.random.fold_in(keys[7], 71), 0),
        "edge_turn": plant(jax.random.randint(keys[6], (N_FACE, N_TILE), 0, 2), jax.random.fold_in(keys[6], 1), 0, 1).astype(jnp.int32),
    }


courant = 0.2


def rounded(values):
    return lax.optimization_barrier(values.astype(jnp.bfloat16)).astype(jnp.float32)


def flipped(values, turned):
    return jnp.where(turned[:, :, None] == 1, jnp.flip(values, -1), values)


def pick_rows(values, index):
    shaped = index.reshape((1,) * (values.ndim - 3) + index.shape + (1,))
    return jnp.take_along_axis(values, jnp.broadcast_to(shaped, values.shape), axis=values.ndim - 3)


def adjoint_update(adjoint, north_values, south_values, western, eastern, wind_west, wind_east, wind_north, wind_south):
    result = adjoint + courant * jnp.minimum(wind_west, 0.0) * (adjoint - western)
    result = result + courant * jnp.maximum(wind_east, 0.0) * (eastern - adjoint)
    result = result + courant * jnp.minimum(wind_north, 0.0) * (adjoint - north_values)
    result = result + courant * jnp.maximum(wind_south, 0.0) * (south_values - adjoint)
    return result


def reference(adjoint_end, stored_rows, stored_owner, stored_unit, stored_valid, edge_match, edge_turn):
    target = jnp.where(stored_valid == 1, stored_unit, UNITS).astype(jnp.int32)
    face_index = jnp.arange(N_FACE, dtype=jnp.int32)[:, None]
    face_winds = jnp.zeros((N_FACE, N_TILE, UNITS, 2, LEVELS, TILE_COLS), jnp.bfloat16)
    face_winds = face_winds.at[face_index, stored_owner, target].set(stored_rows, mode="drop")
    face_winds = face_winds.reshape(N_FACE, N_TILE, STEPS, TILE_ROWS, 2, LEVELS, TILE_COLS)
    below_face = jnp.argsort(edge_match, axis=0).astype(jnp.int32)
    below_turn = jnp.take_along_axis(edge_turn, below_face, axis=0)
    adjoint = adjoint_end
    for time_step in reversed(range(STEPS)):
        step_winds = face_winds[:, :, time_step].astype(jnp.float32)
        west_blocks = jnp.transpose(step_winds[:, :, :, 0], (3, 0, 2, 1, 4))
        north_blocks = jnp.transpose(step_winds[:, :, :, 1], (3, 0, 2, 1, 4))
        blocks = adjoint.reshape(2, LEVELS, N_FACE, TILE_ROWS, N_TILE, TILE_COLS)
        last_rows = rounded(blocks[:, :, :, TILE_ROWS - 1])
        first_rows = rounded(blocks[:, :, :, 0])
        upper_edge = flipped(pick_rows(last_rows, edge_match), edge_turn)
        lower_edge = flipped(pick_rows(first_rows, below_face), below_turn)
        north_values = jnp.concatenate([upper_edge[:, :, :, None], blocks[:, :, :, :-1]], axis=3)
        south_values = jnp.concatenate([blocks[:, :, :, 1:], lower_edge[:, :, :, None]], axis=3)
        south_edge = flipped(pick_rows(north_blocks[:, :, 0], below_face), below_turn)
        south_blocks = jnp.concatenate([north_blocks[:, :, 1:], south_edge[:, :, None]], axis=2)
        wind_west = west_blocks.reshape(LEVELS, NX, NY)
        wind_east = jnp.roll(wind_west, -1, axis=-1)
        western = jnp.roll(adjoint, 1, axis=-1)
        eastern = jnp.roll(adjoint, -1, axis=-1)
        adjoint = adjoint_update(adjoint, north_values.reshape(adjoint.shape), south_values.reshape(adjoint.shape), western, eastern, wind_west, wind_east, north_blocks.reshape(LEVELS, NX, NY), south_blocks.reshape(LEVELS, NX, NY))
    return adjoint
```

```python
import functools

import jax
import jax.numpy as jnp
from jax import lax
from jax.experimental import pallas as pl
from jax.experimental.pallas import tpu as pltpu
from jax.sharding import Mesh
from jax.sharding import PartitionSpec as P

STEPS = 3
COURANT = 0.2
PAD = 40
LABEL, LABEL_EAST = 64, 65
INTERPRET = False

VM = pl.BlockSpec(memory_space=pltpu.VMEM)
SM = pl.BlockSpec(memory_space=pltpu.SMEM)
F32, BF16 = jnp.float32, jnp.bfloat16


def call(kernel, out_shape, in_specs, out_specs, scratch=(), flops=1 << 20, moved=1 << 20):
    return pl.pallas_call(
        kernel,
        out_shape=out_shape,
        in_specs=in_specs,
        out_specs=out_specs,
        scratch_shapes=list(scratch),
        compiler_params=pltpu.CompilerParams(vmem_limit_bytes=40 << 20),
        cost_estimate=pl.CostEstimate(flops=flops, bytes_accessed=moved, transcendentals=0),
        interpret=INTERPRET,
    )


def lanes(rows, width):
    return lax.broadcasted_iota(jnp.int32, (rows, width), 1)


def spread(values, lane, shape):
    return jnp.broadcast_to(values[:, lane : lane + 1], shape)


def pack_kernel(levels, step_unit, owner, unit, valid, rows, out, mini, count, source, label, first, flat):
    slots, width = rows.shape[0], rows.shape[3]
    tiles = mini.shape[0]
    capacity = slots // tiles

    def clear(i, c):
        count[i] = 0
        first[i] = -1
        return c

    lax.fori_loop(0, tiles, clear, 0)

    def blank(i, c):
        source[i] = 0
        label[i] = -1
        return c

    lax.fori_loop(0, slots, blank, 0)

    def place(s, c):
        @pl.when(valid[0, s] == 1)
        def _():
            o, u = owner[0, s], unit[0, s]
            p = o * capacity + count[o]
            source[p] = s
            label[p] = u
            count[o] = count[o] + 1

            @pl.when(u == step_unit)
            def _():
                first[o] = s

        return c

    lax.fori_loop(0, slots, place, 0)

    lane = lanes(levels, width)

    def column(s, held):
        v = rows[s, 0].astype(F32)
        return jnp.where(lane == s, spread(v, 0, v.shape), held)

    held = lax.fori_loop(0, slots, column, jnp.zeros((levels, width), F32), unroll=8)
    flat[...] = jnp.zeros_like(flat)
    flat[0:levels, :] = held
    flat[...] = flat[...].T

    extra_lane = lanes(1, width)
    zeros = jnp.zeros((PAD - levels, width), BF16)

    def fill(p, c):
        s = source[p]
        q = jnp.where(p + capacity >= slots, p + capacity - slots, p + capacity)
        out[p, 0, 0:levels, :] = rows[s, 0]
        out[p, 1, 0:levels, :] = rows[s, 1]
        extra = flat[pl.ds(source[q], 1), :]
        extra = jnp.where(extra_lane == LABEL, label[p].astype(F32), extra)
        extra = jnp.where(extra_lane == LABEL_EAST, label[q].astype(F32), extra)
        out[p, 0, levels:PAD, :] = jnp.broadcast_to(extra, zeros.shape).astype(BF16)
        out[p, 1, levels:PAD, :] = zeros
        return c

    lax.fori_loop(0, slots, fill, 0, unroll=2)

    def fill_mini(o, c):
        s = first[o]
        mini[o, 0:levels, :] = rows[jnp.maximum(s, 0), 1]
        flag = jnp.where(s >= 0, 1.0, 0.0)
        mini[o, levels:PAD, :] = jnp.full(zeros.shape, flag, F32).astype(BF16)
        return c

    lax.fori_loop(0, tiles, fill_mini, 0, unroll=2)


def edges_kernel(levels, row_count, field_stride, adj, turned, item, sides):
    width = adj.shape[1]
    lane = lanes(PAD, width)
    last = jnp.zeros((PAD, width), F32)
    head = jnp.zeros((PAD, width), F32)
    for r in range(row_count):
        for f in range(2):
            for l0 in range(0, levels, 8):
                n = min(8, levels - l0)
                turned[r, f, l0 : l0 + n, :] = adj[pl.ds((f * levels + l0) * row_count + r, n, stride=row_count), :]
            turned[r, f, levels:PAD, :] = jnp.zeros((PAD - levels, width), F32)
            v = turned[r, f]
            q = r * 2 + f
            last = jnp.where(lane == q, spread(v, width - 1, v.shape), last)
            head = jnp.where(lane == q, spread(v, 0, v.shape), head)
            if r == 0:
                item[f] = v.astype(BF16)
            if r == row_count - 1:
                item[2 + f] = v.astype(BF16)
    sides[0] = last
    sides[1] = head


def join_kernel(levels, mini, edge, item):
    holders = mini.shape[0]

    def pick(h, total):
        v = mini[h].astype(F32)
        flag = jnp.broadcast_to(v[levels : levels + 1, :], v.shape)
        return jnp.where(flag > 0.5, v, total)

    wind = lax.fori_loop(0, holders, pick, jnp.zeros(mini.shape[1:], F32), unroll=4)
    item[0] = edge[0]
    item[1] = edge[1]
    item[2] = wind.astype(BF16)
    item[3] = edge[2]
    item[4] = edge[3]


def invert(code, inverse):
    def one(f, c):
        inverse[lax.shift_right_logical(code[0, f], 1)] = f
        return c

    lax.fori_loop(0, code.shape[1], one, 0)


def choose_kernel(sizes, code, where, gathered, out, inverse):
    _, ny, nc = sizes
    invert(code, inverse)
    zl, c = where[0, 0], where[0, 2]
    for y in range(ny):
        dest = (zl * ny + y) * nc + c
        for source, a, b in (
            (inverse[dest], 0, 3),
            (lax.shift_right_logical(code[0, dest], 1), 3, 5),
        ):
            group = (source // (ny * nc)) * nc + source % nc
            for i in range(a, b):
                out[y, i] = gathered[group, i]


def neighbours(sizes, code, where, inverse):
    _, ny, nc = sizes
    invert(code, inverse)
    me = (where[0, 0] * ny + where[0, 1]) * nc + where[0, 2]
    north, south = lax.shift_right_logical(code[0, me], 1), inverse[me]
    return (north // nc) % ny, code[0, me] & 1, (south // nc) % ny, code[0, south] & 1


def oriented(block, turn):
    n, rows, width = block.shape
    i = lax.broadcasted_iota(jnp.int32, (width, width), 0)
    j = lax.broadcasted_iota(jnp.int32, (width, width), 1)
    source = jnp.where(turn == 1, width - 1 - j, j)
    matrix = jnp.where(i == source, 1.0, 0.0).astype(BF16)
    out = jnp.dot(block.reshape(n * rows, width), matrix, preferred_element_type=F32)
    return out.reshape(n, rows, width)


def step_kernel(step, levels, row_count, sizes, *refs):
    opening, closing = step == STEPS - 1, step == 0
    refs = list(refs)
    code, where = refs.pop(0), refs.pop(0)
    if not opening:
        found = refs.pop(0)
    winds, adj, edge, from_west, from_east = (refs.pop(0) for _ in range(5))
    if not opening:
        east_wind = refs.pop(0)
    out = refs.pop(0)
    if not closing:
        item, sides = refs.pop(0), refs.pop(0)
    if opening:
        found_out, east_wind = refs.pop(0), refs.pop(0)
    inverse = refs.pop(0)
    if opening:
        found, sem = refs.pop(0), refs.pop(0)
    width = adj.shape[3]
    slots = winds.shape[0]

    if opening:
        extra = winds[:, 0, PAD - 8 : PAD, :].astype(F32).reshape(slots * 8, width)
        row = lax.broadcasted_iota(jnp.int32, extra.shape, 0)
        ours = (row & 7) == levels - (PAD - 8)
        lane = lanes(slots * 8, width).astype(F32)
        here = ours & (spread(extra, LABEL, extra.shape) == lane)
        there = ours & (spread(extra, LABEL_EAST, extra.shape) == lane)
        slot = lax.shift_right_logical(row, 3).astype(F32)
        index = jnp.sum(jnp.where(here, slot, 0.0), axis=0, keepdims=True)
        found_out[...] = index.astype(jnp.int32)
        copy = pltpu.make_async_copy(found_out, found, sem)
        copy.start()
        columns = lax.dot_general(
            jnp.where(ours, extra, 0.0).astype(BF16),
            jnp.where(there, 1.0, 0.0).astype(BF16),
            (((0,), (0,)), ((), ())),
            preferred_element_type=F32,
        )
        east_wind[...] = columns[0:PAD, :]
        copy.wait()

    y_north, turn_north, y_south, turn_south = neighbours(sizes, code, where, inverse)
    upper = oriented(edge[y_north, 3:5], turn_north)
    lower = oriented(edge[y_south, 0:3], turn_south)

    lane = lanes(PAD, width)
    last = jnp.zeros((PAD, width), F32)
    head = jnp.zeros((PAD, width), F32)
    base = step * row_count
    north_wind = winds[found[0, base], 1].astype(F32)
    for r in range(row_count):
        west_wind = winds[found[0, base + r], 0].astype(F32)
        if r + 1 < row_count:
            south_wind = winds[found[0, base + r + 1], 1].astype(F32)
        else:
            south_wind = lower[2]
        u = base + r
        eastern_wind = jnp.where(
            lane == width - 1, spread(east_wind, u, lane.shape), pltpu.roll(west_wind, width - 1, 1)
        )
        cw = COURANT * jnp.minimum(west_wind, 0.0)
        ce = COURANT * jnp.maximum(eastern_wind, 0.0)
        cn = COURANT * jnp.minimum(north_wind, 0.0)
        cs = COURANT * jnp.maximum(south_wind, 0.0)
        for f in range(2):
            q = r * 2 + f
            a = adj[r, f]
            west = jnp.where(lane == 0, spread(from_west, q, a.shape), pltpu.roll(a, 1, 1))
            east = jnp.where(lane == width - 1, spread(from_east, q, a.shape), pltpu.roll(a, width - 1, 1))
            north = adj[r - 1, f] if r > 0 else upper[f]
            south = adj[r + 1, f] if r + 1 < row_count else lower[f]
            v = a + cw * (a - west)
            v = v + ce * (east - a)
            v = v + cn * (a - north)
            v = v + cs * (south - a)
            if closing:
                for l0 in range(0, levels, 8):
                    n = min(8, levels - l0)
                    out[pl.ds((f * levels + l0) * row_count + r, n, stride=row_count), :] = v[l0 : l0 + n]
            else:
                out[r, f] = v
                last = jnp.where(lane == q, spread(v, width - 1, v.shape), last)
                head = jnp.where(lane == q, spread(v, 0, v.shape), head)
                if r == 0:
                    item[f] = v.astype(BF16)
                if r == row_count - 1:
                    item[3 + f] = v.astype(BF16)
        north_wind = south_wind
    if not closing:
        item[2] = winds[found[0, base - row_count], 1]
        sides[0] = last
        sides[1] = head


def shards(sizes, tile_sizes, adjoint_end, stored_rows, stored_owner, stored_unit, stored_valid, edge_match, edge_turn):
    face, tile, group = ("zl", "y", "c"), ("x", "zh"), ("zl", "c")
    faces = sizes[0] * sizes[1] * sizes[2]
    tiles = tile_sizes[0] * tile_sizes[1]
    levels, row_count, width = adjoint_end.shape[1:]
    slots = stored_rows.shape[1]
    sds = jax.ShapeDtypeStruct

    where = jnp.stack([lax.axis_index(a) for a in face]).astype(jnp.int32).reshape(1, 3)
    code = edge_match * 2 + edge_turn
    code = lax.all_to_all(jnp.broadcast_to(code, (faces, 1)), face, 0, 0, tiled=True).reshape(1, faces)

    payload, mini = call(
        functools.partial(pack_kernel, levels, (STEPS - 1) * row_count),
        (sds((slots, 2, PAD, width), BF16), sds((tiles, PAD, width), BF16)),
        [SM, SM, SM, VM],
        (VM, VM),
        [
            pltpu.SMEM((tiles,), jnp.int32),
            pltpu.SMEM((slots,), jnp.int32),
            pltpu.SMEM((slots,), jnp.int32),
            pltpu.SMEM((tiles,), jnp.int32),
            pltpu.VMEM((width, width), F32),
        ],
    )(stored_owner, stored_unit, stored_valid, stored_rows[0])
    mini = lax.all_to_all(mini, tile, 0, 0, tiled=True)
    winds = lax.all_to_all(payload, tile, 0, 0, tiled=True)

    turned, edge, sides = call(
        functools.partial(edges_kernel, levels, row_count, levels),
        (sds((row_count, 2, PAD, width), F32), sds((4, PAD, width), BF16), sds((2, PAD, width), F32)),
        [VM],
        (VM, VM, VM),
    )(adjoint_end.reshape(2 * levels * row_count, width))
    item = call(
        functools.partial(join_kernel, levels), sds((5, PAD, width), BF16), [VM, VM], VM
    )(mini, edge)

    def to_sides(sides):
        ahead = [(i, (i + 1) % tiles) for i in range(tiles)]
        back = [((i + 1) % tiles, i) for i in range(tiles)]
        return lax.ppermute(sides[0], tile, ahead), lax.ppermute(sides[1], tile, back)

    def exchange(item):
        gathered = lax.all_gather(item, group, axis=0, tiled=False)
        chosen = call(
            functools.partial(choose_kernel, sizes),
            sds((sizes[1],) + item.shape, BF16),
            [SM, SM, VM],
            VM,
            [pltpu.SMEM((faces,), jnp.int32)],
        )(code, where, gathered)
        return lax.all_to_all(chosen, "y", 0, 0, tiled=True)

    found = east_wind = None
    adj = turned
    for step in reversed(range(STEPS)):
        opening, closing = step == STEPS - 1, step == 0
        from_west, from_east = to_sides(sides)
        edge = exchange(item)
        if closing:
            shape, spec = [sds((2 * levels * row_count, width), F32)], [VM]
        else:
            shape = [sds(turned.shape, F32), sds((5, PAD, width), BF16), sds((2, PAD, width), F32)]
            spec = [VM] * 3
        scratch = [pltpu.SMEM((faces,), jnp.int32)]
        if opening:
            shape += [sds((1, width), jnp.int32), sds((PAD, width), F32)]
            spec += [VM, VM]
            scratch += [pltpu.SMEM((1, width), jnp.int32), pltpu.SemaphoreType.DMA]
            ins, args = [SM, SM] + [VM] * 5, [code, where, winds, adj, edge, from_west, from_east]
        else:
            ins = [SM, SM, SM] + [VM] * 6
            args = [code, where, found, winds, adj, edge, from_west, from_east, east_wind]
        got = call(
            functools.partial(step_kernel, step, levels, row_count, sizes),
            tuple(shape),
            ins,
            tuple(spec),
            scratch,
        )(*args)
        if closing:
            return got[0].reshape(adjoint_end.shape)
        adj, item, sides = got[:3]
        if opening:
            found, east_wind = got[3:]


def solution(mesh, sizes=(2, 8, 2), tile_sizes=(8, 4)):
    fine = Mesh(mesh.devices.reshape(sizes + tile_sizes), ("zl", "y", "c", "x", "zh"))
    face, tile = ("zl", "y", "c"), ("x", "zh")
    placed = (
        P(None, None, face, tile),
        P(face, tile, None, None, None),
        P(face, tile),
        P(face, tile),
        P(face, tile),
        P(face, tile),
        P(face, tile),
    )
    return jax.shard_map(
        functools.partial(shards, sizes, tile_sizes),
        mesh=fine,
        in_specs=placed,
        out_specs=P(None, None, face, tile),
        check_vma=False,
    )
```

```python
import functools

import jax
import jax.numpy as jnp
from jax import lax
from jax.experimental import pallas as pl
from jax.experimental.pallas import tpu as pltpu
from jax.sharding import Mesh
from jax.sharding import PartitionSpec as P

STEPS = 3
COURANT = 0.2
PAD = 40
LABEL, LABEL_EAST = 64, 65
INTERPRET = False

VM = pl.BlockSpec(memory_space=pltpu.VMEM)
SM = pl.BlockSpec(memory_space=pltpu.SMEM)
F32, BF16 = jnp.float32, jnp.bfloat16


def call(kernel, out_shape, in_specs, out_specs, scratch=(), flops=1 << 20, moved=1 << 20):
    return pl.pallas_call(
        kernel,
        out_shape=out_shape,
        in_specs=in_specs,
        out_specs=out_specs,
        scratch_shapes=list(scratch),
        compiler_params=pltpu.CompilerParams(vmem_limit_bytes=40 << 20),
        cost_estimate=pl.CostEstimate(flops=flops, bytes_accessed=moved, transcendentals=0),
        interpret=INTERPRET,
    )


def lanes(rows, width):
    return lax.broadcasted_iota(jnp.int32, (rows, width), 1)


def spread(values, lane, shape):
    return jnp.broadcast_to(values[:, lane : lane + 1], shape)


def pack_kernel(levels, tiles, owner, unit, valid, rows, out, count, source, label, flat):
    slots, width = rows.shape[0], rows.shape[3]
    capacity = slots // tiles

    def clear(i, c):
        count[i] = 0
        return c

    lax.fori_loop(0, tiles, clear, 0, unroll=8)

    def blank(i, c):
        source[i] = 0
        label[i] = -1
        return c

    lax.fori_loop(0, slots, blank, 0, unroll=8)

    def place(s, c):
        @pl.when(valid[0, s] == 1)
        def _():
            o = owner[0, s]
            p = o * capacity + count[o]
            source[p] = s
            label[p] = unit[0, s]
            count[o] = count[o] + 1

        return c

    lax.fori_loop(0, slots, place, 0)

    lane = lanes(levels, width)

    def column(s, held):
        v = rows[s, 0].astype(F32)
        return jnp.where(lane == s, spread(v, 0, v.shape), held)

    held = lax.fori_loop(0, slots, column, jnp.zeros((levels, width), F32), unroll=8)
    flat[...] = jnp.zeros_like(flat)
    flat[0:levels, :] = held
    flat[...] = flat[...].T

    extra_lane = lanes(1, width)
    zeros = jnp.zeros((PAD - levels, width), BF16)

    def fill(p, c):
        s = source[p]
        q = jnp.where(p + capacity >= slots, p + capacity - slots, p + capacity)
        out[p, 0, 0:levels, :] = rows[s, 0]
        out[p, 1, 0:levels, :] = rows[s, 1]
        extra = flat[pl.ds(source[q], 1), :]
        extra = jnp.where(extra_lane == LABEL, label[p].astype(F32), extra)
        extra = jnp.where(extra_lane == LABEL_EAST, label[q].astype(F32), extra)
        out[p, 0, levels:PAD, :] = jnp.broadcast_to(extra, zeros.shape).astype(BF16)
        out[p, 1, levels:PAD, :] = zeros
        return c

    lax.fori_loop(0, slots, fill, 0, unroll=4)


def edges_kernel(levels, row_count, adj, turned, item, last_out, head_out):
    width = adj.shape[1]
    lane = lanes(PAD, width)
    last = jnp.zeros((PAD, width), F32)
    head = jnp.zeros((PAD, width), F32)
    for r in range(row_count):
        for f in range(2):
            for l0 in range(0, levels, 8):
                n = min(8, levels - l0)
                turned[r, f, l0 : l0 + n, :] = adj[pl.ds((f * levels + l0) * row_count + r, n, stride=row_count), :]
            turned[r, f, levels:PAD, :] = jnp.zeros((PAD - levels, width), F32)
            v = turned[r, f]
            q = r * 2 + f
            last = jnp.where(lane == q, spread(v, width - 1, v.shape), last)
            head = jnp.where(lane == q, spread(v, 0, v.shape), head)
            if r == 0:
                item[f] = v.astype(BF16)
            if r == row_count - 1:
                item[2 + f] = v.astype(BF16)
    last_out[...] = last
    head_out[...] = head


def invert(code, inverse):
    def one(f, c):
        inverse[lax.shift_right_logical(code[0, f], 1)] = f
        return c

    lax.fori_loop(0, code.shape[1], one, 0)


def choose_kernel(sizes, north_from, shifted, code, where, gathered, *refs):
    _, ny, nc = sizes
    outs, inverse = refs[:-1], refs[-1]
    invert(code, inverse)
    zl, y, c = where[0, 0], where[0, 1], where[0, 2]
    for d in range(ny):
        plane = lax.rem(y + d, ny) if shifted else d
        dest = (zl * ny + plane) * nc + c
        for source, a, b in (
            (inverse[dest], 0, north_from),
            (lax.shift_right_logical(code[0, dest], 1), north_from, gathered.shape[1]),
        ):
            group = (source // (ny * nc)) * nc + source % nc
            for i in range(a, b):
                if shifted:
                    outs[d][i] = gathered[group, i]
                else:
                    outs[0][d, i] = gathered[group, i]


def neighbours(sizes, shifted, code, where, inverse):
    _, ny, nc = sizes
    invert(code, inverse)
    y = where[0, 1]
    me = (where[0, 0] * ny + y) * nc + where[0, 2]
    north, south = lax.shift_right_logical(code[0, me], 1), inverse[me]
    north_plane, south_plane = (north // nc) % ny, (south // nc) % ny
    if shifted:
        north_plane, south_plane = lax.rem(y - north_plane + ny, ny), lax.rem(y - south_plane + ny, ny)
    return north_plane, code[0, me] & 1, south_plane, code[0, south] & 1


def oriented(block, turn):
    n, rows, width = block.shape
    i = lax.broadcasted_iota(jnp.int32, (width, width), 0)
    j = lax.broadcasted_iota(jnp.int32, (width, width), 1)
    source = jnp.where(turn == 1, width - 1 - j, j)
    matrix = jnp.where(i == source, 1.0, 0.0).astype(BF16)
    out = jnp.dot(block.reshape(n * rows, width), matrix, preferred_element_type=F32)
    return out.reshape(n, rows, width)


def find_slots(levels, winds, found_out, found, sem, east_wind):
    slots, width = winds.shape[0], winds.shape[3]
    extra = winds[:, 0, PAD - 8 : PAD, :].astype(F32).reshape(slots * 8, width)
    row = lax.broadcasted_iota(jnp.int32, extra.shape, 0)
    ours = (row & 7) == levels - (PAD - 8)
    lane = lanes(slots * 8, width).astype(F32)
    here = ours & (spread(extra, LABEL, extra.shape) == lane)
    there = ours & (spread(extra, LABEL_EAST, extra.shape) == lane)
    slot = lax.shift_right_logical(row, 3).astype(F32)
    index = jnp.sum(jnp.where(here, slot, 0.0), axis=0, keepdims=True)
    found_out[...] = index.astype(jnp.int32)
    copy = pltpu.make_async_copy(found_out, found, sem)
    copy.start()
    columns = lax.dot_general(
        jnp.where(ours, extra, 0.0).astype(BF16),
        jnp.where(there, 1.0, 0.0).astype(BF16),
        (((0,), (0,)), ((), ())),
        preferred_element_type=F32,
    )
    east_wind[...] = columns[0:PAD, :]
    copy.wait()


def advance(step, winds, found, east_wind, adj, final, upper, lower, south_end, from_west, from_east, put, sides):
    row_count, width = adj.shape[0], adj.shape[3]
    lane = lanes(PAD, width)
    last = jnp.zeros((PAD, width), F32)
    head = jnp.zeros((PAD, width), F32)
    base = step * row_count

    def row(r, f):
        return final[f] if final is not None and r == row_count - 1 else adj[r, f]

    north_wind = winds[found[0, base], 1].astype(F32)
    for r in range(row_count):
        west_wind = winds[found[0, base + r], 0].astype(F32)
        if r + 1 < row_count:
            south_wind = winds[found[0, base + r + 1], 1].astype(F32)
        else:
            south_wind = south_end
        eastern_wind = jnp.where(
            lane == width - 1, spread(east_wind, base + r, lane.shape), pltpu.roll(west_wind, width - 1, 1)
        )
        cw = COURANT * jnp.minimum(west_wind, 0.0)
        ce = COURANT * jnp.maximum(eastern_wind, 0.0)
        cn = COURANT * jnp.minimum(north_wind, 0.0)
        if south_wind is not None:
            cs = COURANT * jnp.maximum(south_wind, 0.0)
        for f in range(2):
            q = r * 2 + f
            a = row(r, f)
            west = jnp.where(lane == 0, spread(from_west, q, a.shape), pltpu.roll(a, 1, 1))
            east = jnp.where(lane == width - 1, spread(from_east, q, a.shape), pltpu.roll(a, width - 1, 1))
            v = a + cw * (a - west)
            v = v + ce * (east - a)
            v = v + cn * (a - (row(r - 1, f) if r > 0 else upper[f]))
            if south_wind is not None:
                v = v + cs * ((row(r + 1, f) if r + 1 < row_count else lower[f]) - a)
            put(r, f, v)
            if sides is not None:
                last = jnp.where(lane == q, spread(v, width - 1, v.shape), last)
                head = jnp.where(lane == q, spread(v, 0, v.shape), head)
        north_wind = south_wind
    if sides is not None:
        sides[0][...] = last
        sides[1][...] = head


def first_kernel(
    step, levels, sizes,
    code, where, winds, adj, edge, from_west, from_east,
    out, item, kept, last_out, head_out, found_out, east_wind,
    inverse, found, sem,
):
    row_count = adj.shape[0]
    end = row_count - 1
    find_slots(levels, winds, found_out, found, sem, east_wind)
    north, turn_north, south, turn_south = neighbours(sizes, True, code, where, inverse)
    upper = oriented(edge[north, 2:4], turn_north)
    lower = oriented(edge[south, 0:2], turn_south)

    def put(r, f, v):
        out[r, f] = v
        if r == 0:
            item[f] = v.astype(BF16)
        if r == end:
            item[4 + f] = v.astype(BF16)
            kept[9 + f] = v

    advance(step, winds, found, east_wind, adj, None, upper, None, None, from_west, from_east, put, (last_out, head_out))
    item[2] = winds[found[0, step * row_count], 1]
    item[3] = winds[found[0, (step - 1) * row_count], 1]
    kept[0:2] = upper
    kept[2:4] = lower
    kept[4:6] = adj[end]
    kept[6:8] = adj[0]
    kept[8] = winds[found[0, step * row_count], 1].astype(F32)


def mend_kernel(sizes, row_count, code, where, edge, kept, last_in, head_in, ends, last_out, head_out, inverse):
    width = kept.shape[2]
    north, turn_north, south, turn_south = neighbours(sizes, False, code, where, inverse)
    lower = oriented(edge[south, 0:4], turn_south)
    cs = COURANT * jnp.maximum(lower[2], 0.0)
    lane = lanes(PAD, width)
    last, head = last_in[...], head_in[...]
    for f in range(2):
        v = kept[9 + f] + cs * (kept[2 + f] - kept[4 + f])
        ends[f] = v
        q = 2 * (row_count - 1) + f
        last = jnp.where(lane == q, spread(v, width - 1, v.shape), last)
        head = jnp.where(lane == q, spread(v, 0, v.shape), head)
    last_out[...] = last
    head_out[...] = head
    upper = oriented(edge[north, 4:6], turn_north)
    cs = COURANT * jnp.maximum(kept[8], 0.0)
    for f in range(2):
        mine = kept[6 + f].astype(BF16).astype(F32)
        v = upper[f] + cs * (mine - kept[f])
        ends[2 + f] = v.astype(BF16).astype(F32)
        ends[4 + f] = lower[f]
    ends[6] = lower[3]


def middle_kernel(step, found, winds, adj, ends, from_west, from_east, east_wind, out, item, last_out, head_out):
    row_count = adj.shape[0]

    def put(r, f, v):
        out[r, f] = v
        if r == 0:
            item[f] = v.astype(BF16)
        if r == row_count - 1:
            item[3 + f] = v.astype(BF16)

    advance(
        step, winds, found, east_wind, adj, (ends[0], ends[1]), (ends[2], ends[3]), (ends[4], ends[5]), ends[6],
        from_west, from_east, put, (last_out, head_out),
    )
    item[2] = winds[found[0, (step - 1) * row_count], 1]


def last_kernel(
    step, levels, sizes, code, where, found, winds, adj, edge, from_west, from_east, east_wind, out, inverse
):
    row_count = adj.shape[0]
    north, turn_north, south, turn_south = neighbours(sizes, False, code, where, inverse)
    upper = oriented(edge[north, 3:5], turn_north)
    lower = oriented(edge[south, 0:3], turn_south)

    def put(r, f, v):
        for l0 in range(0, levels, 8):
            n = min(8, levels - l0)
            out[pl.ds((f * levels + l0) * row_count + r, n, stride=row_count), :] = v[l0 : l0 + n]

    advance(step, winds, found, east_wind, adj, None, upper, lower, lower[2], from_west, from_east, put, None)


def shards(sizes, tile_sizes, adjoint_end, stored_rows, stored_owner, stored_unit, stored_valid, edge_match, edge_turn):
    face, tile, group = ("zl", "y", "c"), ("x", "zh"), ("zl", "c")
    faces = sizes[0] * sizes[1] * sizes[2]
    tiles = tile_sizes[0] * tile_sizes[1]
    levels, row_count, width = adjoint_end.shape[1:]
    slots = stored_rows.shape[1]
    sds = jax.ShapeDtypeStruct
    side = sds((PAD, width), F32)

    where = jnp.stack([lax.axis_index(a) for a in face]).astype(jnp.int32).reshape(1, 3)
    code = edge_match * 2 + edge_turn
    code = lax.all_to_all(jnp.broadcast_to(code, (faces, 1)), face, 0, 0, tiled=True).reshape(1, faces)

    payload = call(
        functools.partial(pack_kernel, levels, tiles),
        sds((slots, 2, PAD, width), BF16),
        [SM, SM, SM, VM],
        VM,
        [
            pltpu.SMEM((tiles,), jnp.int32),
            pltpu.SMEM((slots,), jnp.int32),
            pltpu.SMEM((slots,), jnp.int32),
            pltpu.VMEM((width, width), F32),
        ],
    )(stored_owner, stored_unit, stored_valid, stored_rows[0])
    winds = lax.all_to_all(payload, tile, 0, 0, tiled=True)

    turned, item, *sides = call(
        functools.partial(edges_kernel, levels, row_count),
        (sds((row_count, 2, PAD, width), F32), sds((4, PAD, width), BF16), side, side),
        [VM],
        (VM,) * 4,
    )(adjoint_end.reshape(2 * levels * row_count, width))

    inverse = pltpu.SMEM((faces,), jnp.int32)
    planes = sizes[1]

    def to_sides(sides):
        ahead = [(i, (i + 1) % tiles) for i in range(tiles)]
        back = [((i + 1) % tiles, i) for i in range(tiles)]
        return lax.ppermute(sides[0], tile, ahead), lax.ppermute(sides[1], tile, back)

    def gathered(item, north_from, shifted):
        mates = lax.all_gather(item, group, axis=0, tiled=False)
        if shifted:
            shape, spec = (sds(item.shape, BF16),) * planes, (VM,) * planes
        else:
            shape, spec = sds((planes,) + item.shape, BF16), VM
        kernel = functools.partial(choose_kernel, sizes, north_from, shifted)
        return call(kernel, shape, [SM, SM, VM], spec, [inverse])(code, where, mates)

    from_west, from_east = to_sides(sides)
    parts = gathered(item, 2, True)
    moved = [parts[0]]
    for d in range(1, planes):
        moved.append(lax.ppermute(parts[d], "y", [(i, (i + d) % planes) for i in range(planes)]))
    edge = jnp.stack(moved)

    adj, item, kept, *sides, found, east_wind = call(
        functools.partial(first_kernel, STEPS - 1, levels, sizes),
        (
            sds(turned.shape, F32),
            sds((6, PAD, width), BF16),
            sds((11, PAD, width), F32),
            side,
            side,
            sds((1, width), jnp.int32),
            side,
        ),
        [SM, SM] + [VM] * 5,
        (VM,) * 7,
        [inverse, pltpu.SMEM((1, width), jnp.int32), pltpu.SemaphoreType.DMA],
    )(code, where, winds, turned, edge, from_west, from_east)

    edge = lax.all_to_all(gathered(item, 4, False), "y", 0, 0, tiled=True)
    ends, *sides = call(
        functools.partial(mend_kernel, sizes, row_count),
        (sds((7, PAD, width), F32), side, side),
        [SM, SM] + [VM] * 4,
        (VM,) * 3,
        [inverse],
    )(code, where, edge, kept, *sides)

    from_west, from_east = to_sides(sides)
    adj, item, *sides = call(
        functools.partial(middle_kernel, STEPS - 2),
        (sds(turned.shape, F32), sds((5, PAD, width), BF16), side, side),
        [SM] + [VM] * 6,
        (VM,) * 4,
    )(found, winds, adj, ends, from_west, from_east, east_wind)

    from_west, from_east = to_sides(sides)
    edge = lax.all_to_all(gathered(item, 3, False), "y", 0, 0, tiled=True)
    out = call(
        functools.partial(last_kernel, STEPS - 3, levels, sizes),
        sds((2 * levels * row_count, width), F32),
        [SM, SM, SM] + [VM] * 6,
        VM,
        [inverse],
    )(code, where, found, winds, adj, edge, from_west, from_east, east_wind)
    return out.reshape(adjoint_end.shape)


def solution(mesh, sizes=(2, 8, 2), tile_sizes=(8, 4)):
    fine = Mesh(mesh.devices.reshape(sizes + tile_sizes), ("zl", "y", "c", "x", "zh"))
    face, tile = ("zl", "y", "c"), ("x", "zh")
    placed = (
        P(None, None, face, tile),
        P(face, tile, None, None, None),
        P(face, tile),
        P(face, tile),
        P(face, tile),
        P(face, tile),
        P(face, tile),
    )
    return jax.shard_map(
        functools.partial(shards, sizes, tile_sizes),
        mesh=fine,
        in_specs=placed,
        out_specs=P(None, None, face, tile),
        check_vma=False,
    )
```

```python
import functools

import jax
import jax.numpy as jnp
from jax import lax
from jax.experimental import pallas as pl
from jax.experimental.pallas import tpu as pltpu
from jax.sharding import Mesh
from jax.sharding import PartitionSpec as P

STEPS = 3
COURANT = 0.2
PAD = 40
LABEL, LABEL_EAST = 64, 65
CHUNKS = 4
INTERPRET = False

VM = pl.BlockSpec(memory_space=pltpu.VMEM)
SM = pl.BlockSpec(memory_space=pltpu.SMEM)
HBM = pl.BlockSpec(memory_space=pltpu.HBM)
F32, BF16 = jnp.float32, jnp.bfloat16


def call(kernel, out_shape, in_specs, out_specs, scratch=(), vmem=40 << 20):
    return pl.pallas_call(
        kernel,
        out_shape=out_shape,
        in_specs=in_specs,
        out_specs=out_specs,
        scratch_shapes=list(scratch),
        compiler_params=pltpu.CompilerParams(vmem_limit_bytes=vmem),
        cost_estimate=pl.CostEstimate(flops=1 << 20, bytes_accessed=1 << 20, transcendentals=0),
        interpret=INTERPRET,
    )


def lanes(rows, width):
    return lax.broadcasted_iota(jnp.int32, (rows, width), 1)


def spread(values, lane, shape):
    return jnp.broadcast_to(values[:, lane : lane + 1], shape)


def pack_kernel(levels, tiles, owner, unit, valid, stored, sent, count, source, label, flat, rows, out, sem_in, sem_out):
    slots, width = rows.shape[0], rows.shape[3]
    fetch = pltpu.make_async_copy(stored, rows, sem_in)
    fetch.start()
    capacity = slots // tiles

    def clear(i, c):
        count[i] = 0
        return c

    lax.fori_loop(0, tiles, clear, 0, unroll=8)

    def blank(i, c):
        source[i] = 0
        label[i] = -1
        return c

    lax.fori_loop(0, slots, blank, 0, unroll=8)

    def place(s, c):
        @pl.when(valid[0, s] == 1)
        def _():
            o = owner[0, s]
            p = o * capacity + count[o]
            source[p] = s
            label[p] = unit[0, s]
            count[o] = count[o] + 1

        return c

    lax.fori_loop(0, slots, place, 0, unroll=4)
    fetch.wait()

    lane = lanes(levels, width)

    def column(s, held):
        v = rows[s, 0].astype(F32)
        return jnp.where(lane == s, spread(v, 0, v.shape), held)

    held = lax.fori_loop(0, slots, column, jnp.zeros((levels, width), F32), unroll=8)
    flat[...] = jnp.zeros_like(flat)
    flat[0:levels, :] = held
    flat[...] = flat[...].T

    extra_lane = lanes(1, width)
    zeros = jnp.zeros((PAD - levels, width), BF16)

    def fill(p, c):
        s = source[p]
        q = jnp.where(p + capacity >= slots, p + capacity - slots, p + capacity)
        out[p, 0, 0:levels, :] = rows[s, 0]
        out[p, 1, 0:levels, :] = rows[s, 1]
        extra = flat[pl.ds(source[q], 1), :]
        extra = jnp.where(extra_lane == LABEL, label[p].astype(F32), extra)
        extra = jnp.where(extra_lane == LABEL_EAST, label[q].astype(F32), extra)
        out[p, 0, levels:PAD, :] = jnp.broadcast_to(extra, zeros.shape).astype(BF16)
        out[p, 1, levels:PAD, :] = zeros
        return c

    chunk = slots // CHUNKS
    copies = []
    for i in range(CHUNKS):
        lax.fori_loop(i * chunk, (i + 1) * chunk, fill, 0, unroll=4)
        span = pl.ds(i * chunk, chunk)
        copies.append(pltpu.make_async_copy(out.at[span], sent.at[span], sem_out.at[i]))
        copies[-1].start()
    for copy in copies:
        copy.wait()


def edges_kernel(levels, row_count, adj, turned, item, last_out, head_out):
    width = adj.shape[1]
    lane = lanes(PAD, width)
    last = jnp.zeros((PAD, width), F32)
    head = jnp.zeros((PAD, width), F32)
    for r in range(row_count):
        for f in range(2):
            for l0 in range(0, levels, 8):
                n = min(8, levels - l0)
                turned[r, f, l0 : l0 + n, :] = adj[pl.ds((f * levels + l0) * row_count + r, n, stride=row_count), :]
            turned[r, f, levels:PAD, :] = jnp.zeros((PAD - levels, width), F32)
            v = turned[r, f]
            q = r * 2 + f
            last = jnp.where(lane == q, spread(v, width - 1, v.shape), last)
            head = jnp.where(lane == q, spread(v, 0, v.shape), head)
            if r == 0:
                item[f] = v.astype(BF16)
            if r == row_count - 1:
                item[2 + f] = v.astype(BF16)
    last_out[...] = last
    head_out[...] = head


def invert(code, inverse):
    def one(f, c):
        inverse[lax.shift_right_logical(code[0, f], 1)] = f
        return c

    lax.fori_loop(0, code.shape[1], one, 0)


def choose_kernel(sizes, north_from, shifted, code, where, gathered, *refs):
    _, ny, nc = sizes
    outs, inverse = refs[:-1], refs[-1]
    invert(code, inverse)
    zl, y, c = where[0, 0], where[0, 1], where[0, 2]
    for d in range(ny):
        plane = lax.rem(y + d, ny) if shifted else d
        dest = (zl * ny + plane) * nc + c
        for source, a, b in (
            (inverse[dest], 0, north_from),
            (lax.shift_right_logical(code[0, dest], 1), north_from, gathered.shape[1]),
        ):
            group = (source // (ny * nc)) * nc + source % nc
            for i in range(a, b):
                if shifted:
                    outs[d][i] = gathered[group, i]
                else:
                    outs[0][d, i] = gathered[group, i]


def neighbours(sizes, shifted, code, where, inverse):
    _, ny, nc = sizes
    invert(code, inverse)
    y = where[0, 1]
    me = (where[0, 0] * ny + y) * nc + where[0, 2]
    north, south = lax.shift_right_logical(code[0, me], 1), inverse[me]
    north_plane, south_plane = (north // nc) % ny, (south // nc) % ny
    if shifted:
        north_plane, south_plane = lax.rem(y - north_plane + ny, ny), lax.rem(y - south_plane + ny, ny)
    return north_plane, code[0, me] & 1, south_plane, code[0, south] & 1


def oriented(block, turn):
    n, rows, width = block.shape
    i = lax.broadcasted_iota(jnp.int32, (width, width), 0)
    j = lax.broadcasted_iota(jnp.int32, (width, width), 1)
    source = jnp.where(turn == 1, width - 1 - j, j)
    matrix = jnp.where(i == source, 1.0, 0.0).astype(BF16)
    out = jnp.dot(block.reshape(n * rows, width), matrix, preferred_element_type=F32)
    return out.reshape(n, rows, width)


def find_slots(levels, winds, found_out, found, sem, east_wind):
    slots, width = winds.shape[0], winds.shape[3]
    extra = winds[:, 0, PAD - 8 : PAD, :].astype(F32).reshape(slots * 8, width)
    row = lax.broadcasted_iota(jnp.int32, extra.shape, 0)
    ours = (row & 7) == levels - (PAD - 8)
    lane = lanes(slots * 8, width).astype(F32)
    here = ours & (spread(extra, LABEL, extra.shape) == lane)
    there = ours & (spread(extra, LABEL_EAST, extra.shape) == lane)
    slot = lax.shift_right_logical(row, 3).astype(F32)
    index = jnp.sum(jnp.where(here, slot, 0.0), axis=0, keepdims=True)
    found_out[...] = index.astype(jnp.int32)
    copy = pltpu.make_async_copy(found_out, found, sem)
    copy.start()
    columns = lax.dot_general(
        jnp.where(ours, extra, 0.0).astype(BF16),
        jnp.where(there, 1.0, 0.0).astype(BF16),
        (((0,), (0,)), ((), ())),
        preferred_element_type=F32,
    )
    east_wind[...] = columns[0:PAD, :]
    copy.wait()


def advance(step, winds, found, east_wind, adj, final, upper, lower, south_end, from_west, from_east, put, sides):
    row_count, width = adj.shape[0], adj.shape[3]
    lane = lanes(PAD, width)
    last = jnp.zeros((PAD, width), F32)
    head = jnp.zeros((PAD, width), F32)
    base = step * row_count

    def row(r, f):
        return final[f] if final is not None and r == row_count - 1 else adj[r, f]

    north_wind = winds[found[0, base], 1].astype(F32)
    for r in range(row_count):
        west_wind = winds[found[0, base + r], 0].astype(F32)
        if r + 1 < row_count:
            south_wind = winds[found[0, base + r + 1], 1].astype(F32)
        else:
            south_wind = south_end
        eastern_wind = jnp.where(
            lane == width - 1, spread(east_wind, base + r, lane.shape), pltpu.roll(west_wind, width - 1, 1)
        )
        cw = COURANT * jnp.minimum(west_wind, 0.0)
        ce = COURANT * jnp.maximum(eastern_wind, 0.0)
        cn = COURANT * jnp.minimum(north_wind, 0.0)
        if south_wind is not None:
            cs = COURANT * jnp.maximum(south_wind, 0.0)
        for f in range(2):
            q = r * 2 + f
            a = row(r, f)
            west = jnp.where(lane == 0, spread(from_west, q, a.shape), pltpu.roll(a, 1, 1))
            east = jnp.where(lane == width - 1, spread(from_east, q, a.shape), pltpu.roll(a, width - 1, 1))
            v = a + cw * (a - west)
            v = v + ce * (east - a)
            v = v + cn * (a - (row(r - 1, f) if r > 0 else upper[f]))
            if south_wind is not None:
                v = v + cs * ((row(r + 1, f) if r + 1 < row_count else lower[f]) - a)
            put(r, f, v)
            if sides is not None:
                last = jnp.where(lane == q, spread(v, width - 1, v.shape), last)
                head = jnp.where(lane == q, spread(v, 0, v.shape), head)
        north_wind = south_wind
    if sides is not None:
        sides[0][...] = last
        sides[1][...] = head


def first_kernel(
    step, levels, sizes,
    code, where, winds, adj, edge, from_west, from_east,
    out, item, kept, last_out, head_out, found_out, east_wind,
    inverse, found, sem,
):
    row_count = adj.shape[0]
    end = row_count - 1
    find_slots(levels, winds, found_out, found, sem, east_wind)
    north, turn_north, south, turn_south = neighbours(sizes, True, code, where, inverse)
    upper = oriented(edge[north, 2:4], turn_north)
    lower = oriented(edge[south, 0:2], turn_south)

    def put(r, f, v):
        out[r, f] = v
        if r == 0:
            item[f] = v.astype(BF16)
        if r == end:
            item[4 + f] = v.astype(BF16)
            kept[9 + f] = v

    advance(step, winds, found, east_wind, adj, None, upper, None, None, from_west, from_east, put, (last_out, head_out))
    item[2] = winds[found[0, step * row_count], 1]
    item[3] = winds[found[0, (step - 1) * row_count], 1]
    kept[0:2] = upper
    kept[2:4] = lower
    kept[4:6] = adj[end]
    kept[6:8] = adj[0]
    kept[8] = winds[found[0, step * row_count], 1].astype(F32)


def mend_kernel(sizes, row_count, code, where, edge, kept, last_in, head_in, ends, last_out, head_out, inverse):
    width = kept.shape[2]
    north, turn_north, south, turn_south = neighbours(sizes, False, code, where, inverse)
    lower = oriented(edge[south, 0:4], turn_south)
    cs = COURANT * jnp.maximum(lower[2], 0.0)
    lane = lanes(PAD, width)
    last, head = last_in[...], head_in[...]
    for f in range(2):
        v = kept[9 + f] + cs * (kept[2 + f] - kept[4 + f])
        ends[f] = v
        q = 2 * (row_count - 1) + f
        last = jnp.where(lane == q, spread(v, width - 1, v.shape), last)
        head = jnp.where(lane == q, spread(v, 0, v.shape), head)
    last_out[...] = last
    head_out[...] = head
    upper = oriented(edge[north, 4:6], turn_north)
    cs = COURANT * jnp.maximum(kept[8], 0.0)
    for f in range(2):
        mine = kept[6 + f].astype(BF16).astype(F32)
        v = upper[f] + cs * (mine - kept[f])
        ends[2 + f] = v.astype(BF16).astype(F32)
        ends[4 + f] = lower[f]
    ends[6] = lower[3]


def middle_kernel(step, found, winds, adj, ends, from_west, from_east, east_wind, out, item, last_out, head_out):
    row_count = adj.shape[0]

    def put(r, f, v):
        out[r, f] = v
        if r == 0:
            item[f] = v.astype(BF16)
        if r == row_count - 1:
            item[3 + f] = v.astype(BF16)

    advance(
        step, winds, found, east_wind, adj, (ends[0], ends[1]), (ends[2], ends[3]), (ends[4], ends[5]), ends[6],
        from_west, from_east, put, (last_out, head_out),
    )
    item[2] = winds[found[0, (step - 1) * row_count], 1]


def last_kernel(
    step, levels, sizes, code, where, found, winds, adj, edge, from_west, from_east, east_wind, out, inverse
):
    row_count = adj.shape[0]
    north, turn_north, south, turn_south = neighbours(sizes, False, code, where, inverse)
    upper = oriented(edge[north, 3:5], turn_north)
    lower = oriented(edge[south, 0:3], turn_south)

    def put(r, f, v):
        for l0 in range(0, levels, 8):
            n = min(8, levels - l0)
            out[pl.ds((f * levels + l0) * row_count + r, n, stride=row_count), :] = v[l0 : l0 + n]

    advance(step, winds, found, east_wind, adj, None, upper, lower, lower[2], from_west, from_east, put, None)


def shards(sizes, tile_sizes, adjoint_end, stored_rows, stored_owner, stored_unit, stored_valid, edge_match, edge_turn):
    face, tile, group = ("zl", "y", "c"), ("x", "zh"), ("zl", "c")
    faces = sizes[0] * sizes[1] * sizes[2]
    tiles = tile_sizes[0] * tile_sizes[1]
    levels, row_count, width = adjoint_end.shape[1:]
    slots = stored_rows.shape[1]
    sds = jax.ShapeDtypeStruct
    side = sds((PAD, width), F32)

    where = jnp.stack([lax.axis_index(a) for a in face]).astype(jnp.int32).reshape(1, 3)
    code = edge_match * 2 + edge_turn
    code = lax.all_to_all(jnp.broadcast_to(code, (faces, 1)), face, 0, 0, tiled=True).reshape(1, faces)

    payload = call(
        functools.partial(pack_kernel, levels, tiles),
        sds((slots, 2, PAD, width), BF16),
        [SM, SM, SM, HBM],
        HBM,
        [
            pltpu.SMEM((tiles,), jnp.int32),
            pltpu.SMEM((slots,), jnp.int32),
            pltpu.SMEM((slots,), jnp.int32),
            pltpu.VMEM((width, width), F32),
            pltpu.VMEM(stored_rows.shape[1:], BF16),
            pltpu.VMEM((slots, 2, PAD, width), BF16),
            pltpu.SemaphoreType.DMA,
            pltpu.SemaphoreType.DMA((CHUNKS,)),
        ],
        62 << 20,
    )(stored_owner, stored_unit, stored_valid, stored_rows[0])

    turned, item, *sides = call(
        functools.partial(edges_kernel, levels, row_count),
        (sds((row_count, 2, PAD, width), F32), sds((4, PAD, width), BF16), side, side),
        [VM],
        (VM,) * 4,
    )(adjoint_end.reshape(2 * levels * row_count, width))

    inverse = pltpu.SMEM((faces,), jnp.int32)
    planes = sizes[1]

    def to_sides(sides):
        ahead = [(i, (i + 1) % tiles) for i in range(tiles)]
        back = [((i + 1) % tiles, i) for i in range(tiles)]
        return lax.ppermute(sides[0], tile, ahead), lax.ppermute(sides[1], tile, back)

    def gather(item):
        return lax.all_gather(item, group, axis=0, tiled=False)

    def chosen(mates, north_from, shifted):
        shape_of_one = mates.shape[1:]
        if shifted:
            shape, spec = (sds(shape_of_one, BF16),) * planes, (VM,) * planes
        else:
            shape, spec = sds((planes,) + shape_of_one, BF16), VM
        kernel = functools.partial(choose_kernel, sizes, north_from, shifted)
        return call(kernel, shape, [SM, SM, VM], spec, [inverse])(code, where, mates)

    payload, mates = lax.optimization_barrier((payload, gather(item)))
    winds = lax.all_to_all(payload, tile, 0, 0, tiled=True)
    from_west, from_east = to_sides(sides)
    parts = chosen(mates, 2, True)
    moved = [parts[0]]
    for d in range(1, planes):
        moved.append(lax.ppermute(parts[d], "y", [(i, (i + d) % planes) for i in range(planes)]))
    edge = jnp.stack(moved)

    adj, item, kept, *sides, found, east_wind = call(
        functools.partial(first_kernel, STEPS - 1, levels, sizes),
        (
            sds(turned.shape, F32),
            sds((6, PAD, width), BF16),
            sds((11, PAD, width), F32),
            side,
            side,
            sds((1, width), jnp.int32),
            side,
        ),
        [SM, SM] + [VM] * 5,
        (VM,) * 7,
        [inverse, pltpu.SMEM((1, width), jnp.int32), pltpu.SemaphoreType.DMA],
    )(code, where, winds, turned, edge, from_west, from_east)

    edge = lax.all_to_all(chosen(gather(item), 4, False), "y", 0, 0, tiled=True)
    ends, *sides = call(
        functools.partial(mend_kernel, sizes, row_count),
        (sds((7, PAD, width), F32), side, side),
        [SM, SM] + [VM] * 4,
        (VM,) * 3,
        [inverse],
    )(code, where, edge, kept, *sides)

    from_west, from_east = to_sides(sides)
    adj, item, *sides = call(
        functools.partial(middle_kernel, STEPS - 2),
        (sds(turned.shape, F32), sds((5, PAD, width), BF16), side, side),
        [SM] + [VM] * 6,
        (VM,) * 4,
    )(found, winds, adj, ends, from_west, from_east, east_wind)

    from_west, from_east = to_sides(sides)
    edge = lax.all_to_all(chosen(gather(item), 3, False), "y", 0, 0, tiled=True)
    out = call(
        functools.partial(last_kernel, STEPS - 3, levels, sizes),
        sds((2 * levels * row_count, width), F32),
        [SM, SM, SM] + [VM] * 6,
        VM,
        [inverse],
    )(code, where, found, winds, adj, edge, from_west, from_east, east_wind)
    return out.reshape(adjoint_end.shape)


def solution(mesh, sizes=(2, 8, 2), tile_sizes=(8, 4)):
    fine = Mesh(mesh.devices.reshape(sizes + tile_sizes), ("zl", "y", "c", "x", "zh"))
    face, tile = ("zl", "y", "c"), ("x", "zh")
    placed = (
        P(None, None, face, tile),
        P(face, tile, None, None, None),
        P(face, tile),
        P(face, tile),
        P(face, tile),
        P(face, tile),
        P(face, tile),
    )
    return jax.shard_map(
        functools.partial(shards, sizes, tile_sizes),
        mesh=fine,
        in_specs=placed,
        out_specs=P(None, None, face, tile),
        check_vma=False,
    )
```

```python
import functools

import jax
import jax.numpy as jnp
from jax import lax
from jax.experimental import pallas as pl
from jax.experimental.pallas import tpu as pltpu
from jax.sharding import Mesh
from jax.sharding import PartitionSpec as P

STEPS = 3
ROWS = 16
COURANT = 0.2
PAD = 40
LABEL, LABEL_EAST = 64, 65
CHUNKS = 4
INTERPRET = False

VM = pl.BlockSpec(memory_space=pltpu.VMEM)
SM = pl.BlockSpec(memory_space=pltpu.SMEM)
HBM = pl.BlockSpec(memory_space=pltpu.HBM)
F32, BF16 = jnp.float32, jnp.bfloat16


def call(kernel, out_shape, in_specs, out_specs, scratch=(), vmem=24 << 20):
    return pl.pallas_call(
        kernel,
        out_shape=out_shape,
        in_specs=in_specs,
        out_specs=out_specs,
        scratch_shapes=list(scratch),
        compiler_params=pltpu.CompilerParams(vmem_limit_bytes=vmem),
        cost_estimate=pl.CostEstimate(flops=1 << 20, bytes_accessed=1 << 20, transcendentals=0),
        interpret=INTERPRET,
    )


def lanes(rows, width):
    return lax.broadcasted_iota(jnp.int32, (rows, width), 1)


def spread(values, lane, shape):
    return jnp.broadcast_to(values[:, lane : lane + 1], shape)


def pack_kernel(levels, tiles, owner, unit, valid, stored, sent, count, source, label, flat, rows, out, sem_in, sem_out):
    slots, width = rows.shape[0], rows.shape[3]
    fetch = pltpu.make_async_copy(stored, rows, sem_in)
    fetch.start()
    capacity = slots // tiles

    def clear(i, c):
        count[i] = 0
        return c

    lax.fori_loop(0, tiles, clear, 0, unroll=8)

    def blank(i, c):
        source[i] = 0
        label[i] = -1
        return c

    lax.fori_loop(0, slots, blank, 0, unroll=8)

    def place(s, c):
        @pl.when(valid[0, s] == 1)
        def _():
            o = owner[0, s]
            p = o * capacity + count[o]
            source[p] = s
            label[p] = unit[0, s]
            count[o] = count[o] + 1

        return c

    lax.fori_loop(0, slots, place, 0, unroll=4)
    fetch.wait()

    lane = lanes(levels, width)

    def column(s, held):
        v = rows[s, 0].astype(F32)
        return jnp.where(lane == s, spread(v, 0, v.shape), held)

    held = lax.fori_loop(0, slots, column, jnp.zeros((levels, width), F32), unroll=8)
    flat[...] = jnp.zeros_like(flat)
    flat[0:levels, :] = held
    flat[...] = flat[...].T

    extra_lane = lanes(1, width)
    zeros = jnp.zeros((PAD - levels, width), BF16)

    def fill(p, c):
        s = source[p]
        q = jnp.where(p + capacity >= slots, p + capacity - slots, p + capacity)
        out[p, 0, 0:levels, :] = rows[s, 0]
        out[p, 1, 0:levels, :] = rows[s, 1]
        extra = flat[pl.ds(source[q], 1), :]
        extra = jnp.where(extra_lane == LABEL, label[p].astype(F32), extra)
        extra = jnp.where(extra_lane == LABEL_EAST, label[q].astype(F32), extra)
        out[p, 0, levels:PAD, :] = jnp.broadcast_to(extra, zeros.shape).astype(BF16)
        out[p, 1, levels:PAD, :] = zeros
        return c

    chunk = slots // CHUNKS
    copies = []
    for i in range(CHUNKS):
        lax.fori_loop(i * chunk, (i + 1) * chunk, fill, 0, unroll=4)
        span = pl.ds(i * chunk, chunk)
        copies.append(pltpu.make_async_copy(out.at[span], sent.at[span], sem_out.at[i]))
        copies[-1].start()
    for copy in copies:
        copy.wait()


def edges_kernel(levels, row_count, match, turn, adj, turned, item, last_out, head_out):
    width = adj.shape[1]
    lane = lanes(PAD, width)
    last = jnp.zeros((PAD, width), F32)
    head = jnp.zeros((PAD, width), F32)
    for r in range(row_count):
        for f in range(2):
            for l0 in range(0, levels, 8):
                n = min(8, levels - l0)
                turned[r, f, l0 : l0 + n, :] = adj[pl.ds((f * levels + l0) * row_count + r, n, stride=row_count), :]
            turned[r, f, levels:PAD, :] = jnp.zeros((PAD - levels, width), F32)
            v = turned[r, f]
            q = r * 2 + f
            last = jnp.where(lane == q, spread(v, width - 1, v.shape), last)
            head = jnp.where(lane == q, spread(v, 0, v.shape), head)
            if r == 0:
                item[f] = v.astype(BF16)
            if r == row_count - 1:
                if f == 0:
                    level = lax.broadcasted_iota(jnp.int32, v.shape, 0)
                    v = jnp.where(level == levels, match[0, 0].astype(F32), v)
                    v = jnp.where(level == levels + 1, turn[0, 0].astype(F32), v)
                item[2 + f] = v.astype(BF16)
    last_out[...] = last
    head_out[...] = head


def tail(tile, levels):
    return tile[PAD - 8 : PAD, :].astype(F32)[levels - (PAD - 8) :, :]


def first_send_kernel(sizes, levels, where, mates, *outs):
    nz, ny, nc = sizes
    zl, y, c = where[0, 0], where[0, 1], where[0, 2]
    order = [(i, lax.rem(j + zl, nz)) for j in range(nz) for i in range(nc)]
    shape = mates.shape[3:]
    match = [jnp.broadcast_to(tail(mates[i, z, 2], levels)[0:1], shape) for i, z in order]
    first = [[mates[i, z, f].astype(F32) for f in range(2)] for i, z in order]
    for d, out in enumerate(outs):
        dest = ((zl * ny + lax.rem(y + d, ny)) * nc + c).astype(F32)
        for m, (i, z) in enumerate(order):
            for f in range(2):
                out[2 * m + f] = mates[i, z, 2 + f]
        for f in range(2):
            v = first[0][f]
            for m in range(1, len(order)):
                v = jnp.where(match[m] == dest, first[m][f], v)
            out[2 * len(order) + f] = v.astype(BF16)


def code_kernel(sizes, levels, where, edge, code):
    nz, ny, nc = sizes
    lane = lanes(1, code.shape[1])
    codes = jnp.zeros(code.shape, F32)
    for d in range(ny):
        plane = lax.rem(where[0, 1] - d + ny, ny)
        for m in range(nz * nc):
            t = tail(edge[d, 2 * m], levels)
            face = ((m // nc) * ny + plane) * nc + m % nc
            codes = jnp.where(lane == face, 2.0 * t[0:1] + t[1:2], codes)
    code[...] = codes.astype(jnp.int32)


def invert(sizes, code, inverse):
    def one(f, c):
        inverse[lax.shift_right_logical(code[0, f], 1)] = f
        return c

    lax.fori_loop(0, sizes[0] * sizes[1] * sizes[2], one, 0, unroll=8)


def choose_kernel(sizes, north_from, code, where, gathered, out, inverse):
    _, ny, nc = sizes
    invert(sizes, code, inverse)
    zl, c = where[0, 0], where[0, 2]
    for d in range(ny):
        dest = (zl * ny + d) * nc + c
        for source, a, b in (
            (inverse[dest], 0, north_from),
            (lax.shift_right_logical(code[0, dest], 1), north_from, gathered.shape[1]),
        ):
            group = (source // (ny * nc)) * nc + source % nc
            for i in range(a, b):
                out[d, i] = gathered[group, i]


def neighbours(sizes, code, where, inverse):
    _, ny, nc = sizes
    invert(sizes, code, inverse)
    me = (where[0, 0] * ny + where[0, 1]) * nc + where[0, 2]
    found = []
    for face, turn in ((lax.shift_right_logical(code[0, me], 1), code[0, me] & 1), (inverse[me], code[0, inverse[me]] & 1)):
        found += [(face // nc) % ny, (face // (ny * nc)) * nc + face % nc, turn]
    return found


def oriented(block, turn):
    n, rows, width = block.shape
    i = lax.broadcasted_iota(jnp.int32, (width, width), 0)
    j = lax.broadcasted_iota(jnp.int32, (width, width), 1)
    source = jnp.where(turn == 1, width - 1 - j, j)
    matrix = jnp.where(i == source, 1.0, 0.0).astype(BF16)
    out = jnp.dot(block.reshape(n * rows, width), matrix, preferred_element_type=F32)
    return out.reshape(n, rows, width)


def find_slots(levels, winds, found_out, found, sem, east_wind):
    slots, width = winds.shape[0], winds.shape[3]
    extra = winds[:, 0, PAD - 8 : PAD, :].astype(F32).reshape(slots * 8, width)
    row = lax.broadcasted_iota(jnp.int32, extra.shape, 0)
    ours = (row & 7) == levels - (PAD - 8)
    lane = lanes(slots * 8, width).astype(F32)
    here = ours & (spread(extra, LABEL, extra.shape) == lane)
    there = ours & (spread(extra, LABEL_EAST, extra.shape) == lane)
    slot = lax.shift_right_logical(row, 3).astype(F32)
    index = jnp.sum(jnp.where(here, slot, 0.0), axis=0, keepdims=True)
    found_out[...] = index.astype(jnp.int32)
    copy = pltpu.make_async_copy(found_out, found, sem)
    copy.start()
    columns = lax.dot_general(
        jnp.where(ours, extra, 0.0).astype(BF16),
        jnp.where(there, 1.0, 0.0).astype(BF16),
        (((0,), (0,)), ((), ())),
        preferred_element_type=F32,
    )
    east_wind[...] = columns[0:PAD, :]
    copy.wait()


def advance(step, rows, winds, found, east_wind, row, upper, lower, south_end, from_west, from_east, put):
    row_count, width = ROWS, winds.shape[3]
    lane = lanes(PAD, width)
    base = step * row_count

    def wind(r, i):
        return winds[found[0, base + r], i].astype(F32)

    south_wind, at = None, None
    for r in rows:
        west_wind = wind(r, 0)
        north_wind = south_wind if at == r - 1 else wind(r, 1)
        south_wind, at = (wind(r + 1, 1) if r + 1 < row_count else south_end), r
        eastern_wind = jnp.where(
            lane == width - 1, spread(east_wind, base + r, lane.shape), pltpu.roll(west_wind, width - 1, 1)
        )
        cw = COURANT * jnp.minimum(west_wind, 0.0)
        ce = COURANT * jnp.maximum(eastern_wind, 0.0)
        cn = COURANT * jnp.minimum(north_wind, 0.0)
        if south_wind is not None:
            cs = COURANT * jnp.maximum(south_wind, 0.0)
        for f in range(2):
            q = r * 2 + f
            a = row(r, f)
            west = jnp.where(lane == 0, spread(from_west, q, a.shape), pltpu.roll(a, 1, 1))
            east = jnp.where(lane == width - 1, spread(from_east, q, a.shape), pltpu.roll(a, width - 1, 1))
            v = a + cw * (a - west)
            v = v + ce * (east - a)
            v = v + cn * (a - (row(r - 1, f) if r > 0 else upper[f]))
            if south_wind is not None:
                v = v + cs * ((row(r + 1, f) if r + 1 < row_count else lower[f]) - a)
            put(r, f, v)


class Columns:
    def __init__(self, width):
        self.lane = lanes(PAD, width)
        self.last = self.head = jnp.zeros((PAD, width), F32)

    def add(self, r, f, v):
        here = self.lane == r * 2 + f
        self.last = jnp.where(here, spread(v, v.shape[1] - 1, v.shape), self.last)
        self.head = jnp.where(here, spread(v, 0, v.shape), self.head)

    def write(self, last_out, head_out):
        last_out[...] = self.last
        head_out[...] = self.head


def first_kernel(
    step, levels, sizes,
    code, where, winds, adj, edge, from_west, from_east,
    item, kept, found_out, east_wind,
    inverse, found, sem,
):
    end = adj.shape[0] - 1
    mates = sizes[0] * sizes[2]
    find_slots(levels, winds, found_out, found, sem, east_wind)
    north, north_mate, turn_north, south, _, turn_south = neighbours(sizes, code, where, inverse)
    y, ny = where[0, 1], sizes[1]
    upper = oriented(edge[lax.rem(y - north + ny, ny), pl.ds(2 * north_mate, 2)], turn_north)
    lower = oriented(edge[lax.rem(y - south + ny, ny), 2 * mates : 2 * mates + 2], turn_south)

    def put(r, f, v):
        item[f if r == 0 else 4 + f] = v.astype(BF16)
        kept[(11 if r == 0 else 9) + f] = v

    def row(r, f):
        return adj[r, f]

    advance(step, (0, end), winds, found, east_wind, row, upper, None, None, from_west, from_east, put)
    item[2] = winds[found[0, step * ROWS], 1]
    item[3] = winds[found[0, (step - 1) * ROWS], 1]
    kept[0:2] = upper
    kept[2:4] = lower
    kept[4:6] = adj[end]
    kept[6:8] = adj[0]
    kept[8] = winds[found[0, step * ROWS], 1].astype(F32)


def inner_kernel(step, first_at, last_at, replaced, found, winds, adj, ends, from_west, from_east, east_wind, out, last_out, head_out):
    row_count, width = adj.shape[0], adj.shape[3]
    columns = Columns(width)

    def put(r, f, v):
        out[r, f] = v
        columns.add(r, f, v)

    def row(r, f):
        return ends[f] if replaced and r == row_count - 1 else adj[r, f]

    rows = range(1, row_count - 1)
    advance(step, rows, winds, found, east_wind, row, None, None, None, from_west, from_east, put)
    for f in range(2):
        put(0, f, ends[first_at + f])
        put(row_count - 1, f, ends[last_at + f])
    columns.write(last_out, head_out)


def mend_kernel(sizes, row_count, code, where, edge, kept, last_in, head_in, ends, last_out, head_out, inverse):
    width = kept.shape[2]
    north, _, turn_north, south, _, turn_south = neighbours(sizes, code, where, inverse)
    lower = oriented(edge[south, 0:4], turn_south)
    cs = COURANT * jnp.maximum(lower[2], 0.0)
    columns = Columns(width)
    columns.last, columns.head = last_in[...], head_in[...]
    for f in range(2):
        v = kept[9 + f] + cs * (kept[2 + f] - kept[4 + f])
        ends[f] = v
        columns.add(row_count - 1, f, v)
    columns.write(last_out, head_out)
    upper = oriented(edge[north, 4:6], turn_north)
    cs = COURANT * jnp.maximum(kept[8], 0.0)
    for f in range(2):
        mine = kept[6 + f].astype(BF16).astype(F32)
        v = upper[f] + cs * (mine - kept[f])
        ends[2 + f] = v.astype(BF16).astype(F32)
        ends[4 + f] = lower[f]
    ends[6] = lower[3]


def middle_kernel(step, found, winds, adj, ends, from_west, from_east, east_wind, item, both):
    end = adj.shape[0] - 1

    def put(r, f, v):
        item[f if r == 0 else 3 + f] = v.astype(BF16)
        both[(2 if r == 0 else 4) + f] = v

    def row(r, f):
        return ends[f] if r == end else adj[r, f]

    advance(
        step, (0, end), winds, found, east_wind, row, (ends[2], ends[3]), (ends[4], ends[5]), ends[6],
        from_west, from_east, put,
    )
    both[0] = ends[0]
    both[1] = ends[1]
    item[2] = winds[found[0, (step - 1) * ROWS], 1]


def late_kernel(step, found, winds, adj, from_west, from_east, east_wind, out):
    rows = range(1, adj.shape[0] - 1)

    def put(r, f, v):
        out[r - 1, f] = v

    def row(r, f):
        return adj[r, f]

    advance(step, rows, winds, found, east_wind, row, None, None, None, from_west, from_east, put)


def last_kernel(
    step, levels, sizes, code, where, found, winds, adj, edge, from_west, from_east, east_wind, inner, out, inverse
):
    end = adj.shape[0] - 1
    north, _, turn_north, south, _, turn_south = neighbours(sizes, code, where, inverse)
    upper = oriented(edge[north, 3:5], turn_north)
    lower = oriented(edge[south, 0:3], turn_south)

    def put(r, f, v):
        for l0 in range(0, levels, 8):
            n = min(8, levels - l0)
            out[pl.ds((f * levels + l0) * ROWS + r, n, stride=ROWS), :] = v[l0 : l0 + n]

    def row(r, f):
        return adj[r, f]

    for r in range(1, end):
        for f in range(2):
            put(r, f, inner[r - 1, f])
    advance(step, (0, end), winds, found, east_wind, row, upper, lower, lower[2], from_west, from_east, put)


def shards(sizes, tile_sizes, adjoint_end, stored_rows, stored_owner, stored_unit, stored_valid, edge_match, edge_turn):
    face, tile, group = ("zl", "y", "c"), ("x", "zh"), ("zl", "c")
    faces = sizes[0] * sizes[1] * sizes[2]
    tiles = tile_sizes[0] * tile_sizes[1]
    levels, row_count, width = adjoint_end.shape[1:]
    slots = stored_rows.shape[1]
    sds = jax.ShapeDtypeStruct
    side = sds((PAD, width), F32)

    where = jnp.stack([lax.axis_index(a) for a in face]).astype(jnp.int32).reshape(1, 3)
    payload = call(
        functools.partial(pack_kernel, levels, tiles),
        sds((slots, 2, PAD, width), BF16),
        [SM, SM, SM, HBM],
        HBM,
        [
            pltpu.SMEM((tiles,), jnp.int32),
            pltpu.SMEM((slots,), jnp.int32),
            pltpu.SMEM((slots,), jnp.int32),
            pltpu.VMEM((width, width), F32),
            pltpu.VMEM(stored_rows.shape[1:], BF16),
            pltpu.VMEM((slots, 2, PAD, width), BF16),
            pltpu.SemaphoreType.DMA,
            pltpu.SemaphoreType.DMA((CHUNKS,)),
        ],
        62 << 20,
    )(stored_owner, stored_unit, stored_valid, stored_rows[0])

    turned, item, *sides = call(
        functools.partial(edges_kernel, levels, row_count),
        (sds((row_count, 2, PAD, width), F32), sds((4, PAD, width), BF16), side, side),
        [SM, SM, VM],
        (VM,) * 4,
    )(edge_match, edge_turn, adjoint_end.reshape(2 * levels * row_count, width))

    inverse = pltpu.SMEM((faces,), jnp.int32)
    planes, mates = sizes[1], sizes[0] * sizes[2]

    def to_sides(sides):
        ahead = [(i, (i + 1) % tiles) for i in range(tiles)]
        back = [((i + 1) % tiles, i) for i in range(tiles)]
        return lax.ppermute(sides[0], tile, ahead), lax.ppermute(sides[1], tile, back)

    def exchange(item, north_from):
        gathered = lax.all_gather(item, group, axis=0, tiled=False)
        chosen = call(
            functools.partial(choose_kernel, sizes, north_from),
            sds((planes,) + item.shape, BF16),
            [SM, SM, VM],
            VM,
            [inverse],
        )(code, where, gathered)
        return lax.all_to_all(chosen, "y", 0, 0, tiled=True)

    other = lax.ppermute(item, "zl", [(i, (i + 1) % sizes[0]) for i in range(sizes[0])])
    payload, other = lax.optimization_barrier((payload, other))
    winds = lax.all_to_all(payload, tile, 0, 0, tiled=True)
    from_west, from_east = to_sides(sides)
    near = lax.all_gather(jnp.stack([item, other]), "c", axis=0, tiled=False)
    parts = call(
        functools.partial(first_send_kernel, sizes, levels),
        (sds((2 * mates + 2, PAD, width), BF16),) * planes,
        [SM, VM],
        (VM,) * planes,
    )(where, near)
    moved = [parts[0]]
    for d in range(1, planes):
        moved.append(lax.ppermute(parts[d], "y", [(i, (i + d) % planes) for i in range(planes)]))
    edge = jnp.stack(moved)
    code = call(
        functools.partial(code_kernel, sizes, levels), sds((1, width), jnp.int32), [SM, VM], VM
    )(where, edge)

    item, kept, found, east_wind = call(
        functools.partial(first_kernel, STEPS - 1, levels, sizes),
        (sds((6, PAD, width), BF16), sds((13, PAD, width), F32), sds((1, width), jnp.int32), side),
        [SM, SM] + [VM] * 5,
        (VM,) * 4,
        [inverse, pltpu.SMEM((1, width), jnp.int32), pltpu.SemaphoreType.DMA],
    )(code, where, winds, turned, edge, from_west, from_east)
    edge = exchange(item, 4)

    def inner(step, first_at, last_at, replaced, adj, ends):
        adj, *sides = call(
            functools.partial(inner_kernel, step, first_at, last_at, replaced),
            (sds(turned.shape, F32), side, side),
            [SM] + [VM] * 6,
            (VM,) * 3,
        )(found, winds, adj, ends, from_west, from_east, east_wind)
        return adj, sides

    adj, sides = inner(STEPS - 1, 11, 9, False, turned, kept)
    ends, *sides = call(
        functools.partial(mend_kernel, sizes, row_count),
        (sds((7, PAD, width), F32), side, side),
        [SM, SM] + [VM] * 4,
        (VM,) * 3,
        [inverse],
    )(code, where, edge, kept, *sides)

    from_west, from_east = to_sides(sides)
    item, both = call(
        functools.partial(middle_kernel, STEPS - 2),
        (sds((5, PAD, width), BF16), sds((6, PAD, width), F32)),
        [SM] + [VM] * 6,
        (VM,) * 2,
    )(found, winds, adj, ends, from_west, from_east, east_wind)
    edge = exchange(item, 3)
    adj, sides = inner(STEPS - 2, 2, 4, True, adj, both)

    from_west, from_east = to_sides(sides)
    late = call(
        functools.partial(late_kernel, STEPS - 3),
        sds((row_count - 2,) + turned.shape[1:], F32),
        [SM] + [VM] * 5,
        VM,
    )(found, winds, adj, from_west, from_east, east_wind)
    out = call(
        functools.partial(last_kernel, STEPS - 3, levels, sizes),
        sds((2 * levels * row_count, width), F32),
        [SM, SM, SM] + [VM] * 7,
        VM,
        [inverse],
    )(code, where, found, winds, adj, edge, from_west, from_east, east_wind, late)
    return out.reshape(adjoint_end.shape)


def solution(mesh, sizes=(2, 8, 2), tile_sizes=(8, 4)):
    fine = Mesh(mesh.devices.reshape(sizes + tile_sizes), ("zl", "y", "c", "x", "zh"))
    face, tile = ("zl", "y", "c"), ("x", "zh")
    placed = (
        P(None, None, face, tile),
        P(face, tile, None, None, None),
        P(face, tile),
        P(face, tile),
        P(face, tile),
        P(face, tile),
        P(face, tile),
    )
    return jax.shard_map(
        functools.partial(shards, sizes, tile_sizes),
        mesh=fine,
        in_specs=placed,
        out_specs=P(None, None, face, tile),
        check_vma=False,
    )
```

```python
import functools

import jax
import jax.numpy as jnp
from jax import lax
from jax.experimental import pallas as pl
from jax.experimental.pallas import tpu as pltpu
from jax.sharding import Mesh
from jax.sharding import PartitionSpec as P

STEPS = 3
ROWS = 16
CAPACITY = 3
COURANT = 0.2
PAD = 40
LABEL, LABEL_EAST = 64, 65
CHUNKS = 4
HALF = 64
MATCH, TURN = 40, 41
EDGE_COLUMN = 32
INTERPRET = False

VM = pl.BlockSpec(memory_space=pltpu.VMEM)
SM = pl.BlockSpec(memory_space=pltpu.SMEM)
HBM = pl.BlockSpec(memory_space=pltpu.HBM)
F32, BF16 = jnp.float32, jnp.bfloat16


def call(kernel, out_shape, in_specs, out_specs, scratch=(), vmem=24 << 20):
    return pl.pallas_call(
        kernel,
        out_shape=out_shape,
        in_specs=in_specs,
        out_specs=out_specs,
        scratch_shapes=list(scratch),
        compiler_params=pltpu.CompilerParams(vmem_limit_bytes=vmem),
        cost_estimate=pl.CostEstimate(flops=1 << 20, bytes_accessed=1 << 20, transcendentals=0),
        interpret=INTERPRET,
    )


def lanes(rows, width):
    return lax.broadcasted_iota(jnp.int32, (rows, width), 1)


def spread(values, lane, shape):
    return jnp.broadcast_to(values[:, lane : lane + 1], shape)


def pack_kernel(
    levels, tiles, edge_unit, owner, unit, valid, rows, sent, count, source, label, first, flat, corner, out, sem_out
):
    slots, width = rows.shape[0], rows.shape[3]
    capacity = slots // tiles
    block = out.shape[0] // tiles
    whole = levels // 8 * 8

    def clear(i, c):
        count[i] = 0
        first[i] = -1
        return c

    lax.fori_loop(0, tiles, clear, 0, unroll=8)

    def blank(i, c):
        source[i] = 0
        label[i] = -1
        return c

    lax.fori_loop(0, slots, blank, 0, unroll=8)

    def place(s, c):
        @pl.when(valid[0, s] == 1)
        def _():
            o, u = owner[0, s], unit[0, s]
            p = o * capacity + count[o]
            source[p] = s
            label[p] = u
            count[o] = count[o] + 1

            @pl.when(u == edge_unit)
            def _():
                first[o] = s

        return c

    lax.fori_loop(0, slots, place, 0, unroll=4)

    lane = lanes(levels, width)

    def column(s, held):
        v = rows[s, 0].astype(F32)
        return jnp.where(lane == s, spread(v, 0, v.shape), held)

    def corners(o, held):
        v = rows[jnp.maximum(first[o], 0), 1].astype(F32)
        held = jnp.where(lane == o, spread(v, 0, v.shape), held)
        return jnp.where(lane == tiles + o, spread(v, width - 1, v.shape), held)

    for ref, one, n in ((flat, column, slots), (corner, corners, tiles)):
        held = lax.fori_loop(0, n, one, jnp.zeros((levels, width), F32), unroll=8)
        ref[...] = jnp.zeros_like(ref)
        ref[0:levels, :] = held
        ref[...] = ref[...].T

    extra_lane = lanes(8, width)
    extra_row = lax.broadcasted_iota(jnp.int32, (8, width), 0)

    def at(ref, i):
        return jnp.broadcast_to(ref[pl.ds(i, 1), :], (8, width))

    def fill(o, c):
        base = o * block
        east = jnp.where(o + 1 == tiles, 0, o + 1)
        west = jnp.where(o == 0, tiles - 1, o - 1)
        extra = jnp.zeros((8, width), F32)
        for i in range(capacity):
            p, q = o * capacity + i, east * capacity + i
            s = source[p]
            at_slot = base + i * (2 * levels // 8)
            for j in range(2):
                v = rows[s, j, 0:whole].astype(F32).reshape(whole // 8, 8, width)
                out[pl.ds(at_slot + j * (whole // 8), whole // 8)] = v.astype(BF16)
            rest = [rows[s, j, whole:levels].astype(F32) for j in range(2)]
            out[at_slot + 2 * whole // 8] = jnp.concatenate(rest, axis=0).astype(BF16)
            line = at(flat, source[q])
            line = jnp.where(extra_lane == LABEL, label[p].astype(F32), line)
            line = jnp.where(extra_lane == LABEL_EAST, label[q].astype(F32), line)
            extra = jnp.where(extra_row == i, line, extra)
        for i, side in ((capacity, east), (capacity + 1, west)):
            line = jnp.where(extra_lane < HALF, at(corner, side), pltpu.roll(at(corner, tiles + side), HALF, 1))
            line = jnp.where(extra_lane == width - 1, jnp.where(first[side] >= 0, 1.0, 0.0), line)
            extra = jnp.where(extra_row == i, line, extra)
        out[base + block - 1] = extra.astype(BF16)
        return c

    chunk = tiles // CHUNKS
    copies = []
    for i in range(CHUNKS):
        lax.fori_loop(i * chunk, (i + 1) * chunk, fill, 0)
        span = pl.ds(i * chunk * block, chunk * block)
        copies.append(pltpu.make_async_copy(out.at[span], sent.at[span], sem_out.at[i]))
        copies[-1].start()
    for copy in copies:
        copy.wait()


def edges_kernel(levels, row_count, match, turn, adj, turned, item, last_out, head_out):
    width = adj.shape[1]
    lane = lanes(PAD, width)
    last = jnp.zeros((PAD, width), F32)
    head = jnp.zeros((PAD, width), F32)
    for r in range(row_count):
        for f in range(2):
            for l0 in range(0, levels, 8):
                n = min(8, levels - l0)
                turned[r, f, l0 : l0 + n, :] = adj[pl.ds((f * levels + l0) * row_count + r, n, stride=row_count), :]
            turned[r, f, levels:PAD, :] = jnp.zeros((PAD - levels, width), F32)
            v = turned[r, f]
            q = r * 2 + f
            last = jnp.where(lane == q, spread(v, width - 1, v.shape), last)
            head = jnp.where(lane == q, spread(v, 0, v.shape), head)
            if r == 0:
                item[f] = v.astype(BF16)
            if r == row_count - 1:
                if f == 0:
                    level = lax.broadcasted_iota(jnp.int32, v.shape, 0)
                    v = jnp.where(level == levels, match[0, 0].astype(F32), v)
                    v = jnp.where(level == levels + 1, turn[0, 0].astype(F32), v)
                item[2 + f] = v.astype(BF16)
    for out, v in ((last_out, last), (head_out, head)):
        v = jnp.where(lane == MATCH, match[0, 0].astype(F32), v)
        out[...] = jnp.where(lane == TURN, turn[0, 0].astype(F32), v)


def tail(tile, levels):
    return tile[PAD - 8 : PAD, :].astype(F32)[levels - (PAD - 8) :, :]


def first_send_kernel(sizes, levels, where, mates, *outs):
    nz, ny, nc = sizes
    zl, y, c = where[0, 0], where[0, 1], where[0, 2]
    order = [(i, lax.rem(j + zl, nz)) for j in range(nz) for i in range(nc)]
    shape = mates.shape[3:]
    match = [jnp.broadcast_to(tail(mates[i, z, 2], levels)[0:1], shape) for i, z in order]
    first = [[mates[i, z, f].astype(F32) for f in range(2)] for i, z in order]
    for d, out in enumerate(outs):
        dest = ((zl * ny + lax.rem(y + d, ny)) * nc + c).astype(F32)
        for m, (i, z) in enumerate(order):
            for f in range(2):
                out[2 * m + f] = mates[i, z, 2 + f]
        for f in range(2):
            v = first[0][f]
            for m in range(1, len(order)):
                v = jnp.where(match[m] == dest, first[m][f], v)
            out[2 * len(order) + f] = v.astype(BF16)


def code_kernel(sizes, levels, where, edge, code, inverse):
    nz, ny, nc = sizes
    lane = lanes(1, code.shape[1])
    codes = jnp.zeros(code.shape, F32)
    south = jnp.zeros(code.shape, jnp.int32)
    for d in range(ny):
        plane = lax.rem(where[0, 1] - d + ny, ny)
        for m in range(nz * nc):
            t = tail(edge[d, 2 * m], levels)
            face = ((m // nc) * ny + plane) * nc + m % nc
            codes = jnp.where(lane == face, 2.0 * t[0:1] + t[1:2], codes)
            south = jnp.where(lane.astype(F32) == t[0:1], face, south)
    code[...] = codes.astype(jnp.int32)
    inverse[...] = south


def choose_kernel(sizes, levels, north_from, rows, code, inverse, where, gathered, out):
    _, ny, nc = sizes
    zl, c = where[0, 0], where[0, 2]
    if gathered.shape[1] > rows:
        corner = [gathered[m, rows].astype(F32) for m in range(gathered.shape[0])]
        shape = corner[0].shape
        lane = lanes(*shape)
        to = [[jnp.broadcast_to(tail(k, levels)[i : i + 1], shape) for i in range(2)] for k in corner]
    for d in range(ny):
        dest = (zl * ny + d) * nc + c
        for source, a, b in (
            (inverse[0, dest], 0, north_from),
            (lax.shift_right_logical(code[0, dest], 1), north_from, rows),
        ):
            group = (source // (ny * nc)) * nc + source % nc
            for i in range(a, b):
                out[d, i] = gathered[group, i]
        if gathered.shape[1] > rows:
            v = jnp.zeros(shape, F32)
            for k, both in zip(corner, to):
                for i in range(2):
                    hit = both[i] == dest.astype(F32)
                    v = jnp.where(hit & (lane == i), k, v)
                    v = jnp.where(hit & (lane == 2 + i), 1.0, v)
            out[d, rows] = v.astype(BF16)


def neighbours(sizes, code, inverse, where):
    _, ny, nc = sizes
    me = (where[0, 0] * ny + where[0, 1]) * nc + where[0, 2]
    south = inverse[0, me]
    found = []
    for face, turn in ((lax.shift_right_logical(code[0, me], 1), code[0, me] & 1), (south, code[0, south] & 1)):
        found += [(face // nc) % ny, (face // (ny * nc)) * nc + face % nc, turn]
    return found


def oriented(block, turn):
    n, rows, width = block.shape
    i = lax.broadcasted_iota(jnp.int32, (width, width), 0)
    j = lax.broadcasted_iota(jnp.int32, (width, width), 1)
    source = jnp.where(turn == 1, width - 1 - j, j)
    matrix = jnp.where(i == source, 1.0, 0.0).astype(BF16)
    out = jnp.dot(block.reshape(n * rows, width), matrix, preferred_element_type=F32)
    return out.reshape(n, rows, width)


def find_slots(levels, tiles, capacity, winds, found_out, found, sem, extras):
    block = winds.shape[0] // tiles
    extra = jnp.concatenate([winds[h * block + block - 1].astype(F32) for h in range(tiles)], axis=0)
    row = lax.broadcasted_iota(jnp.int32, extra.shape, 0)
    holder, at = lax.shift_right_logical(row, 3), row & 7
    lane = lanes(*extra.shape)
    here = (at < capacity) & (spread(extra, LABEL, extra.shape) == lane.astype(F32))
    there = (at < capacity) & (spread(extra, LABEL_EAST, extra.shape) == lane.astype(F32))
    sides = (at - capacity == lane - HALF) & (at >= capacity) & (at < capacity + 2)
    there = there | (sides & (spread(extra, extra.shape[1] - 1, extra.shape) > 0.5))
    place = (holder * block + at * (2 * levels // 8)).astype(F32)
    index = jnp.sum(jnp.where(here, place, 0.0), axis=0, keepdims=True)
    found_out[...] = index.astype(jnp.int32)
    copy = pltpu.make_async_copy(found_out, found, sem)
    copy.start()
    extras[...] = lax.dot_general(
        extra.astype(BF16), jnp.where(there, 1.0, 0.0).astype(BF16), (((0,), (0,)), ((), ())), preferred_element_type=F32
    )
    copy.wait()


def wind(levels, winds, found, unit, i):
    whole = levels // 8 * 8
    base = found[0, unit]
    rest = winds[base + 2 * whole // 8].astype(F32)
    if i == 1:
        rest = pltpu.roll(rest, 8 - (levels - whole), 0)
    main = winds[pl.ds(base + i * (whole // 8), whole // 8)].astype(F32).reshape(whole, rest.shape[1])
    return jnp.concatenate([main, rest], axis=0)


def advance(step, rows, levels, winds, found, east_wind, row, upper, lower, south_end, from_west, from_east, put):
    row_count, width = ROWS, winds.shape[2]
    lane = lanes(PAD, width)
    base = step * row_count

    def of(r, i):
        return wind(levels, winds, found, base + r, i)

    south_wind, at = None, None
    for r in rows:
        west_wind = of(r, 0)
        north_wind = south_wind if at == r - 1 else of(r, 1)
        south_wind, at = (of(r + 1, 1) if r + 1 < row_count else south_end), r
        eastern_wind = jnp.where(
            lane == width - 1, spread(east_wind, base + r, lane.shape), pltpu.roll(west_wind, width - 1, 1)
        )
        cw = COURANT * jnp.minimum(west_wind, 0.0)
        ce = COURANT * jnp.maximum(eastern_wind, 0.0)
        cn = COURANT * jnp.minimum(north_wind, 0.0)
        if south_wind is not None:
            cs = COURANT * jnp.maximum(south_wind, 0.0)
        for f in range(2):
            q = r * 2 + f
            a = row(r, f)
            west = jnp.where(lane == 0, spread(from_west, q, a.shape), pltpu.roll(a, 1, 1))
            east = jnp.where(lane == width - 1, spread(from_east, q, a.shape), pltpu.roll(a, width - 1, 1))
            v = a + cw * (a - west)
            v = v + ce * (east - a)
            v = v + cn * (a - (row(r - 1, f) if r > 0 else upper[f]))
            if south_wind is not None:
                v = v + cs * ((row(r + 1, f) if r + 1 < row_count else lower[f]) - a)
            put(r, f, v)


class Columns:
    def __init__(self, width):
        self.lane = lanes(PAD, width)
        self.last = self.head = jnp.zeros((PAD, width), F32)

    def add(self, r, f, v):
        here = self.lane == r * 2 + f
        self.last = jnp.where(here, spread(v, v.shape[1] - 1, v.shape), self.last)
        self.head = jnp.where(here, spread(v, 0, v.shape), self.head)

    def write(self, last_out, head_out):
        last_out[...] = self.last
        head_out[...] = self.head


def first_kernel(
    step, levels, sizes, tiles,
    code, inverse, where, winds, adj, edge, from_west, from_east,
    item, kept, found_out, east_wind,
    found, sem, extras,
):
    end, width = adj.shape[0] - 1, adj.shape[3]
    mates = sizes[0] * sizes[2]
    find_slots(levels, tiles, CAPACITY, winds, found_out, found, sem, extras)
    east_wind[...] = extras[0:PAD, :]
    north, north_mate, turn_north, south, _, turn_south = neighbours(sizes, code, inverse, where)
    y, ny = where[0, 1], sizes[1]
    upper = oriented(edge[lax.rem(y - north + ny, ny), pl.ds(2 * north_mate, 2)], turn_north)
    lower = oriented(edge[lax.rem(y - south + ny, ny), 2 * mates : 2 * mates + 2], turn_south)

    def put(r, f, v):
        item[f if r == 0 else 4 + f] = v.astype(BF16)
        kept[(11 if r == 0 else 9) + f] = v

    def row(r, f):
        return adj[r, f]

    advance(step, (0, end), levels, winds, found, east_wind, row, upper, None, None, from_west, from_east, put)
    edge_wind = wind(levels, winds, found, step * ROWS, 1)
    item[2] = edge_wind.astype(BF16)
    item[3] = wind(levels, winds, found, (step - 1) * ROWS, 1).astype(BF16)
    kept[0:2] = upper
    kept[2:4] = lower
    kept[4:6] = adj[end]
    kept[6:8] = adj[0]
    kept[8] = edge_wind

    shape = (PAD, width)
    lane, level = lanes(*shape), lax.broadcasted_iota(jnp.int32, shape, 0)
    head, last = extras[0:PAD, :], extras[HALF : HALF + PAD, :]
    turned_west = spread(from_west, TURN, shape) > 0.5
    turned_east = spread(from_east, TURN, shape) > 0.5
    west = jnp.where(turned_west, spread(head, HALF + 1, shape), spread(last, HALF + 1, shape))
    east = jnp.where(turned_east, spread(last, HALF, shape), spread(head, HALF, shape))
    v = jnp.where(lane == 0, west, jnp.where(lane == 1, east, 0.0))
    v = jnp.where(level == levels, spread(from_west, MATCH, shape), v)
    v = jnp.where(level == levels + 1, spread(from_east, MATCH, shape), v)
    item[6] = v.astype(BF16)


def inner_kernel(
    step, levels, opening, found, winds, adj, ends, from_west, from_east, east_wind, out, last_out, head_out
):
    row_count, width = adj.shape[0], adj.shape[3]
    columns = Columns(width)
    first_at, last_at = (11, 9) if opening else (2, 4)

    def put(r, f, v):
        out[r, f] = v
        columns.add(r, f, v)

    def row(r, f):
        return ends[f] if r == row_count - 1 and not opening else adj[r, f]

    rows = range(1, row_count - 1)
    advance(step, rows, levels, winds, found, east_wind, row, None, None, None, from_west, from_east, put)
    for f in range(2):
        put(0, f, ends[first_at + f])
        put(row_count - 1, f, ends[last_at + f])
    if opening:
        for f in range(2):
            v = ends[2 + f] - ends[4 + f]
            here = columns.lane == EDGE_COLUMN + f
            columns.last = jnp.where(here, spread(v, width - 1, v.shape), columns.last)
            columns.head = jnp.where(here, spread(v, 0, v.shape), columns.head)
    columns.write(last_out, head_out)


def middle_kernel(
    step, levels, sizes,
    code, inverse, where, found, winds, adj, edge, kept, from_west, from_east, east_wind,
    item, both,
):
    end = adj.shape[0] - 1
    north, _, turn_north, south, _, turn_south = neighbours(sizes, code, inverse, where)
    lower = oriented(edge[south, 0:4], turn_south)
    upper = oriented(edge[north, 4:6], turn_north)
    cs = COURANT * jnp.maximum(lower[2], 0.0)
    final = [kept[9 + f] + cs * (kept[2 + f] - kept[4 + f]) for f in range(2)]
    cs = COURANT * jnp.maximum(kept[8], 0.0)
    northern = []
    for f in range(2):
        v = upper[f] + cs * (kept[6 + f].astype(BF16).astype(F32) - kept[f])
        northern.append(v.astype(BF16).astype(F32))
    shape = final[0].shape
    lane = lanes(*shape)
    sides = []
    for i, columns in enumerate((from_west[...], from_east[...])):
        corner = jnp.zeros(shape, F32)
        for d in range(sizes[1]):
            k = edge[d, 6].astype(F32)
            corner = jnp.where(spread(k, 2 + i, shape) > 0.5, spread(k, i, shape), corner)
        cs = COURANT * jnp.maximum(corner, 0.0)
        mended = columns
        for f in range(2):
            mended = jnp.where(lane == 2 * end + f, columns + cs * spread(columns, EDGE_COLUMN + f, shape), mended)
        sides.append(mended)

    def put(r, f, v):
        item[f if r == 0 else 3 + f] = v.astype(BF16)
        both[(2 if r == 0 else 4) + f] = v

    def row(r, f):
        return final[f] if r == end else adj[r, f]

    advance(step, (0, end), levels, winds, found, east_wind, row, northern, lower, lower[3], *sides, put)
    both[0] = final[0]
    both[1] = final[1]
    item[2] = wind(levels, winds, found, (step - 1) * ROWS, 1).astype(BF16)


def late_kernel(step, levels, found, winds, adj, from_west, from_east, east_wind, out):
    rows = range(1, adj.shape[0] - 1)

    def put(r, f, v):
        out[r - 1, f] = v

    def row(r, f):
        return adj[r, f]

    advance(step, rows, levels, winds, found, east_wind, row, None, None, None, from_west, from_east, put)


def last_kernel(
    step, levels, sizes, code, inverse, where, found, winds, adj, edge, from_west, from_east, east_wind, inner, out
):
    end = adj.shape[0] - 1
    north, _, turn_north, south, _, turn_south = neighbours(sizes, code, inverse, where)
    upper = oriented(edge[north, 3:5], turn_north)
    lower = oriented(edge[south, 0:3], turn_south)

    def put(r, f, v):
        for l0 in range(0, levels, 8):
            n = min(8, levels - l0)
            out[pl.ds((f * levels + l0) * ROWS + r, n, stride=ROWS), :] = v[l0 : l0 + n]

    def row(r, f):
        return adj[r, f]

    for r in range(1, end):
        for f in range(2):
            put(r, f, inner[r - 1, f])
    advance(step, (0, end), levels, winds, found, east_wind, row, upper, lower, lower[2], from_west, from_east, put)


def shards(sizes, tile_sizes, adjoint_end, stored_rows, stored_owner, stored_unit, stored_valid, edge_match, edge_turn):
    face, tile, group = ("zl", "y", "c"), ("x", "zh"), ("zl", "c")
    faces = sizes[0] * sizes[1] * sizes[2]
    tiles = tile_sizes[0] * tile_sizes[1]
    levels, row_count, width = adjoint_end.shape[1:]
    slots = stored_rows.shape[1]
    sds = jax.ShapeDtypeStruct
    side = sds((PAD, width), F32)

    where = jnp.stack([lax.axis_index(a) for a in face]).astype(jnp.int32).reshape(1, 3)
    block = CAPACITY * 2 * levels // 8 + 1
    payload = call(
        functools.partial(pack_kernel, levels, tiles, (STEPS - 1) * row_count),
        sds((tiles * block, 8, width), BF16),
        [SM, SM, SM, VM],
        HBM,
        [
            pltpu.SMEM((tiles,), jnp.int32),
            pltpu.SMEM((slots,), jnp.int32),
            pltpu.SMEM((slots,), jnp.int32),
            pltpu.SMEM((tiles,), jnp.int32),
            pltpu.VMEM((width, width), F32),
            pltpu.VMEM((width, width), F32),
            pltpu.VMEM((tiles * block, 8, width), BF16),
            pltpu.SemaphoreType.DMA((CHUNKS,)),
        ],
        61 << 20,
    )(stored_owner, stored_unit, stored_valid, stored_rows[0])

    turned, item, *sides = call(
        functools.partial(edges_kernel, levels, row_count),
        (sds((row_count, 2, PAD, width), F32), sds((4, PAD, width), BF16), side, side),
        [SM, SM, VM],
        (VM,) * 4,
    )(edge_match, edge_turn, adjoint_end.reshape(2 * levels * row_count, width))

    planes, mates = sizes[1], sizes[0] * sizes[2]

    def to_sides(sides):
        ahead = [(i, (i + 1) % tiles) for i in range(tiles)]
        back = [((i + 1) % tiles, i) for i in range(tiles)]
        return lax.ppermute(sides[0], tile, ahead), lax.ppermute(sides[1], tile, back)

    def exchange(item, north_from, rows):
        gathered = lax.all_gather(item, group, axis=0, tiled=False)
        chosen = call(
            functools.partial(choose_kernel, sizes, levels, north_from, rows),
            sds((planes,) + item.shape, BF16),
            [SM, SM, SM, VM],
            VM,
        )(code, inverse, where, gathered)
        return lax.all_to_all(chosen, "y", 0, 0, tiled=True)

    other = lax.ppermute(item, "zl", [(i, (i + 1) % sizes[0]) for i in range(sizes[0])])
    payload, other = lax.optimization_barrier((payload, other))
    winds = lax.all_to_all(payload, tile, 0, 0, tiled=True)
    from_west, from_east = to_sides(sides)
    near = lax.all_gather(jnp.stack([item, other]), "c", axis=0, tiled=False)
    parts = call(
        functools.partial(first_send_kernel, sizes, levels),
        (sds((2 * mates + 2, PAD, width), BF16),) * planes,
        [SM, VM],
        (VM,) * planes,
    )(where, near)
    moved = [parts[0]]
    for d in range(1, planes):
        moved.append(lax.ppermute(parts[d], "y", [(i, (i + d) % planes) for i in range(planes)]))
    edge = jnp.stack(moved)
    table = sds((1, width), jnp.int32)
    code, inverse = call(
        functools.partial(code_kernel, sizes, levels), (table, table), [SM, VM], (VM, VM)
    )(where, edge)

    item, kept, found, east_wind = call(
        functools.partial(first_kernel, STEPS - 1, levels, sizes, tiles),
        (sds((7, PAD, width), BF16), sds((13, PAD, width), F32), table, side),
        [SM, SM, SM] + [VM] * 5,
        (VM,) * 4,
        [pltpu.SMEM((1, width), jnp.int32), pltpu.SemaphoreType.DMA, pltpu.VMEM((width, width), F32)],
    )(code, inverse, where, winds, turned, edge, from_west, from_east)
    edge = exchange(item, 4, 6)

    def inner(step, opening, adj, ends):
        adj, *sides = call(
            functools.partial(inner_kernel, step, levels, opening),
            (sds(turned.shape, F32), side, side),
            [SM] + [VM] * 6,
            (VM,) * 3,
        )(found, winds, adj, ends, from_west, from_east, east_wind)
        return adj, sides

    adj, sides = inner(STEPS - 1, True, turned, kept)
    from_west, from_east = to_sides(sides)
    item, both = call(
        functools.partial(middle_kernel, STEPS - 2, levels, sizes),
        (sds((5, PAD, width), BF16), sds((6, PAD, width), F32)),
        [SM] * 4 + [VM] * 7,
        (VM,) * 2,
    )(code, inverse, where, found, winds, adj, edge, kept, from_west, from_east, east_wind)
    edge = exchange(item, 3, 5)
    adj, sides = inner(STEPS - 2, False, adj, both)

    from_west, from_east = to_sides(sides)
    late = call(
        functools.partial(late_kernel, STEPS - 3, levels),
        sds((row_count - 2,) + turned.shape[1:], F32),
        [SM] + [VM] * 5,
        VM,
    )(found, winds, adj, from_west, from_east, east_wind)
    out = call(
        functools.partial(last_kernel, STEPS - 3, levels, sizes),
        sds((2 * levels * row_count, width), F32),
        [SM] * 4 + [VM] * 7,
        VM,
    )(code, inverse, where, found, winds, adj, edge, from_west, from_east, east_wind, late)
    return out.reshape(adjoint_end.shape)


def solution(mesh, sizes=(2, 8, 2), tile_sizes=(8, 4)):
    fine = Mesh(mesh.devices.reshape(sizes + tile_sizes), ("zl", "y", "c", "x", "zh"))
    face, tile = ("zl", "y", "c"), ("x", "zh")
    placed = (
        P(None, None, face, tile),
        P(face, tile, None, None, None),
        P(face, tile),
        P(face, tile),
        P(face, tile),
        P(face, tile),
        P(face, tile),
    )
    return jax.shard_map(
        functools.partial(shards, sizes, tile_sizes),
        mesh=fine,
        in_specs=placed,
        out_specs=P(None, None, face, tile),
        check_vma=False,
    )
```

```python
import functools

import jax
import jax.numpy as jnp
from jax import lax
from jax.experimental import pallas as pl
from jax.experimental.pallas import tpu as pltpu
from jax.sharding import Mesh
from jax.sharding import PartitionSpec as P

STEPS = 3
ROWS = 16
CAPACITY = 3
COURANT = 0.2
PAD = 40
LABEL, LABEL_EAST = 64, 65
CHUNKS = 4
HALF = 64
MATCH, TURN = 40, 41
EDGE_COLUMN = 32
INTERPRET = False

VM = pl.BlockSpec(memory_space=pltpu.VMEM)
SM = pl.BlockSpec(memory_space=pltpu.SMEM)
HBM = pl.BlockSpec(memory_space=pltpu.HBM)
F32, BF16 = jnp.float32, jnp.bfloat16


def call(kernel, out_shape, in_specs, out_specs, scratch=(), vmem=24 << 20):
    return pl.pallas_call(
        kernel,
        out_shape=out_shape,
        in_specs=in_specs,
        out_specs=out_specs,
        scratch_shapes=list(scratch),
        compiler_params=pltpu.CompilerParams(vmem_limit_bytes=vmem),
        cost_estimate=pl.CostEstimate(flops=1 << 20, bytes_accessed=1 << 20, transcendentals=0),
        interpret=INTERPRET,
    )


def lanes(rows, width):
    return lax.broadcasted_iota(jnp.int32, (rows, width), 1)


def spread(values, lane, shape):
    return jnp.broadcast_to(values[:, lane : lane + 1], shape)


def pack_kernel(
    levels, tiles, edge_unit, owner, unit, valid, stored, sent, count, source, label, first, flat, corner, rows, out, sem_in, sem_out
):
    fetch = pltpu.make_async_copy(stored, rows, sem_in)
    fetch.start()
    slots, width = rows.shape[0], rows.shape[3]
    capacity = slots // tiles
    block = out.shape[0] // tiles
    whole = levels // 8 * 8

    def clear(i, c):
        count[i] = 0
        first[i] = -1
        return c

    lax.fori_loop(0, tiles, clear, 0, unroll=8)

    def blank(i, c):
        source[i] = 0
        label[i] = -1
        return c

    lax.fori_loop(0, slots, blank, 0, unroll=8)

    def place(s, c):
        o, u, v = owner[0, s], unit[0, s], valid[0, s]
        have = count[o]
        p = jnp.where(v == 1, o * capacity + have, slots)
        source[p] = s
        label[p] = u
        count[o] = have + v
        first[jnp.where((v == 1) & (u == edge_unit), o, tiles)] = s
        return c

    lax.fori_loop(0, slots, place, 0, unroll=8)
    fetch.wait()

    lane = lanes(levels, width)

    def column(s, held):
        v = rows[s, 0].astype(F32)
        return jnp.where(lane == s, spread(v, 0, v.shape), held)

    def corners(o, held):
        v = rows[jnp.maximum(first[o], 0), 1].astype(F32)
        held = jnp.where(lane == o, spread(v, 0, v.shape), held)
        return jnp.where(lane == tiles + o, spread(v, width - 1, v.shape), held)

    for ref, one, n in ((flat, column, slots), (corner, corners, tiles)):
        held = lax.fori_loop(0, n, one, jnp.zeros((levels, width), F32), unroll=8)
        ref[...] = jnp.zeros_like(ref)
        ref[0:levels, :] = held
        ref[...] = ref[...].T

    extra_lane = lanes(8, width)
    extra_row = lax.broadcasted_iota(jnp.int32, (8, width), 0)

    def at(ref, i):
        return jnp.broadcast_to(ref[pl.ds(i, 1), :], (8, width))

    def fill(o, c):
        base = o * block
        east = jnp.where(o + 1 == tiles, 0, o + 1)
        west = jnp.where(o == 0, tiles - 1, o - 1)
        extra = jnp.zeros((8, width), F32)
        for i in range(capacity):
            p, q = o * capacity + i, east * capacity + i
            s = source[p]
            at_slot = base + i * (2 * levels // 8)
            for j in range(2):
                for k in range(whole // 8):
                    out[at_slot + j * (whole // 8) + k] = rows[s, j, 8 * k : 8 * k + 8]
            rest = [rows[s, j, whole:levels].astype(F32) for j in range(2)]
            out[at_slot + 2 * whole // 8] = jnp.concatenate(rest, axis=0).astype(BF16)
            line = at(flat, source[q])
            line = jnp.where(extra_lane == LABEL, label[p].astype(F32), line)
            line = jnp.where(extra_lane == LABEL_EAST, label[q].astype(F32), line)
            extra = jnp.where(extra_row == i, line, extra)
        for i, side in ((capacity, east), (capacity + 1, west)):
            line = jnp.where(extra_lane < HALF, at(corner, side), pltpu.roll(at(corner, tiles + side), HALF, 1))
            line = jnp.where(extra_lane == width - 1, jnp.where(first[side] >= 0, 1.0, 0.0), line)
            extra = jnp.where(extra_row == i, line, extra)
        out[base + block - 1] = extra.astype(BF16)
        return c

    chunk = tiles // CHUNKS
    copies = []
    for i in range(CHUNKS):
        lax.fori_loop(i * chunk, (i + 1) * chunk, fill, 0, unroll=2)
        span = pl.ds(i * chunk * block, chunk * block)
        copies.append(pltpu.make_async_copy(out.at[span], sent.at[span], sem_out.at[i]))
        copies[-1].start()
    for copy in copies:
        copy.wait()


def edges_kernel(levels, row_count, match, turn, adj, turned, item, last_out, head_out):
    width = adj.shape[1]
    lane = lanes(PAD, width)
    last = jnp.zeros((PAD, width), F32)
    head = jnp.zeros((PAD, width), F32)
    for r in range(row_count):
        for f in range(2):
            for l0 in range(0, levels, 8):
                n = min(8, levels - l0)
                turned[r, f, l0 : l0 + n, :] = adj[pl.ds((f * levels + l0) * row_count + r, n, stride=row_count), :]
            turned[r, f, levels:PAD, :] = jnp.zeros((PAD - levels, width), F32)
            v = turned[r, f]
            q = r * 2 + f
            last = jnp.where(lane == q, spread(v, width - 1, v.shape), last)
            head = jnp.where(lane == q, spread(v, 0, v.shape), head)
            if r == 0:
                item[f] = v.astype(BF16)
            if r == row_count - 1:
                if f == 0:
                    level = lax.broadcasted_iota(jnp.int32, v.shape, 0)
                    v = jnp.where(level == levels, match[0, 0].astype(F32), v)
                    v = jnp.where(level == levels + 1, turn[0, 0].astype(F32), v)
                item[2 + f] = v.astype(BF16)
    for out, v in ((last_out, last), (head_out, head)):
        v = jnp.where(lane == MATCH, match[0, 0].astype(F32), v)
        out[...] = jnp.where(lane == TURN, turn[0, 0].astype(F32), v)


def tail(tile, levels):
    return tile[PAD - 8 : PAD, :].astype(F32)[levels - (PAD - 8) :, :]


def first_send_kernel(sizes, levels, where, mates, *outs):
    nz, ny, nc = sizes
    zl, y, c = where[0, 0], where[0, 1], where[0, 2]
    order = [(i, lax.rem(j + zl, nz)) for j in range(nz) for i in range(nc)]
    shape = mates.shape[3:]
    match = [jnp.broadcast_to(tail(mates[i, z, 2], levels)[0:1], shape) for i, z in order]
    first = [[mates[i, z, f].astype(F32) for f in range(2)] for i, z in order]
    for d, out in enumerate(outs):
        plane = lax.rem(jnp.where(c == 0, y + d, y - d + ny), ny)
        for m, (i, z) in enumerate(order):
            for f in range(2):
                out[2 * m + f] = mates[i, z, 2 + f]
        for core in range(nc):
            dest = ((zl * ny + plane) * nc + core).astype(F32)
            for f in range(2):
                v = first[0][f]
                for m in range(1, len(order)):
                    v = jnp.where(match[m] == dest, first[m][f], v)
                out[2 * (len(order) + core) + f] = v.astype(BF16)


def code_kernel(sizes, levels, where, own, edge, code, inverse):
    nz, ny, nc = sizes
    half = ny // 2
    lane = lanes(1, code.shape[1])
    codes = jnp.zeros(code.shape, F32)
    south = jnp.zeros(code.shape, jnp.int32)
    for d in range(ny):
        plane = lax.rem(where[0, 1] - d + ny, ny)
        for m in range(nz * nc):
            t = tail(own[2 * m] if d == 0 else edge[d - 1 if d <= half else half + ny - d - 1, 2 * m], levels)
            face = ((m // nc) * ny + plane) * nc + m % nc
            codes = jnp.where(lane == face, 2.0 * t[0:1] + t[1:2], codes)
            south = jnp.where(lane.astype(F32) == t[0:1], face, south)
    code[...] = codes.astype(jnp.int32)
    inverse[...] = south


def choose_kernel(sizes, levels, north_from, rows, code, inverse, where, gathered, out):
    _, ny, nc = sizes
    zl, c = where[0, 0], where[0, 2]
    if gathered.shape[1] > rows:
        corner = [gathered[m, rows].astype(F32) for m in range(gathered.shape[0])]
        shape = corner[0].shape
        lane = lanes(*shape)
        to = [[jnp.broadcast_to(tail(k, levels)[i : i + 1], shape) for i in range(2)] for k in corner]
    for d in range(ny):
        dest = (zl * ny + d) * nc + c
        for source, a, b in (
            (inverse[0, dest], 0, north_from),
            (lax.shift_right_logical(code[0, dest], 1), north_from, rows),
        ):
            group = (source // (ny * nc)) * nc + source % nc
            for i in range(a, b):
                out[d, i] = gathered[group, i]
        if gathered.shape[1] > rows:
            v = jnp.zeros(shape, F32)
            for k, both in zip(corner, to):
                for i in range(2):
                    hit = both[i] == dest.astype(F32)
                    v = jnp.where(hit & (lane == i), k, v)
                    v = jnp.where(hit & (lane == 2 + i), 1.0, v)
            out[d, rows] = v.astype(BF16)


def neighbours(sizes, code, inverse, where):
    _, ny, nc = sizes
    me = (where[0, 0] * ny + where[0, 1]) * nc + where[0, 2]
    south = inverse[0, me]
    found = []
    for face, turn in ((lax.shift_right_logical(code[0, me], 1), code[0, me] & 1), (south, code[0, south] & 1)):
        found += [(face // nc) % ny, (face // (ny * nc)) * nc + face % nc, turn]
    return found


def oriented(block, turn):
    n, rows, width = block.shape
    i = lax.broadcasted_iota(jnp.int32, (width, width), 0)
    j = lax.broadcasted_iota(jnp.int32, (width, width), 1)
    source = jnp.where(turn == 1, width - 1 - j, j)
    matrix = jnp.where(i == source, 1.0, 0.0).astype(BF16)
    out = jnp.dot(block.reshape(n * rows, width), matrix, preferred_element_type=F32)
    return out.reshape(n, rows, width)


def find_slots(levels, tiles, capacity, winds, found_out, found, sem, extras):
    block = winds.shape[0] // tiles
    extra = jnp.concatenate([winds[h * block + block - 1].astype(F32) for h in range(tiles)], axis=0)
    row = lax.broadcasted_iota(jnp.int32, extra.shape, 0)
    holder, at = lax.shift_right_logical(row, 3), row & 7
    lane = lanes(*extra.shape)
    here = (at < capacity) & (spread(extra, LABEL, extra.shape) == lane.astype(F32))
    there = (at < capacity) & (spread(extra, LABEL_EAST, extra.shape) == lane.astype(F32))
    sides = (at - capacity == lane - HALF) & (at >= capacity) & (at < capacity + 2)
    there = there | (sides & (spread(extra, extra.shape[1] - 1, extra.shape) > 0.5))
    place = (holder * block + at * (2 * levels // 8)).astype(F32)
    index = jnp.sum(jnp.where(here, place, 0.0), axis=0, keepdims=True)
    found_out[...] = index.astype(jnp.int32)
    copy = pltpu.make_async_copy(found_out, found, sem)
    copy.start()
    extras[...] = lax.dot_general(
        extra.astype(BF16), jnp.where(there, 1.0, 0.0).astype(BF16), (((0,), (0,)), ((), ())), preferred_element_type=F32
    )
    copy.wait()


def wind(levels, winds, found, unit, i):
    whole = levels // 8 * 8
    base = found[0, unit]
    rest = winds[base + 2 * whole // 8].astype(F32)
    if i == 1:
        rest = pltpu.roll(rest, 8 - (levels - whole), 0)
    main = winds[pl.ds(base + i * (whole // 8), whole // 8)].astype(F32).reshape(whole, rest.shape[1])
    return jnp.concatenate([main, rest], axis=0)


def advance(step, rows, levels, winds, found, east_wind, row, upper, lower, south_end, from_west, from_east, put):
    row_count, width = ROWS, winds.shape[2]
    lane = lanes(PAD, width)
    base = step * row_count

    def of(r, i):
        return wind(levels, winds, found, base + r, i)

    south_wind, at = None, None
    for r in rows:
        west_wind = of(r, 0)
        north_wind = south_wind if at == r - 1 else of(r, 1)
        south_wind, at = (of(r + 1, 1) if r + 1 < row_count else south_end), r
        eastern_wind = jnp.where(
            lane == width - 1, spread(east_wind, base + r, lane.shape), pltpu.roll(west_wind, width - 1, 1)
        )
        cw = COURANT * jnp.minimum(west_wind, 0.0)
        ce = COURANT * jnp.maximum(eastern_wind, 0.0)
        cn = COURANT * jnp.minimum(north_wind, 0.0)
        if south_wind is not None:
            cs = COURANT * jnp.maximum(south_wind, 0.0)
        for f in range(2):
            q = r * 2 + f
            a = row(r, f)
            west = jnp.where(lane == 0, spread(from_west, q, a.shape), pltpu.roll(a, 1, 1))
            east = jnp.where(lane == width - 1, spread(from_east, q, a.shape), pltpu.roll(a, width - 1, 1))
            v = a + cw * (a - west)
            v = v + ce * (east - a)
            v = v + cn * (a - (row(r - 1, f) if r > 0 else upper[f]))
            if south_wind is not None:
                v = v + cs * ((row(r + 1, f) if r + 1 < row_count else lower[f]) - a)
            put(r, f, v)


class Columns:
    def __init__(self, width):
        self.lane = lanes(PAD, width)
        self.last = self.head = jnp.zeros((PAD, width), F32)

    def add(self, r, f, v):
        here = self.lane == r * 2 + f
        self.last = jnp.where(here, spread(v, v.shape[1] - 1, v.shape), self.last)
        self.head = jnp.where(here, spread(v, 0, v.shape), self.head)

    def write(self, last_out, head_out):
        last_out[...] = self.last
        head_out[...] = self.head


def first_kernel(
    step, levels, sizes, tiles,
    code, inverse, where, winds, adj, own, edge, from_west, from_east,
    item, kept, found_out, east_wind,
    found, sem, extras,
):
    end, width = adj.shape[0] - 1, adj.shape[3]
    mates = sizes[0] * sizes[2]
    find_slots(levels, tiles, CAPACITY, winds, found_out, found, sem, extras)
    east_wind[...] = extras[0:PAD, :]
    north, north_mate, turn_north, south, _, turn_south = neighbours(sizes, code, inverse, where)
    y, c, ny = where[0, 1], where[0, 2], sizes[1]
    half = ny // 2

    def arrived(plane, row):
        d = lax.rem(y - plane + ny, ny)
        i = jnp.where(d <= half, jnp.maximum(d - 1, 0), half + ny - d - 1)
        both = own[pl.ds(row, 2)].astype(F32), edge[i, pl.ds(row, 2)].astype(F32)
        return jnp.where(d == 0, *both).astype(BF16)

    upper = oriented(arrived(north, 2 * north_mate), turn_north)
    lower = oriented(arrived(south, 2 * (mates + c)), turn_south)

    def put(r, f, v):
        item[f if r == 0 else 4 + f] = v.astype(BF16)
        kept[(7 if r == 0 else 5) + f] = v

    def row(r, f):
        return adj[r, f]

    advance(step, (0, end), levels, winds, found, east_wind, row, upper, None, None, from_west, from_east, put)
    edge_wind = wind(levels, winds, found, step * ROWS, 1)
    item[2] = edge_wind.astype(BF16)
    item[3] = wind(levels, winds, found, (step - 1) * ROWS, 1).astype(BF16)
    for f in range(2):
        kept[f] = lower[f] - adj[end, f]
        kept[2 + f] = adj[0, f].astype(BF16).astype(F32) - upper[f]
    kept[4] = edge_wind

    shape = (PAD, width)
    lane, level = lanes(*shape), lax.broadcasted_iota(jnp.int32, shape, 0)
    head, last = extras[0:PAD, :], extras[HALF : HALF + PAD, :]
    turned_west = spread(from_west, TURN, shape) > 0.5
    turned_east = spread(from_east, TURN, shape) > 0.5
    west = jnp.where(turned_west, spread(head, HALF + 1, shape), spread(last, HALF + 1, shape))
    east = jnp.where(turned_east, spread(last, HALF, shape), spread(head, HALF, shape))
    v = jnp.where(lane == 0, west, jnp.where(lane == 1, east, 0.0))
    v = jnp.where(level == levels, spread(from_west, MATCH, shape), v)
    v = jnp.where(level == levels + 1, spread(from_east, MATCH, shape), v)
    item[6] = v.astype(BF16)


def inner_kernel(
    step, levels, opening, found, winds, adj, ends, from_west, from_east, east_wind, out, last_out, head_out
):
    row_count, width = adj.shape[0], adj.shape[3]
    columns = Columns(width)
    first_at, last_at = (7, 5) if opening else (2, 4)

    def put(r, f, v):
        out[r, f] = v
        columns.add(r, f, v)

    def row(r, f):
        return ends[f] if r == row_count - 1 and not opening else adj[r, f]

    rows = range(1, row_count - 1)
    advance(step, rows, levels, winds, found, east_wind, row, None, None, None, from_west, from_east, put)
    for f in range(2):
        put(0, f, ends[first_at + f])
        put(row_count - 1, f, ends[last_at + f])
    if opening:
        for f in range(2):
            v = ends[f]
            here = columns.lane == EDGE_COLUMN + f
            columns.last = jnp.where(here, spread(v, width - 1, v.shape), columns.last)
            columns.head = jnp.where(here, spread(v, 0, v.shape), columns.head)
    columns.write(last_out, head_out)


def middle_kernel(
    step, levels, sizes,
    code, inverse, where, found, winds, adj, edge, kept, from_west, from_east, east_wind,
    item, both,
):
    end = adj.shape[0] - 1
    north, _, turn_north, south, _, turn_south = neighbours(sizes, code, inverse, where)
    lower = oriented(edge[south, 0:4], turn_south)
    upper = oriented(edge[north, 4:6], turn_north)
    cs = COURANT * jnp.maximum(lower[2], 0.0)
    final = [kept[5 + f] + cs * kept[f] for f in range(2)]
    cs = COURANT * jnp.maximum(kept[4], 0.0)
    northern = []
    for f in range(2):
        v = upper[f] + cs * kept[2 + f]
        northern.append(v.astype(BF16).astype(F32))
    shape = final[0].shape
    lane = lanes(*shape)
    sides = []
    for i, columns in enumerate((from_west[...], from_east[...])):
        corner = jnp.zeros(shape, F32)
        for d in range(sizes[1]):
            k = edge[d, 6].astype(F32)
            corner = jnp.where(spread(k, 2 + i, shape) > 0.5, spread(k, i, shape), corner)
        cs = COURANT * jnp.maximum(corner, 0.0)
        mended = columns
        for f in range(2):
            mended = jnp.where(lane == 2 * end + f, columns + cs * spread(columns, EDGE_COLUMN + f, shape), mended)
        sides.append(mended)

    def put(r, f, v):
        item[f if r == 0 else 3 + f] = v.astype(BF16)
        both[(2 if r == 0 else 4) + f] = v

    def row(r, f):
        return final[f] if r == end else adj[r, f]

    advance(step, (0, end), levels, winds, found, east_wind, row, northern, lower, lower[3], *sides, put)
    both[0] = final[0]
    both[1] = final[1]
    item[2] = wind(levels, winds, found, (step - 1) * ROWS, 1).astype(BF16)


def late_kernel(step, levels, found, winds, adj, from_west, from_east, east_wind, out):
    rows = range(1, adj.shape[0] - 1)

    def put(r, f, v):
        out[r - 1, f] = v

    def row(r, f):
        return adj[r, f]

    advance(step, rows, levels, winds, found, east_wind, row, None, None, None, from_west, from_east, put)


def last_kernel(
    step, levels, sizes, code, inverse, where, found, winds, adj, edge, from_west, from_east, east_wind, inner, out
):
    end = adj.shape[0] - 1
    north, _, turn_north, south, _, turn_south = neighbours(sizes, code, inverse, where)
    upper = oriented(edge[north, 3:5], turn_north)
    lower = oriented(edge[south, 0:3], turn_south)

    def put(r, f, v):
        for l0 in range(0, levels, 8):
            n = min(8, levels - l0)
            out[pl.ds((f * levels + l0) * ROWS + r, n, stride=ROWS), :] = v[l0 : l0 + n]

    def row(r, f):
        return adj[r, f]

    for r in range(1, end):
        for f in range(2):
            put(r, f, inner[r - 1, f])
    advance(step, (0, end), levels, winds, found, east_wind, row, upper, lower, lower[2], from_west, from_east, put)


def shards(sizes, tile_sizes, adjoint_end, stored_rows, stored_owner, stored_unit, stored_valid, edge_match, edge_turn):
    face, tile, group = ("zl", "y", "c"), ("x", "zh"), ("zl", "c")
    faces = sizes[0] * sizes[1] * sizes[2]
    tiles = tile_sizes[0] * tile_sizes[1]
    levels, row_count, width = adjoint_end.shape[1:]
    slots = stored_rows.shape[1]
    sds = jax.ShapeDtypeStruct
    side = sds((PAD, width), F32)

    where = jnp.stack([lax.axis_index(a) for a in face]).astype(jnp.int32).reshape(1, 3)
    block = CAPACITY * 2 * levels // 8 + 1
    payload = call(
        functools.partial(pack_kernel, levels, tiles, (STEPS - 1) * row_count),
        sds((tiles * block, 8, width), BF16),
        [SM, SM, SM, HBM],
        HBM,
        [
            pltpu.SMEM((tiles,), jnp.int32),
            pltpu.SMEM((slots + 1,), jnp.int32),
            pltpu.SMEM((slots + 1,), jnp.int32),
            pltpu.SMEM((tiles + 1,), jnp.int32),
            pltpu.VMEM((width, width), F32),
            pltpu.VMEM((width, width), F32),
            pltpu.VMEM(stored_rows.shape[1:], BF16),
            pltpu.VMEM((tiles * block, 8, width), BF16),
            pltpu.SemaphoreType.DMA,
            pltpu.SemaphoreType.DMA((CHUNKS,)),
        ],
        61 << 20,
    )(stored_owner, stored_unit, stored_valid, stored_rows[0])

    turned, item, *sides = call(
        functools.partial(edges_kernel, levels, row_count),
        (sds((row_count, 2, PAD, width), F32), sds((4, PAD, width), BF16), side, side),
        [SM, SM, VM],
        (VM,) * 4,
    )(edge_match, edge_turn, adjoint_end.reshape(2 * levels * row_count, width))

    planes, mates = sizes[1], sizes[0] * sizes[2]

    def to_sides(sides):
        ahead = [(i, (i + 1) % tiles) for i in range(tiles)]
        back = [((i + 1) % tiles, i) for i in range(tiles)]
        return lax.ppermute(sides[0], tile, ahead), lax.ppermute(sides[1], tile, back)

    def exchange(item, north_from, rows):
        gathered = lax.all_gather(item, group, axis=0, tiled=False)
        chosen = call(
            functools.partial(choose_kernel, sizes, levels, north_from, rows),
            sds((planes,) + item.shape, BF16),
            [SM, SM, SM, VM],
            VM,
        )(code, inverse, where, gathered)
        return lax.all_to_all(chosen, "y", 0, 0, tiled=True)

    other = lax.ppermute(item, "zl", [(i, (i + 1) % sizes[0]) for i in range(sizes[0])])
    payload, other = lax.optimization_barrier((payload, other))
    winds = lax.all_to_all(payload, tile, 0, 0, tiled=True)
    from_west, from_east = to_sides(sides)
    near = lax.all_gather(jnp.stack([item, other]), "c", axis=0, tiled=False)
    half, cores = planes // 2, sizes[2]
    own, *parts = call(
        functools.partial(first_send_kernel, sizes, levels),
        (sds((2 * (mates + cores), PAD, width), BF16),) * (half + 1),
        [SM, VM],
        (VM,) * (half + 1),
    )(where, near)
    moved = []
    for d, part in enumerate(parts, 1):
        ways = [(c, d if c == 0 else -d) for c in range(cores) if c == 0 or d < half]
        route = [(y * cores + c, (y + way) % planes * cores + c) for y in range(planes) for c, way in ways]
        moved.append(lax.ppermute(part, ("y", "c"), route))
    edge = lax.all_gather(jnp.stack(moved), "c", axis=0, tiled=True)
    table = sds((1, width), jnp.int32)
    code, inverse = call(
        functools.partial(code_kernel, sizes, levels), (table, table), [SM, VM, VM], (VM, VM)
    )(where, own, edge)

    item, kept, found, east_wind = call(
        functools.partial(first_kernel, STEPS - 1, levels, sizes, tiles),
        (sds((7, PAD, width), BF16), sds((9, PAD, width), F32), table, side),
        [SM, SM, SM] + [VM] * 6,
        (VM,) * 4,
        [pltpu.SMEM((1, width), jnp.int32), pltpu.SemaphoreType.DMA, pltpu.VMEM((width, width), F32)],
    )(code, inverse, where, winds, turned, own, edge, from_west, from_east)
    edge = exchange(item, 4, 6)

    def inner(step, opening, adj, ends):
        adj, *sides = call(
            functools.partial(inner_kernel, step, levels, opening),
            (sds(turned.shape, F32), side, side),
            [SM] + [VM] * 6,
            (VM,) * 3,
        )(found, winds, adj, ends, from_west, from_east, east_wind)
        return adj, sides

    adj, sides = inner(STEPS - 1, True, turned, kept)
    from_west, from_east = to_sides(sides)
    item, both = call(
        functools.partial(middle_kernel, STEPS - 2, levels, sizes),
        (sds((5, PAD, width), BF16), sds((6, PAD, width), F32)),
        [SM] * 4 + [VM] * 7,
        (VM,) * 2,
    )(code, inverse, where, found, winds, adj, edge, kept, from_west, from_east, east_wind)
    edge = exchange(item, 3, 5)
    adj, sides = inner(STEPS - 2, False, adj, both)

    from_west, from_east = to_sides(sides)
    late = call(
        functools.partial(late_kernel, STEPS - 3, levels),
        sds((row_count - 2,) + turned.shape[1:], F32),
        [SM] + [VM] * 5,
        VM,
    )(found, winds, adj, from_west, from_east, east_wind)
    out = call(
        functools.partial(last_kernel, STEPS - 3, levels, sizes),
        sds((2 * levels * row_count, width), F32),
        [SM] * 4 + [VM] * 7,
        VM,
    )(code, inverse, where, found, winds, adj, edge, from_west, from_east, east_wind, late)
    return out.reshape(adjoint_end.shape)


def solution(mesh, sizes=(2, 8, 2), tile_sizes=(8, 4)):
    fine = Mesh(mesh.devices.reshape(sizes + tile_sizes), ("zl", "y", "c", "x", "zh"))
    face, tile = ("zl", "y", "c"), ("x", "zh")
    placed = (
        P(None, None, face, tile),
        P(face, tile, None, None, None),
        P(face, tile),
        P(face, tile),
        P(face, tile),
        P(face, tile),
        P(face, tile),
    )
    return jax.shard_map(
        functools.partial(shards, sizes, tile_sizes),
        mesh=fine,
        in_specs=placed,
        out_specs=P(None, None, face, tile),
        check_vma=False,
    )
```

```python
import functools

import jax
import jax.numpy as jnp
from jax import lax
from jax.experimental import pallas as pl
from jax.experimental.pallas import tpu as pltpu
from jax.sharding import Mesh
from jax.sharding import PartitionSpec as P

STEPS = 3
ROWS = 16
CAPACITY = 3
COURANT = 0.2
PAD = 40
LABEL, LABEL_EAST = 64, 65
CHUNKS = 4
HALF = 64
MATCH, TURN = 96, 97
EDGE_COLUMN = 32
INTERPRET = False

VM = pl.BlockSpec(memory_space=pltpu.VMEM)
SM = pl.BlockSpec(memory_space=pltpu.SMEM)
HBM = pl.BlockSpec(memory_space=pltpu.HBM)
F32, BF16 = jnp.float32, jnp.bfloat16


def call(kernel, out_shape, in_specs, out_specs, scratch=(), vmem=24 << 20):
    return pl.pallas_call(
        kernel,
        out_shape=out_shape,
        in_specs=in_specs,
        out_specs=out_specs,
        scratch_shapes=list(scratch),
        compiler_params=pltpu.CompilerParams(vmem_limit_bytes=vmem),
        cost_estimate=pl.CostEstimate(flops=1 << 20, bytes_accessed=1 << 20, transcendentals=0),
        interpret=INTERPRET,
    )


def lanes(rows, width):
    return lax.broadcasted_iota(jnp.int32, (rows, width), 1)


def spread(values, lane, shape):
    return jnp.broadcast_to(values[:, lane : lane + 1], shape)


def pack_kernel(
    levels, tiles, edge_unit, owner, unit, valid, stored, sent, count, source, label, first, flat, corner, rows, out, sem_in, sem_out
):
    fetch = pltpu.make_async_copy(stored, rows, sem_in)
    fetch.start()
    slots, width = rows.shape[0], rows.shape[3]
    capacity = slots // tiles
    block = out.shape[0] // tiles
    whole = levels // 8 * 8

    def clear(i, c):
        count[i] = 0
        first[i] = -1
        return c

    lax.fori_loop(0, tiles, clear, 0, unroll=8)

    def blank(i, c):
        source[i] = 0
        label[i] = -1
        return c

    lax.fori_loop(0, slots, blank, 0, unroll=8)

    def place(s, c):
        o, u, v = owner[0, s], unit[0, s], valid[0, s]
        have = count[o]
        p = jnp.where(v == 1, o * capacity + have, slots)
        source[p] = s
        label[p] = u
        count[o] = have + v
        first[jnp.where((v == 1) & (u == edge_unit), o, tiles)] = s
        return c

    lax.fori_loop(0, slots, place, 0, unroll=8)
    fetch.wait()

    lane = lanes(levels, width)

    def column(s, held):
        v = rows[s, 0].astype(F32)
        return jnp.where(lane == s, spread(v, 0, v.shape), held)

    def corners(o, held):
        v = rows[jnp.maximum(first[o], 0), 1].astype(F32)
        held = jnp.where(lane == o, spread(v, 0, v.shape), held)
        return jnp.where(lane == tiles + o, spread(v, width - 1, v.shape), held)

    for ref, one, n in ((flat, column, slots), (corner, corners, tiles)):
        held = lax.fori_loop(0, n, one, jnp.zeros((levels, width), F32), unroll=8)
        ref[...] = jnp.zeros_like(ref)
        ref[0:levels, :] = held
        ref[...] = ref[...].T

    extra_lane = lanes(8, width)
    extra_row = lax.broadcasted_iota(jnp.int32, (8, width), 0)

    def at(ref, i):
        return jnp.broadcast_to(ref[pl.ds(i, 1), :], (8, width))

    def fill(o, c):
        base = o * block
        east = jnp.where(o + 1 == tiles, 0, o + 1)
        west = jnp.where(o == 0, tiles - 1, o - 1)
        extra = jnp.zeros((8, width), F32)
        for i in range(capacity):
            p, q = o * capacity + i, east * capacity + i
            s = source[p]
            at_slot = base + i * (2 * levels // 8)
            for j in range(2):
                for k in range(whole // 8):
                    out[at_slot + j * (whole // 8) + k] = rows[s, j, 8 * k : 8 * k + 8]
            rest = [rows[s, j, whole:levels].astype(F32) for j in range(2)]
            out[at_slot + 2 * whole // 8] = jnp.concatenate(rest, axis=0).astype(BF16)
            line = at(flat, source[q])
            line = jnp.where(extra_lane == LABEL, label[p].astype(F32), line)
            line = jnp.where(extra_lane == LABEL_EAST, label[q].astype(F32), line)
            extra = jnp.where(extra_row == i, line, extra)
        for i, side in ((capacity, east), (capacity + 1, west)):
            line = jnp.where(extra_lane < HALF, at(corner, side), pltpu.roll(at(corner, tiles + side), HALF, 1))
            line = jnp.where(extra_lane == width - 1, jnp.where(first[side] >= 0, 1.0, 0.0), line)
            extra = jnp.where(extra_row == i, line, extra)
        out[base + block - 1] = extra.astype(BF16)
        return c

    chunk = tiles // CHUNKS
    copies = []
    for i in range(CHUNKS):
        lax.fori_loop(i * chunk, (i + 1) * chunk, fill, 0, unroll=2)
        span = pl.ds(i * chunk * block, chunk * block)
        copies.append(pltpu.make_async_copy(out.at[span], sent.at[span], sem_out.at[i]))
        copies[-1].start()
    for copy in copies:
        copy.wait()


class Columns:
    def __init__(self, width):
        self.pair = lax.shift_right_logical(lanes(PAD, width), 1)
        self.held = jnp.zeros((PAD, width), F32)

    def add(self, q, v):
        self.held = jnp.where(self.pair == q, pltpu.roll(v, 2 * q + 1, 1), self.held)


def joined(from_west, from_east):
    shape = from_west.shape
    even = (lanes(*shape) & 1) == 0
    return jnp.where(even, pltpu.roll(from_east[...], shape[1] - 1, 1), pltpu.roll(from_west[...], 1, 1))


def edges_kernel(levels, row_count, match, turn, adj, turned, item, sides):
    width = adj.shape[1]
    lane = lanes(PAD, width)
    columns = Columns(width)
    for r in range(row_count):
        for f in range(2):
            for l0 in range(0, levels, 8):
                n = min(8, levels - l0)
                turned[r, f, l0 : l0 + n, :] = adj[pl.ds((f * levels + l0) * row_count + r, n, stride=row_count), :]
            turned[r, f, levels:PAD, :] = jnp.zeros((PAD - levels, width), F32)
            v = turned[r, f]
            columns.add(r * 2 + f, v)
            if r == 0:
                item[f] = v.astype(BF16)
            if r == row_count - 1:
                if f == 0:
                    level = lax.broadcasted_iota(jnp.int32, v.shape, 0)
                    v = jnp.where(level == levels, match[0, 0].astype(F32), v)
                    v = jnp.where(level == levels + 1, turn[0, 0].astype(F32), v)
                item[2 + f] = v.astype(BF16)
    v = jnp.where(lane == MATCH, match[0, 0].astype(F32), columns.held)
    sides[...] = jnp.where(lane == TURN, turn[0, 0].astype(F32), v)


def tail(tile, levels):
    return tile[PAD - 8 : PAD, :].astype(F32)[levels - (PAD - 8) :, :]


def first_send_kernel(sizes, levels, where, mates, *outs):
    nz, ny, nc = sizes
    zl, y, c = where[0, 0], where[0, 1], where[0, 2]
    order = [(i, lax.rem(j + zl, nz)) for j in range(nz) for i in range(nc)]
    shape = mates.shape[3:]
    match = [jnp.broadcast_to(tail(mates[i, z, 2], levels)[0:1], shape) for i, z in order]
    first = [[mates[i, z, f].astype(F32) for f in range(2)] for i, z in order]
    for d, out in enumerate(outs):
        plane = lax.rem(jnp.where(c == 0, y + d, y - d + ny), ny)
        for m, (i, z) in enumerate(order):
            for f in range(2):
                out[2 * m + f] = mates[i, z, 2 + f]
        for core in range(nc):
            dest = ((zl * ny + plane) * nc + core).astype(F32)
            for f in range(2):
                v = first[0][f]
                for m in range(1, len(order)):
                    v = jnp.where(match[m] == dest, first[m][f], v)
                out[2 * (len(order) + core) + f] = v.astype(BF16)


def code_kernel(sizes, levels, where, own, edge, code, inverse):
    nz, ny, nc = sizes
    half = ny // 2
    lane = lanes(1, code.shape[1])
    codes = jnp.zeros(code.shape, F32)
    south = jnp.zeros(code.shape, jnp.int32)
    for d in range(ny):
        plane = lax.rem(where[0, 1] - d + ny, ny)
        for m in range(nz * nc):
            t = tail(own[2 * m] if d == 0 else edge[d - 1 if d <= half else half + ny - d - 1, 2 * m], levels)
            face = ((m // nc) * ny + plane) * nc + m % nc
            codes = jnp.where(lane == face, 2.0 * t[0:1] + t[1:2], codes)
            south = jnp.where(lane.astype(F32) == t[0:1], face, south)
    code[...] = codes.astype(jnp.int32)
    inverse[...] = south


def choose_kernel(sizes, levels, north_from, rows, code, inverse, where, gathered, out):
    _, ny, nc = sizes
    zl, c = where[0, 0], where[0, 2]
    if gathered.shape[1] > rows:
        corner = [gathered[m, rows].astype(F32) for m in range(gathered.shape[0])]
        shape = corner[0].shape
        lane = lanes(*shape)
        to = [[jnp.broadcast_to(tail(k, levels)[i : i + 1], shape) for i in range(2)] for k in corner]
    for d in range(ny):
        dest = (zl * ny + d) * nc + c
        for source, a, b in (
            (inverse[0, dest], 0, north_from),
            (lax.shift_right_logical(code[0, dest], 1), north_from, rows),
        ):
            group = (source // (ny * nc)) * nc + source % nc
            for i in range(a, b):
                out[d, i] = gathered[group, i]
        if gathered.shape[1] > rows:
            v = jnp.zeros(shape, F32)
            for k, both in zip(corner, to):
                for i in range(2):
                    hit = both[i] == dest.astype(F32)
                    v = jnp.where(hit & (lane == i), k, v)
                    v = jnp.where(hit & (lane == 2 + i), 1.0, v)
            out[d, rows] = v.astype(BF16)


def neighbours(sizes, code, inverse, where):
    _, ny, nc = sizes
    me = (where[0, 0] * ny + where[0, 1]) * nc + where[0, 2]
    south = inverse[0, me]
    found = []
    for face, turn in ((lax.shift_right_logical(code[0, me], 1), code[0, me] & 1), (south, code[0, south] & 1)):
        found += [(face // nc) % ny, (face // (ny * nc)) * nc + face % nc, turn]
    return found


def oriented(block, turn):
    n, rows, width = block.shape
    i = lax.broadcasted_iota(jnp.int32, (width, width), 0)
    j = lax.broadcasted_iota(jnp.int32, (width, width), 1)
    source = jnp.where(turn == 1, width - 1 - j, j)
    matrix = jnp.where(i == source, 1.0, 0.0).astype(BF16)
    out = jnp.dot(block.reshape(n * rows, width), matrix, preferred_element_type=F32)
    return out.reshape(n, rows, width)


def find_slots(levels, tiles, capacity, winds, found_out, found, sem, extras):
    block = winds.shape[0] // tiles
    extra = jnp.concatenate([winds[h * block + block - 1].astype(F32) for h in range(tiles)], axis=0)
    row = lax.broadcasted_iota(jnp.int32, extra.shape, 0)
    holder, at = lax.shift_right_logical(row, 3), row & 7
    lane = lanes(*extra.shape)
    here = (at < capacity) & (spread(extra, LABEL, extra.shape) == lane.astype(F32))
    there = (at < capacity) & (spread(extra, LABEL_EAST, extra.shape) == lane.astype(F32))
    sides = (at - capacity == lane - HALF) & (at >= capacity) & (at < capacity + 2)
    there = there | (sides & (spread(extra, extra.shape[1] - 1, extra.shape) > 0.5))
    place = (holder * block + at * (2 * levels // 8)).astype(F32)
    index = jnp.sum(jnp.where(here, place, 0.0), axis=0, keepdims=True)
    found_out[...] = index.astype(jnp.int32)
    copy = pltpu.make_async_copy(found_out, found, sem)
    copy.start()
    extras[...] = lax.dot_general(
        extra.astype(BF16), jnp.where(there, 1.0, 0.0).astype(BF16), (((0,), (0,)), ((), ())), preferred_element_type=F32
    )
    copy.wait()


def wind(levels, winds, found, unit, i):
    whole = levels // 8 * 8
    base = found[0, unit]
    rest = winds[base + 2 * whole // 8].astype(F32)
    if i == 1:
        rest = pltpu.roll(rest, 8 - (levels - whole), 0)
    main = winds[pl.ds(base + i * (whole // 8), whole // 8)].astype(F32).reshape(whole, rest.shape[1])
    return jnp.concatenate([main, rest], axis=0)


def advance(step, rows, levels, winds, found, east_wind, row, upper, lower, south_end, halo, put):
    row_count, width = ROWS, winds.shape[2]
    lane = lanes(PAD, width)
    base = step * row_count

    def of(r, i):
        return wind(levels, winds, found, base + r, i)

    south_wind, at = None, None
    for r in rows:
        west_wind = of(r, 0)
        north_wind = south_wind if at == r - 1 else of(r, 1)
        south_wind, at = (of(r + 1, 1) if r + 1 < row_count else south_end), r
        eastern_wind = jnp.where(
            lane == width - 1, spread(east_wind, base + r, lane.shape), pltpu.roll(west_wind, width - 1, 1)
        )
        cw = COURANT * jnp.minimum(west_wind, 0.0)
        ce = COURANT * jnp.maximum(eastern_wind, 0.0)
        cn = COURANT * jnp.minimum(north_wind, 0.0)
        if south_wind is not None:
            cs = COURANT * jnp.maximum(south_wind, 0.0)
        for f in range(2):
            q = r * 2 + f
            a = row(r, f)
            beside = pltpu.roll(halo, width - 1 - 2 * q, 1)
            west = jnp.where(lane == 0, beside, pltpu.roll(a, 1, 1))
            east = jnp.where(lane == width - 1, beside, pltpu.roll(a, width - 1, 1))
            v = a + cw * (a - west)
            v = v + ce * (east - a)
            v = v + cn * (a - (row(r - 1, f) if r > 0 else upper[f]))
            if south_wind is not None:
                v = v + cs * ((row(r + 1, f) if r + 1 < row_count else lower[f]) - a)
            put(r, f, v)


def prepare_kernel(sizes, code, inverse, where, own, edge, ends):
    mates = sizes[0] * sizes[2]
    north, north_mate, turn_north, south, _, turn_south = neighbours(sizes, code, inverse, where)
    y, c, ny = where[0, 1], where[0, 2], sizes[1]
    half = ny // 2

    def arrived(plane, row):
        d = lax.rem(y - plane + ny, ny)
        i = jnp.where(d <= half, jnp.maximum(d - 1, 0), half + ny - d - 1)
        both = own[pl.ds(row, 2)].astype(F32), edge[i, pl.ds(row, 2)].astype(F32)
        return jnp.where(d == 0, *both).astype(BF16)

    ends[0:2] = oriented(arrived(north, 2 * north_mate), turn_north)
    ends[2:4] = oriented(arrived(south, 2 * (mates + c)), turn_south)


def first_kernel(
    step, levels, tiles,
    winds, adj, ends, from_west, from_east,
    item, kept, found_out, east_wind,
    found, sem, extras,
):
    end, width = adj.shape[0] - 1, adj.shape[3]
    find_slots(levels, tiles, CAPACITY, winds, found_out, found, sem, extras)
    east_wind[...] = extras[0:PAD, :]
    halo = joined(from_west, from_east)
    upper = (ends[0], ends[1])

    def put(r, f, v):
        item[f if r == 0 else 4 + f] = v.astype(BF16)
        kept[(7 if r == 0 else 5) + f] = v

    def row(r, f):
        return adj[r, f]

    advance(step, (0, end), levels, winds, found, east_wind, row, upper, None, None, halo, put)
    edge_wind = wind(levels, winds, found, step * ROWS, 1)
    item[2] = edge_wind.astype(BF16)
    item[3] = wind(levels, winds, found, (step - 1) * ROWS, 1).astype(BF16)
    for f in range(2):
        kept[f] = ends[2 + f] - adj[end, f]
        kept[2 + f] = adj[0, f].astype(BF16).astype(F32) - upper[f]
    kept[4] = edge_wind

    shape = (PAD, width)
    lane, level = lanes(*shape), lax.broadcasted_iota(jnp.int32, shape, 0)
    head, last = extras[0:PAD, :], extras[HALF : HALF + PAD, :]
    turned_west = spread(from_west, TURN, shape) > 0.5
    turned_east = spread(from_east, TURN, shape) > 0.5
    west = jnp.where(turned_west, spread(head, HALF + 1, shape), spread(last, HALF + 1, shape))
    east = jnp.where(turned_east, spread(last, HALF, shape), spread(head, HALF, shape))
    v = jnp.where(lane == 0, west, jnp.where(lane == 1, east, 0.0))
    v = jnp.where(level == levels, spread(from_west, MATCH, shape), v)
    v = jnp.where(level == levels + 1, spread(from_east, MATCH, shape), v)
    item[6] = v.astype(BF16)


def inner_kernel(
    step, levels, opening, found, winds, adj, ends, from_west, from_east, east_wind, out, sides
):
    row_count, width = adj.shape[0], adj.shape[3]
    columns = Columns(width)
    first_at, last_at = (7, 5) if opening else (2, 4)

    def put(r, f, v):
        out[r, f] = v
        columns.add(2 * r + f, v)

    def row(r, f):
        return ends[f] if r == row_count - 1 and not opening else adj[r, f]

    rows = range(1, row_count - 1)
    advance(step, rows, levels, winds, found, east_wind, row, None, None, None, joined(from_west, from_east), put)
    for f in range(2):
        put(0, f, ends[first_at + f])
        put(row_count - 1, f, ends[last_at + f])
    if opening:
        for f in range(2):
            columns.add(EDGE_COLUMN + f, ends[f])
    sides[...] = columns.held


def middle_kernel(
    step, levels, sizes,
    code, inverse, where, found, winds, adj, edge, kept, from_west, from_east, east_wind,
    item, both,
):
    end = adj.shape[0] - 1
    north, _, turn_north, south, _, turn_south = neighbours(sizes, code, inverse, where)
    lower = oriented(edge[south, 0:4], turn_south)
    upper = oriented(edge[north, 4:6], turn_north)
    cs = COURANT * jnp.maximum(lower[2], 0.0)
    final = [kept[5 + f] + cs * kept[f] for f in range(2)]
    cs = COURANT * jnp.maximum(kept[4], 0.0)
    northern = []
    for f in range(2):
        v = upper[f] + cs * kept[2 + f]
        northern.append(v.astype(BF16).astype(F32))
    shape = final[0].shape
    lane = lanes(*shape)
    sides = []
    for i, columns in enumerate((from_west[...], from_east[...])):
        corner = jnp.zeros(shape, F32)
        for d in range(sizes[1]):
            k = edge[d, 6].astype(F32)
            corner = jnp.where(spread(k, 2 + i, shape) > 0.5, spread(k, i, shape), corner)
        cs = COURANT * jnp.maximum(corner, 0.0)
        mended = columns
        for f in range(2):
            change = cs * spread(columns, 2 * (EDGE_COLUMN + f) + i, shape)
            mended = jnp.where(lane == 2 * (2 * end + f) + i, columns + change, mended)
        sides.append(mended)

    def put(r, f, v):
        item[f if r == 0 else 3 + f] = v.astype(BF16)
        both[(2 if r == 0 else 4) + f] = v

    def row(r, f):
        return final[f] if r == end else adj[r, f]

    advance(step, (0, end), levels, winds, found, east_wind, row, northern, lower, lower[3], joined(*sides), put)
    both[0] = final[0]
    both[1] = final[1]
    item[2] = wind(levels, winds, found, (step - 1) * ROWS, 1).astype(BF16)


def last_kernel(
    step, levels, sizes, code, inverse, where, found, winds, adj, edge, from_west, from_east, east_wind, out
):
    north, _, turn_north, south, _, turn_south = neighbours(sizes, code, inverse, where)
    upper = oriented(edge[north, 3:5], turn_north)
    lower = oriented(edge[south, 0:3], turn_south)

    def put(r, f, v):
        for l0 in range(0, levels, 8):
            n = min(8, levels - l0)
            out[pl.ds((f * levels + l0) * ROWS + r, n, stride=ROWS), :] = v[l0 : l0 + n]

    def row(r, f):
        return adj[r, f]

    halo = joined(from_west, from_east)
    advance(step, range(ROWS), levels, winds, found, east_wind, row, upper, lower, lower[2], halo, put)


def shards(sizes, tile_sizes, adjoint_end, stored_rows, stored_owner, stored_unit, stored_valid, edge_match, edge_turn):
    face, tile, group = ("zl", "y", "c"), ("x", "zh"), ("zl", "c")
    faces = sizes[0] * sizes[1] * sizes[2]
    tiles = tile_sizes[0] * tile_sizes[1]
    levels, row_count, width = adjoint_end.shape[1:]
    slots = stored_rows.shape[1]
    sds = jax.ShapeDtypeStruct
    side = sds((PAD, width), F32)

    where = jnp.stack([lax.axis_index(a) for a in face]).astype(jnp.int32).reshape(1, 3)
    block = CAPACITY * 2 * levels // 8 + 1
    payload = call(
        functools.partial(pack_kernel, levels, tiles, (STEPS - 1) * row_count),
        sds((tiles * block, 8, width), BF16),
        [SM, SM, SM, HBM],
        HBM,
        [
            pltpu.SMEM((tiles,), jnp.int32),
            pltpu.SMEM((slots + 1,), jnp.int32),
            pltpu.SMEM((slots + 1,), jnp.int32),
            pltpu.SMEM((tiles + 1,), jnp.int32),
            pltpu.VMEM((width, width), F32),
            pltpu.VMEM((width, width), F32),
            pltpu.VMEM(stored_rows.shape[1:], BF16),
            pltpu.VMEM((tiles * block, 8, width), BF16),
            pltpu.SemaphoreType.DMA,
            pltpu.SemaphoreType.DMA((CHUNKS,)),
        ],
        61 << 20,
    )(stored_owner, stored_unit, stored_valid, stored_rows[0])

    turned, item, sides = call(
        functools.partial(edges_kernel, levels, row_count),
        (sds((row_count, 2, PAD, width), F32), sds((4, PAD, width), BF16), side),
        [SM, SM, VM],
        (VM,) * 3,
    )(edge_match, edge_turn, adjoint_end.reshape(2 * levels * row_count, width))

    planes, mates = sizes[1], sizes[0] * sizes[2]

    def to_sides(sides):
        ahead = [(i, (i + 1) % tiles) for i in range(tiles)]
        back = [((i + 1) % tiles, i) for i in range(tiles)]
        return lax.ppermute(sides, tile, ahead), lax.ppermute(sides, tile, back)

    def exchange(item, north_from, rows):
        gathered = lax.all_gather(item, group, axis=0, tiled=False)
        chosen = call(
            functools.partial(choose_kernel, sizes, levels, north_from, rows),
            sds((planes,) + item.shape, BF16),
            [SM, SM, SM, VM],
            VM,
        )(code, inverse, where, gathered)
        return lax.all_to_all(chosen, "y", 0, 0, tiled=True)

    other = lax.ppermute(item, "zl", [(i, (i + 1) % sizes[0]) for i in range(sizes[0])])
    payload, other = lax.optimization_barrier((payload, other))
    winds = lax.all_to_all(payload, tile, 0, 0, tiled=True)
    from_west, from_east = to_sides(sides)
    near = lax.all_gather(jnp.stack([item, other]), "c", axis=0, tiled=False)
    half, cores = planes // 2, sizes[2]
    own, *parts = call(
        functools.partial(first_send_kernel, sizes, levels),
        (sds((2 * (mates + cores), PAD, width), BF16),) * (half + 1),
        [SM, VM],
        (VM,) * (half + 1),
    )(where, near)
    moved = []
    for d, part in enumerate(parts, 1):
        ways = [(c, d if c == 0 else -d) for c in range(cores) if c == 0 or d < half]
        route = [(y * cores + c, (y + way) % planes * cores + c) for y in range(planes) for c, way in ways]
        moved.append(lax.ppermute(part, ("y", "c"), route))
    edge = lax.all_gather(jnp.stack(moved), "c", axis=0, tiled=True)
    table = sds((1, width), jnp.int32)
    code, inverse = call(
        functools.partial(code_kernel, sizes, levels), (table, table), [SM, VM, VM], (VM, VM)
    )(where, own, edge)

    ends = call(
        functools.partial(prepare_kernel, sizes), sds((4, PAD, width), F32), [SM, SM, SM, VM, VM], VM
    )(code, inverse, where, own, edge)

    item, kept, found, east_wind = call(
        functools.partial(first_kernel, STEPS - 1, levels, tiles),
        (sds((7, PAD, width), BF16), sds((9, PAD, width), F32), table, side),
        [VM] * 5,
        (VM,) * 4,
        [pltpu.SMEM((1, width), jnp.int32), pltpu.SemaphoreType.DMA, pltpu.VMEM((width, width), F32)],
    )(winds, turned, ends, from_west, from_east)
    edge = exchange(item, 4, 6)

    def inner(step, opening, adj, ends):
        return call(
            functools.partial(inner_kernel, step, levels, opening),
            (sds(turned.shape, F32), side),
            [SM] + [VM] * 6,
            (VM,) * 2,
        )(found, winds, adj, ends, from_west, from_east, east_wind)

    adj, sides = inner(STEPS - 1, True, turned, kept)
    from_west, from_east = to_sides(sides)
    item, both = call(
        functools.partial(middle_kernel, STEPS - 2, levels, sizes),
        (sds((5, PAD, width), BF16), sds((6, PAD, width), F32)),
        [SM] * 4 + [VM] * 7,
        (VM,) * 2,
    )(code, inverse, where, found, winds, adj, edge, kept, from_west, from_east, east_wind)
    edge = exchange(item, 3, 5)
    adj, sides = inner(STEPS - 2, False, adj, both)

    from_west, from_east = to_sides(sides)
    out = call(
        functools.partial(last_kernel, STEPS - 3, levels, sizes),
        sds((2 * levels * row_count, width), F32),
        [SM] * 4 + [VM] * 6,
        VM,
    )(code, inverse, where, found, winds, adj, edge, from_west, from_east, east_wind)
    return out.reshape(adjoint_end.shape)


def solution(mesh, sizes=(2, 8, 2), tile_sizes=(8, 4)):
    fine = Mesh(mesh.devices.reshape(sizes + tile_sizes), ("zl", "y", "c", "x", "zh"))
    face, tile = ("zl", "y", "c"), ("x", "zh")
    placed = (
        P(None, None, face, tile),
        P(face, tile, None, None, None),
        P(face, tile),
        P(face, tile),
        P(face, tile),
        P(face, tile),
        P(face, tile),
    )
    return jax.shard_map(
        functools.partial(shards, sizes, tile_sizes),
        mesh=fine,
        in_specs=placed,
        out_specs=P(None, None, face, tile),
        check_vma=False,
    )
```

```python
import functools

import jax
import jax.numpy as jnp
from jax import lax
from jax.experimental import pallas as pl
from jax.experimental.pallas import tpu as pltpu
from jax.sharding import Mesh
from jax.sharding import PartitionSpec as P

STEPS = 3
ROWS = 16
CAPACITY = 3
COURANT = 0.2
PAD = 40
LABEL, LABEL_EAST = 64, 65
CHUNKS = 4
HALF = 64
MATCH, TURN = 96, 97
EDGE_COLUMN = 32
INTERPRET = False

VM = pl.BlockSpec(memory_space=pltpu.VMEM)
SM = pl.BlockSpec(memory_space=pltpu.SMEM)
HBM = pl.BlockSpec(memory_space=pltpu.HBM)
F32, BF16 = jnp.float32, jnp.bfloat16


def call(kernel, out_shape, in_specs, out_specs, scratch=(), vmem=24 << 20):
    return pl.pallas_call(
        kernel,
        out_shape=out_shape,
        in_specs=in_specs,
        out_specs=out_specs,
        scratch_shapes=list(scratch),
        compiler_params=pltpu.CompilerParams(vmem_limit_bytes=vmem),
        cost_estimate=pl.CostEstimate(flops=1 << 20, bytes_accessed=1 << 20, transcendentals=0),
        interpret=INTERPRET,
    )


def lanes(rows, width):
    return lax.broadcasted_iota(jnp.int32, (rows, width), 1)


def spread(values, lane, shape):
    return jnp.broadcast_to(values[:, lane : lane + 1], shape)


def pack_kernel(
    levels, tiles, edge_unit, owner, unit, valid, stored, sent, count, source, label, first, flat, corner, rows, out, sem_in, sem_out
):
    fetch = pltpu.make_async_copy(stored, rows, sem_in)
    fetch.start()
    slots, width = rows.shape[0], rows.shape[3]
    capacity = slots // tiles
    block = out.shape[0] // tiles
    whole = levels // 8 * 8

    def clear(i, c):
        count[i] = 0
        first[i] = -1
        return c

    lax.fori_loop(0, tiles, clear, 0, unroll=8)

    def blank(i, c):
        source[i] = 0
        label[i] = -1
        return c

    lax.fori_loop(0, slots, blank, 0, unroll=8)

    def place(s, c):
        o, u, v = owner[0, s], unit[0, s], valid[0, s]
        have = count[o]
        p = jnp.where(v == 1, o * capacity + have, slots)
        source[p] = s
        label[p] = u
        count[o] = have + v
        first[jnp.where((v == 1) & (u == edge_unit), o, tiles)] = s
        return c

    lax.fori_loop(0, slots, place, 0, unroll=8)
    fetch.wait()

    lane = lanes(levels, width)

    def column(s, held):
        v = rows[s, 0].astype(F32)
        return jnp.where(lane == s, spread(v, 0, v.shape), held)

    def corners(o, held):
        v = rows[jnp.maximum(first[o], 0), 1].astype(F32)
        held = jnp.where(lane == o, spread(v, 0, v.shape), held)
        return jnp.where(lane == tiles + o, spread(v, width - 1, v.shape), held)

    for ref, one, n in ((flat, column, slots), (corner, corners, tiles)):
        held = lax.fori_loop(0, n, one, jnp.zeros((levels, width), F32), unroll=8)
        ref[...] = jnp.zeros_like(ref)
        ref[0:levels, :] = held
        ref[...] = ref[...].T

    extra_lane = lanes(8, width)
    extra_row = lax.broadcasted_iota(jnp.int32, (8, width), 0)

    def at(ref, i):
        return jnp.broadcast_to(ref[pl.ds(i, 1), :], (8, width))

    def fill(o, c):
        base = o * block
        east = jnp.where(o + 1 == tiles, 0, o + 1)
        west = jnp.where(o == 0, tiles - 1, o - 1)
        extra = jnp.zeros((8, width), F32)
        for i in range(capacity):
            p, q = o * capacity + i, east * capacity + i
            s = source[p]
            at_slot = base + i * (2 * levels // 8)
            for j in range(2):
                for k in range(whole // 8):
                    out[at_slot + j * (whole // 8) + k] = rows[s, j, 8 * k : 8 * k + 8]
            rest = [rows[s, j, whole:levels].astype(F32) for j in range(2)]
            out[at_slot + 2 * whole // 8] = jnp.concatenate(rest, axis=0).astype(BF16)
            line = at(flat, source[q])
            line = jnp.where(extra_lane == LABEL, label[p].astype(F32), line)
            line = jnp.where(extra_lane == LABEL_EAST, label[q].astype(F32), line)
            extra = jnp.where(extra_row == i, line, extra)
        for i, side in ((capacity, east), (capacity + 1, west)):
            line = jnp.where(extra_lane < HALF, at(corner, side), pltpu.roll(at(corner, tiles + side), HALF, 1))
            line = jnp.where(extra_lane == width - 1, jnp.where(first[side] >= 0, 1.0, 0.0), line)
            extra = jnp.where(extra_row == i, line, extra)
        out[base + block - 1] = extra.astype(BF16)
        return c

    chunk = tiles // CHUNKS
    copies = []
    for i in range(CHUNKS):
        lax.fori_loop(i * chunk, (i + 1) * chunk, fill, 0, unroll=2)
        span = pl.ds(i * chunk * block, chunk * block)
        copies.append(pltpu.make_async_copy(out.at[span], sent.at[span], sem_out.at[i]))
        copies[-1].start()
    for copy in copies:
        copy.wait()


class Columns:
    def __init__(self, width):
        self.pair = lax.shift_right_logical(lanes(PAD, width), 1)
        self.held = jnp.zeros((PAD, width), F32)

    def add(self, q, v):
        self.held = jnp.where(self.pair == q, pltpu.roll(v, 2 * q + 1, 1), self.held)


def joined(from_west, from_east):
    shape = from_west.shape
    even = (lanes(*shape) & 1) == 0
    return jnp.where(even, pltpu.roll(from_east[...], shape[1] - 1, 1), pltpu.roll(from_west[...], 1, 1))


def edges_kernel(levels, row_count, match, turn, adj, turned, item, sides):
    width = adj.shape[1]
    lane = lanes(PAD, width)
    columns = Columns(width)
    for r in range(row_count):
        for f in range(2):
            for l0 in range(0, levels, 8):
                n = min(8, levels - l0)
                turned[r, f, l0 : l0 + n, :] = adj[pl.ds((f * levels + l0) * row_count + r, n, stride=row_count), :]
            turned[r, f, levels:PAD, :] = jnp.zeros((PAD - levels, width), F32)
            v = turned[r, f]
            columns.add(r * 2 + f, v)
            if r == 0:
                item[f] = v.astype(BF16)
            if r == row_count - 1:
                if f == 0:
                    level = lax.broadcasted_iota(jnp.int32, v.shape, 0)
                    v = jnp.where(level == levels, match[0, 0].astype(F32), v)
                    v = jnp.where(level == levels + 1, turn[0, 0].astype(F32), v)
                item[2 + f] = v.astype(BF16)
    v = jnp.where(lane == MATCH, match[0, 0].astype(F32), columns.held)
    sides[...] = jnp.where(lane == TURN, turn[0, 0].astype(F32), v)


def tail(tile, levels):
    return tile[PAD - 8 : PAD, :].astype(F32)[levels - (PAD - 8) :, :]


def first_send_kernel(sizes, levels, where, mates, *outs):
    nz, ny, nc = sizes
    zl, y, c = where[0, 0], where[0, 1], where[0, 2]
    order = [(i, lax.rem(j + zl, nz)) for j in range(nz) for i in range(nc)]
    shape = mates.shape[3:]
    match = [jnp.broadcast_to(tail(mates[i, z, 2], levels)[0:1], shape) for i, z in order]
    first = [[mates[i, z, f].astype(F32) for f in range(2)] for i, z in order]
    for d, out in enumerate(outs):
        plane = lax.rem(jnp.where(c == 0, y + d, y - d + ny), ny)
        for m, (i, z) in enumerate(order):
            for f in range(2):
                out[2 * m + f] = mates[i, z, 2 + f]
        for core in range(nc):
            dest = ((zl * ny + plane) * nc + core).astype(F32)
            for f in range(2):
                v = first[0][f]
                for m in range(1, len(order)):
                    v = jnp.where(match[m] == dest, first[m][f], v)
                out[2 * (len(order) + core) + f] = v.astype(BF16)


def code_kernel(sizes, levels, where, own, edge, code, inverse):
    nz, ny, nc = sizes
    half = ny // 2
    lane = lanes(1, code.shape[1])
    codes = jnp.zeros(code.shape, F32)
    south = jnp.zeros(code.shape, jnp.int32)
    for d in range(ny):
        plane = lax.rem(where[0, 1] - d + ny, ny)
        for m in range(nz * nc):
            t = tail(own[2 * m] if d == 0 else edge[d - 1 if d <= half else half + ny - d - 1, 2 * m], levels)
            face = ((m // nc) * ny + plane) * nc + m % nc
            codes = jnp.where(lane == face, 2.0 * t[0:1] + t[1:2], codes)
            south = jnp.where(lane.astype(F32) == t[0:1], face, south)
    code[...] = codes.astype(jnp.int32)
    inverse[...] = south


def choose_kernel(sizes, levels, north_from, rows, code, inverse, where, gathered, out):
    _, ny, nc = sizes
    zl, c = where[0, 0], where[0, 2]
    if gathered.shape[1] > rows:
        corner = [gathered[m, rows].astype(F32) for m in range(gathered.shape[0])]
        shape = corner[0].shape
        lane = lanes(*shape)
        to = [[jnp.broadcast_to(tail(k, levels)[i : i + 1], shape) for i in range(2)] for k in corner]
    for d in range(ny):
        dest = (zl * ny + d) * nc + c
        for source, a, b in (
            (inverse[0, dest], 0, north_from),
            (lax.shift_right_logical(code[0, dest], 1), north_from, rows),
        ):
            group = (source // (ny * nc)) * nc + source % nc
            for i in range(a, b):
                out[d, i] = gathered[group, i]
        if gathered.shape[1] > rows:
            v = jnp.zeros(shape, F32)
            for k, both in zip(corner, to):
                for i in range(2):
                    hit = both[i] == dest.astype(F32)
                    v = jnp.where(hit & (lane == i), k, v)
                    v = jnp.where(hit & (lane == 2 + i), 1.0, v)
            out[d, rows] = v.astype(BF16)


def neighbours(sizes, code, inverse, where):
    _, ny, nc = sizes
    me = (where[0, 0] * ny + where[0, 1]) * nc + where[0, 2]
    south = inverse[0, me]
    found = []
    for face, turn in ((lax.shift_right_logical(code[0, me], 1), code[0, me] & 1), (south, code[0, south] & 1)):
        found += [(face // nc) % ny, (face // (ny * nc)) * nc + face % nc, turn]
    return found


def oriented(block, turn):
    n, rows, width = block.shape
    i = lax.broadcasted_iota(jnp.int32, (width, width), 0)
    j = lax.broadcasted_iota(jnp.int32, (width, width), 1)
    source = jnp.where(turn == 1, width - 1 - j, j)
    matrix = jnp.where(i == source, 1.0, 0.0).astype(BF16)
    out = jnp.dot(block.reshape(n * rows, width), matrix, preferred_element_type=F32)
    return out.reshape(n, rows, width)


def find_slots(levels, tiles, capacity, winds, found_out, found, sem, extras):
    block = winds.shape[0] // tiles
    extra = jnp.concatenate([winds[h * block + block - 1].astype(F32) for h in range(tiles)], axis=0)
    row = lax.broadcasted_iota(jnp.int32, extra.shape, 0)
    holder, at = lax.shift_right_logical(row, 3), row & 7
    lane = lanes(*extra.shape)
    here = (at < capacity) & (spread(extra, LABEL, extra.shape) == lane.astype(F32))
    there = (at < capacity) & (spread(extra, LABEL_EAST, extra.shape) == lane.astype(F32))
    sides = (at - capacity == lane - HALF) & (at >= capacity) & (at < capacity + 2)
    there = there | (sides & (spread(extra, extra.shape[1] - 1, extra.shape) > 0.5))
    place = (holder * block + at * (2 * levels // 8)).astype(F32)
    index = jnp.sum(jnp.where(here, place, 0.0), axis=0, keepdims=True)
    found_out[...] = index.astype(jnp.int32)
    copy = pltpu.make_async_copy(found_out, found, sem)
    copy.start()
    extras[...] = lax.dot_general(
        extra.astype(BF16), jnp.where(there, 1.0, 0.0).astype(BF16), (((0,), (0,)), ((), ())), preferred_element_type=F32
    )
    copy.wait()


def wind(levels, winds, found, unit, i):
    whole = levels // 8 * 8
    base = found[0, unit]
    rest = winds[base + 2 * whole // 8].astype(F32)
    if i == 1:
        rest = pltpu.roll(rest, 8 - (levels - whole), 0)
    main = winds[pl.ds(base + i * (whole // 8), whole // 8)].astype(F32).reshape(whole, rest.shape[1])
    return jnp.concatenate([main, rest], axis=0)


def advance(step, rows, levels, winds, found, east_wind, row, upper, lower, south_end, halo, put):
    row_count, width = ROWS, winds.shape[2]
    lane = lanes(PAD, width)
    base = step * row_count

    def of(r, i):
        return wind(levels, winds, found, base + r, i)

    south_wind, at = None, None
    for r in rows:
        west_wind = of(r, 0)
        north_wind = south_wind if at == r - 1 else of(r, 1)
        south_wind, at = (of(r + 1, 1) if r + 1 < row_count else south_end), r
        eastern_wind = jnp.where(
            lane == width - 1, spread(east_wind, base + r, lane.shape), pltpu.roll(west_wind, width - 1, 1)
        )
        cw = COURANT * jnp.minimum(west_wind, 0.0)
        ce = COURANT * jnp.maximum(eastern_wind, 0.0)
        cn = COURANT * jnp.minimum(north_wind, 0.0)
        if south_wind is not None:
            cs = COURANT * jnp.maximum(south_wind, 0.0)
        for f in range(2):
            q = r * 2 + f
            a = row(r, f)
            beside = pltpu.roll(halo, width - 1 - 2 * q, 1)
            west = jnp.where(lane == 0, beside, pltpu.roll(a, 1, 1))
            east = jnp.where(lane == width - 1, beside, pltpu.roll(a, width - 1, 1))
            v = a + cw * (a - west)
            v = v + ce * (east - a)
            v = v + cn * (a - (row(r - 1, f) if r > 0 else upper[f]))
            if south_wind is not None:
                v = v + cs * ((row(r + 1, f) if r + 1 < row_count else lower[f]) - a)
            put(r, f, v)


def prepare_kernel(sizes, code, inverse, where, own, edge, ends):
    mates = sizes[0] * sizes[2]
    north, north_mate, turn_north, south, _, turn_south = neighbours(sizes, code, inverse, where)
    y, c, ny = where[0, 1], where[0, 2], sizes[1]
    half = ny // 2

    def arrived(plane, row):
        d = lax.rem(y - plane + ny, ny)
        i = jnp.where(d <= half, jnp.maximum(d - 1, 0), half + ny - d - 1)
        both = own[pl.ds(row, 2)].astype(F32), edge[i, pl.ds(row, 2)].astype(F32)
        return jnp.where(d == 0, *both).astype(BF16)

    ends[0:2] = oriented(arrived(north, 2 * north_mate), turn_north)
    ends[2:4] = oriented(arrived(south, 2 * (mates + c)), turn_south)


def first_kernel(
    step, levels, tiles,
    winds, adj, ends, from_west, from_east,
    item, kept, found_out, east_wind,
    found, sem, extras,
):
    end, width = adj.shape[0] - 1, adj.shape[3]
    find_slots(levels, tiles, CAPACITY, winds, found_out, found, sem, extras)
    east_wind[...] = extras[0:PAD, :]
    halo = joined(from_west, from_east)
    upper = (ends[0], ends[1])

    def put(r, f, v):
        item[f if r == 0 else 4 + f] = v.astype(BF16)
        kept[(7 if r == 0 else 5) + f] = v

    def row(r, f):
        return adj[r, f]

    advance(step, (0, end), levels, winds, found, east_wind, row, upper, None, None, halo, put)
    edge_wind = wind(levels, winds, found, step * ROWS, 1)
    item[2] = edge_wind.astype(BF16)
    item[3] = wind(levels, winds, found, (step - 1) * ROWS, 1).astype(BF16)
    for f in range(2):
        kept[f] = ends[2 + f] - adj[end, f]
        kept[2 + f] = adj[0, f].astype(BF16).astype(F32) - upper[f]
    kept[4] = edge_wind

    shape = (PAD, width)
    lane, level = lanes(*shape), lax.broadcasted_iota(jnp.int32, shape, 0)
    head, last = extras[0:PAD, :], extras[HALF : HALF + PAD, :]
    turned_west = spread(from_west, TURN, shape) > 0.5
    turned_east = spread(from_east, TURN, shape) > 0.5
    west = jnp.where(turned_west, spread(head, HALF + 1, shape), spread(last, HALF + 1, shape))
    east = jnp.where(turned_east, spread(last, HALF, shape), spread(head, HALF, shape))
    v = jnp.where(lane == 0, west, jnp.where(lane == 1, east, 0.0))
    v = jnp.where(level == levels, spread(from_west, MATCH, shape), v)
    v = jnp.where(level == levels + 1, spread(from_east, MATCH, shape), v)
    item[6] = v.astype(BF16)


def inner_kernel(
    step, levels, opening, found, winds, adj, ends, from_west, from_east, east_wind, out, sides
):
    row_count, width = adj.shape[0], adj.shape[3]
    columns = Columns(width)
    first_at, last_at = (7, 5) if opening else (2, 4)

    def put(r, f, v):
        out[r, f] = v
        columns.add(2 * r + f, v)

    def row(r, f):
        return ends[f] if r == row_count - 1 and not opening else adj[r, f]

    rows = range(1, row_count - 1)
    advance(step, rows, levels, winds, found, east_wind, row, None, None, None, joined(from_west, from_east), put)
    for f in range(2):
        put(0, f, ends[first_at + f])
        put(row_count - 1, f, ends[last_at + f])
    if opening:
        for f in range(2):
            columns.add(EDGE_COLUMN + f, ends[f])
    sides[...] = columns.held


def middle_kernel(
    step, levels, sizes,
    code, inverse, where, found, winds, adj, edge, kept, from_west, from_east, east_wind,
    item, both,
):
    end = adj.shape[0] - 1
    north, _, turn_north, south, _, turn_south = neighbours(sizes, code, inverse, where)
    lower = oriented(edge[south, 0:4], turn_south)
    upper = oriented(edge[north, 4:6], turn_north)
    cs = COURANT * jnp.maximum(lower[2], 0.0)
    final = [kept[5 + f] + cs * kept[f] for f in range(2)]
    cs = COURANT * jnp.maximum(kept[4], 0.0)
    northern = []
    for f in range(2):
        v = upper[f] + cs * kept[2 + f]
        northern.append(v.astype(BF16).astype(F32))
    shape = final[0].shape
    lane = lanes(*shape)
    sides = []
    for i, columns in enumerate((from_west[...], from_east[...])):
        corner = jnp.zeros(shape, F32)
        for d in range(sizes[1]):
            k = edge[d, 6].astype(F32)
            corner = jnp.where(spread(k, 2 + i, shape) > 0.5, spread(k, i, shape), corner)
        cs = COURANT * jnp.maximum(corner, 0.0)
        mended = columns
        for f in range(2):
            change = cs * spread(columns, 2 * (EDGE_COLUMN + f) + i, shape)
            mended = jnp.where(lane == 2 * (2 * end + f) + i, columns + change, mended)
        sides.append(mended)

    def put(r, f, v):
        item[f if r == 0 else 3 + f] = v.astype(BF16)
        both[(2 if r == 0 else 4) + f] = v

    def row(r, f):
        return final[f] if r == end else adj[r, f]

    advance(step, (0, end), levels, winds, found, east_wind, row, northern, lower, lower[3], joined(*sides), put)
    both[0] = final[0]
    both[1] = final[1]
    item[2] = wind(levels, winds, found, (step - 1) * ROWS, 1).astype(BF16)


def last_kernel(
    step, levels, sizes, code, inverse, where, found, winds, adj, edge, from_east, from_west, east_wind, out
):
    north, _, turn_north, south, _, turn_south = neighbours(sizes, code, inverse, where)
    upper = oriented(edge[north, 3:5], turn_north)
    lower = oriented(edge[south, 0:3], turn_south)

    def put(r, f, v):
        for l0 in range(0, levels, 8):
            n = min(8, levels - l0)
            out[pl.ds((f * levels + l0) * ROWS + r, n, stride=ROWS), :] = v[l0 : l0 + n]

    def row(r, f):
        return adj[r, f]

    halo = joined(from_west, from_east)
    advance(step, range(ROWS), levels, winds, found, east_wind, row, upper, lower, lower[2], halo, put)


def shards(sizes, tile_sizes, adjoint_end, stored_rows, stored_owner, stored_unit, stored_valid, edge_match, edge_turn):
    face, tile, group = ("zl", "y", "c"), ("x", "zh"), ("zl", "c")
    faces = sizes[0] * sizes[1] * sizes[2]
    tiles = tile_sizes[0] * tile_sizes[1]
    levels, row_count, width = adjoint_end.shape[1:]
    slots = stored_rows.shape[1]
    sds = jax.ShapeDtypeStruct
    side = sds((PAD, width), F32)

    where = jnp.stack([lax.axis_index(a) for a in face]).astype(jnp.int32).reshape(1, 3)
    block = CAPACITY * 2 * levels // 8 + 1
    payload = call(
        functools.partial(pack_kernel, levels, tiles, (STEPS - 1) * row_count),
        sds((tiles * block, 8, width), BF16),
        [SM, SM, SM, HBM],
        HBM,
        [
            pltpu.SMEM((tiles,), jnp.int32),
            pltpu.SMEM((slots + 1,), jnp.int32),
            pltpu.SMEM((slots + 1,), jnp.int32),
            pltpu.SMEM((tiles + 1,), jnp.int32),
            pltpu.VMEM((width, width), F32),
            pltpu.VMEM((width, width), F32),
            pltpu.VMEM(stored_rows.shape[1:], BF16),
            pltpu.VMEM((tiles * block, 8, width), BF16),
            pltpu.SemaphoreType.DMA,
            pltpu.SemaphoreType.DMA((CHUNKS,)),
        ],
        61 << 20,
    )(stored_owner, stored_unit, stored_valid, stored_rows[0])

    turned, item, sides = call(
        functools.partial(edges_kernel, levels, row_count),
        (sds((row_count, 2, PAD, width), F32), sds((4, PAD, width), BF16), side),
        [SM, SM, VM],
        (VM,) * 3,
    )(edge_match, edge_turn, adjoint_end.reshape(2 * levels * row_count, width))

    planes, mates = sizes[1], sizes[0] * sizes[2]

    def to_sides(sides):
        ahead = [(i, (i + 1) % tiles) for i in range(tiles)]
        back = [((i + 1) % tiles, i) for i in range(tiles)]
        return lax.ppermute(sides, tile, ahead), lax.ppermute(sides, tile, back)

    def exchange(item, north_from, rows):
        gathered = lax.all_gather(item, group, axis=0, tiled=False)
        chosen = call(
            functools.partial(choose_kernel, sizes, levels, north_from, rows),
            sds((planes,) + item.shape, BF16),
            [SM, SM, SM, VM],
            VM,
        )(code, inverse, where, gathered)
        return lax.all_to_all(chosen, "y", 0, 0, tiled=True)

    other = lax.ppermute(item, "zl", [(i, (i + 1) % sizes[0]) for i in range(sizes[0])])
    payload, other = lax.optimization_barrier((payload, other))
    winds = lax.all_to_all(payload, tile, 0, 0, tiled=True)
    from_west, from_east = to_sides(sides)
    near = lax.all_gather(jnp.stack([item, other]), "c", axis=0, tiled=False)
    half, cores = planes // 2, sizes[2]
    own, *parts = call(
        functools.partial(first_send_kernel, sizes, levels),
        (sds((2 * (mates + cores), PAD, width), BF16),) * (half + 1),
        [SM, VM],
        (VM,) * (half + 1),
    )(where, near)
    moved = []
    for d, part in enumerate(parts, 1):
        ways = [(c, d if c == 0 else -d) for c in range(cores) if c == 0 or d < half]
        route = [(y * cores + c, (y + way) % planes * cores + c) for y in range(planes) for c, way in ways]
        moved.append(lax.ppermute(part, ("y", "c"), route))
    edge = lax.all_gather(jnp.stack(moved), "c", axis=0, tiled=True)
    table = sds((1, width), jnp.int32)
    code, inverse = call(
        functools.partial(code_kernel, sizes, levels), (table, table), [SM, VM, VM], (VM, VM)
    )(where, own, edge)

    ends = call(
        functools.partial(prepare_kernel, sizes), sds((4, PAD, width), F32), [SM, SM, SM, VM, VM], VM
    )(code, inverse, where, own, edge)

    item, kept, found, east_wind = call(
        functools.partial(first_kernel, STEPS - 1, levels, tiles),
        (sds((7, PAD, width), BF16), sds((9, PAD, width), F32), table, side),
        [VM] * 5,
        (VM,) * 4,
        [pltpu.SMEM((1, width), jnp.int32), pltpu.SemaphoreType.DMA, pltpu.VMEM((width, width), F32)],
    )(winds, turned, ends, from_west, from_east)
    edge = exchange(item, 4, 6)

    def inner(step, opening, adj, ends):
        return call(
            functools.partial(inner_kernel, step, levels, opening),
            (sds(turned.shape, F32), side),
            [SM] + [VM] * 6,
            (VM,) * 2,
        )(found, winds, adj, ends, from_west, from_east, east_wind)

    adj, sides = inner(STEPS - 1, True, turned, kept)
    from_west, from_east = to_sides(sides)
    item, both = call(
        functools.partial(middle_kernel, STEPS - 2, levels, sizes),
        (sds((5, PAD, width), BF16), sds((6, PAD, width), F32)),
        [SM] * 4 + [VM] * 7,
        (VM,) * 2,
    )(code, inverse, where, found, winds, adj, edge, kept, from_west, from_east, east_wind)
    edge = exchange(item, 3, 5)
    adj, sides = inner(STEPS - 2, False, adj, both)

    from_west, from_east = to_sides(sides)
    out = call(
        functools.partial(last_kernel, STEPS - 3, levels, sizes),
        sds((2 * levels * row_count, width), F32),
        [SM] * 4 + [VM] * 6,
        VM,
    )(code, inverse, where, found, winds, adj, edge, from_east, from_west, east_wind)
    return out.reshape(adjoint_end.shape)


def solution(mesh, sizes=(2, 8, 2), tile_sizes=(8, 4)):
    fine = Mesh(mesh.devices.reshape(sizes + tile_sizes), ("zl", "y", "c", "x", "zh"))
    face, tile = ("zl", "y", "c"), ("x", "zh")
    placed = (
        P(None, None, face, tile),
        P(face, tile, None, None, None),
        P(face, tile),
        P(face, tile),
        P(face, tile),
        P(face, tile),
        P(face, tile),
    )
    return jax.shard_map(
        functools.partial(shards, sizes, tile_sizes),
        mesh=fine,
        in_specs=placed,
        out_specs=P(None, None, face, tile),
        check_vma=False,
    )
```

```python
import functools

import jax
import jax.numpy as jnp
from jax import lax
from jax.experimental import pallas as pl
from jax.experimental.pallas import tpu as pltpu
from jax.sharding import Mesh
from jax.sharding import PartitionSpec as P

STEPS = 3
ROWS = 16
CAPACITY = 3
COURANT = 0.2
PAD = 40
LABEL, LABEL_EAST = 64, 65
CHUNKS = 8
HALF = 64
MATCH, TURN = 96, 97
EDGE_COLUMN = 32
INTERPRET = False

VM = pl.BlockSpec(memory_space=pltpu.VMEM)
SM = pl.BlockSpec(memory_space=pltpu.SMEM)
HBM = pl.BlockSpec(memory_space=pltpu.HBM)
F32, BF16 = jnp.float32, jnp.bfloat16


def call(kernel, out_shape, in_specs, out_specs, scratch=(), vmem=24 << 20):
    return pl.pallas_call(
        kernel,
        out_shape=out_shape,
        in_specs=in_specs,
        out_specs=out_specs,
        scratch_shapes=list(scratch),
        compiler_params=pltpu.CompilerParams(vmem_limit_bytes=vmem),
        cost_estimate=pl.CostEstimate(flops=1 << 20, bytes_accessed=1 << 20, transcendentals=0),
        interpret=INTERPRET,
    )


def lanes(rows, width):
    return lax.broadcasted_iota(jnp.int32, (rows, width), 1)


def spread(values, lane, shape):
    return jnp.broadcast_to(values[:, lane : lane + 1], shape)


def pack_kernel(
    levels, tiles, edge_unit, owner, unit, valid, stored, sent, count, source, label, first, flat, corner, rows, out, sem_in, sem_out
):
    fetch = pltpu.make_async_copy(stored, rows, sem_in)
    fetch.start()
    slots, width = rows.shape[0], rows.shape[3]
    capacity = slots // tiles
    block = out.shape[0] // tiles
    whole = levels // 8 * 8

    def clear(i, c):
        count[i] = 0
        first[i] = -1
        return c

    lax.fori_loop(0, tiles, clear, 0, unroll=8)

    def blank(i, c):
        source[i] = 0
        label[i] = -1
        return c

    lax.fori_loop(0, slots, blank, 0, unroll=8)

    def place(s, c):
        o, u, v = owner[0, s], unit[0, s], valid[0, s]
        have = count[o]
        p = jnp.where(v == 1, o * capacity + have, slots)
        source[p] = s
        label[p] = u
        count[o] = have + v
        first[jnp.where((v == 1) & (u == edge_unit), o, tiles)] = s
        return c

    lax.fori_loop(0, slots, place, 0, unroll=8)
    fetch.wait()

    lane = lanes(levels, width)

    def column(s, held):
        v = rows[s, 0].astype(F32)
        return jnp.where(lane == s, spread(v, 0, v.shape), held)

    def corners(o, held):
        v = rows[jnp.maximum(first[o], 0), 1].astype(F32)
        held = jnp.where(lane == o, spread(v, 0, v.shape), held)
        return jnp.where(lane == tiles + o, spread(v, width - 1, v.shape), held)

    for ref, one, n in ((flat, column, slots), (corner, corners, tiles)):
        held = lax.fori_loop(0, n, one, jnp.zeros((levels, width), F32), unroll=8)
        ref[...] = jnp.zeros_like(ref)
        ref[0:levels, :] = held
        ref[...] = ref[...].T

    extra_lane = lanes(8, width)
    extra_row = lax.broadcasted_iota(jnp.int32, (8, width), 0)

    def at(ref, i):
        return jnp.broadcast_to(ref[pl.ds(i, 1), :], (8, width))

    def fill(o, c):
        base = o * block
        east = jnp.where(o + 1 == tiles, 0, o + 1)
        west = jnp.where(o == 0, tiles - 1, o - 1)
        extra = jnp.zeros((8, width), F32)
        for i in range(capacity):
            p, q = o * capacity + i, east * capacity + i
            s = source[p]
            at_slot = base + i * (2 * levels // 8)
            for j in range(2):
                for k in range(whole // 8):
                    out[at_slot + j * (whole // 8) + k] = rows[s, j, 8 * k : 8 * k + 8]
            rest = [rows[s, j, whole:levels].astype(F32) for j in range(2)]
            out[at_slot + 2 * whole // 8] = jnp.concatenate(rest, axis=0).astype(BF16)
            line = at(flat, source[q])
            line = jnp.where(extra_lane == LABEL, label[p].astype(F32), line)
            line = jnp.where(extra_lane == LABEL_EAST, label[q].astype(F32), line)
            extra = jnp.where(extra_row == i, line, extra)
        for i, side in ((capacity, east), (capacity + 1, west)):
            line = jnp.where(extra_lane < HALF, at(corner, side), pltpu.roll(at(corner, tiles + side), HALF, 1))
            line = jnp.where(extra_lane == width - 1, jnp.where(first[side] >= 0, 1.0, 0.0), line)
            extra = jnp.where(extra_row == i, line, extra)
        out[base + block - 1] = extra.astype(BF16)
        return c

    chunk = tiles // CHUNKS
    copies = []
    for i in range(CHUNKS):
        lax.fori_loop(i * chunk, (i + 1) * chunk, fill, 0, unroll=4)
        span = pl.ds(i * chunk * block, chunk * block)
        copies.append(pltpu.make_async_copy(out.at[span], sent.at[span], sem_out.at[i]))
        copies[-1].start()
    for copy in copies:
        copy.wait()


class Columns:
    def __init__(self, width):
        self.pair = lax.shift_right_logical(lanes(PAD, width), 1)
        self.held = jnp.zeros((PAD, width), F32)

    def add(self, q, v):
        self.held = jnp.where(self.pair == q, pltpu.roll(v, 2 * q + 1, 1), self.held)


def joined(from_west, from_east):
    shape = from_west.shape
    even = (lanes(*shape) & 1) == 0
    return jnp.where(even, pltpu.roll(from_east[...], shape[1] - 1, 1), pltpu.roll(from_west[...], 1, 1))


def edges_kernel(levels, row_count, match, turn, adj, turned, item, sides):
    width = adj.shape[1]
    lane = lanes(PAD, width)
    columns = Columns(width)
    for r in range(row_count):
        for f in range(2):
            for l0 in range(0, levels, 8):
                n = min(8, levels - l0)
                turned[r, f, l0 : l0 + n, :] = adj[pl.ds((f * levels + l0) * row_count + r, n, stride=row_count), :]
            turned[r, f, levels:PAD, :] = jnp.zeros((PAD - levels, width), F32)
            v = turned[r, f]
            columns.add(r * 2 + f, v)
            if r == 0:
                item[f] = v.astype(BF16)
            if r == row_count - 1:
                if f == 0:
                    level = lax.broadcasted_iota(jnp.int32, v.shape, 0)
                    v = jnp.where(level == levels, match[0, 0].astype(F32), v)
                    v = jnp.where(level == levels + 1, turn[0, 0].astype(F32), v)
                item[2 + f] = v.astype(BF16)
    v = jnp.where(lane == MATCH, match[0, 0].astype(F32), columns.held)
    sides[...] = jnp.where(lane == TURN, turn[0, 0].astype(F32), v)


def tail(tile, levels):
    return tile[PAD - 8 : PAD, :].astype(F32)[levels - (PAD - 8) :, :]


def first_send_kernel(sizes, levels, where, mates, *outs):
    nz, ny, nc = sizes
    zl, y, c = where[0, 0], where[0, 1], where[0, 2]
    order = [(i, lax.rem(j + zl, nz)) for j in range(nz) for i in range(nc)]
    shape = mates.shape[3:]
    match = [jnp.broadcast_to(tail(mates[i, z, 2], levels)[0:1], shape) for i, z in order]
    first = [[mates[i, z, f].astype(F32) for f in range(2)] for i, z in order]
    for d, out in enumerate(outs):
        plane = lax.rem(jnp.where(c == 0, y + d, y - d + ny), ny)
        for m, (i, z) in enumerate(order):
            for f in range(2):
                out[2 * m + f] = mates[i, z, 2 + f]
        for core in range(nc):
            dest = ((zl * ny + plane) * nc + core).astype(F32)
            for f in range(2):
                v = first[0][f]
                for m in range(1, len(order)):
                    v = jnp.where(match[m] == dest, first[m][f], v)
                out[2 * (len(order) + core) + f] = v.astype(BF16)


def code_kernel(sizes, levels, where, own, edge, code, inverse):
    nz, ny, nc = sizes
    half = ny // 2
    lane = lanes(1, code.shape[1])
    codes = jnp.zeros(code.shape, F32)
    south = jnp.zeros(code.shape, jnp.int32)
    for d in range(ny):
        plane = lax.rem(where[0, 1] - d + ny, ny)
        for m in range(nz * nc):
            t = tail(own[2 * m] if d == 0 else edge[d - 1 if d <= half else half + ny - d - 1, 2 * m], levels)
            face = ((m // nc) * ny + plane) * nc + m % nc
            codes = jnp.where(lane == face, 2.0 * t[0:1] + t[1:2], codes)
            south = jnp.where(lane.astype(F32) == t[0:1], face, south)
    code[...] = codes.astype(jnp.int32)
    inverse[...] = south


def choose_kernel(sizes, levels, north_from, rows, code, inverse, where, gathered, out):
    _, ny, nc = sizes
    zl, c = where[0, 0], where[0, 2]
    if gathered.shape[1] > rows:
        corner = [gathered[m, rows].astype(F32) for m in range(gathered.shape[0])]
        shape = corner[0].shape
        lane = lanes(*shape)
        to = [[jnp.broadcast_to(tail(k, levels)[i : i + 1], shape) for i in range(2)] for k in corner]
    for d in range(ny):
        dest = (zl * ny + d) * nc + c
        for source, a, b in (
            (inverse[0, dest], 0, north_from),
            (lax.shift_right_logical(code[0, dest], 1), north_from, rows),
        ):
            group = (source // (ny * nc)) * nc + source % nc
            for i in range(a, b):
                out[d, i] = gathered[group, i]
        if gathered.shape[1] > rows:
            v = jnp.zeros(shape, F32)
            for k, both in zip(corner, to):
                for i in range(2):
                    hit = both[i] == dest.astype(F32)
                    v = jnp.where(hit & (lane == i), k, v)
                    v = jnp.where(hit & (lane == 2 + i), 1.0, v)
            out[d, rows] = v.astype(BF16)


def neighbours(sizes, code, inverse, where):
    _, ny, nc = sizes
    me = (where[0, 0] * ny + where[0, 1]) * nc + where[0, 2]
    south = inverse[0, me]
    found = []
    for face, turn in ((lax.shift_right_logical(code[0, me], 1), code[0, me] & 1), (south, code[0, south] & 1)):
        found += [(face // nc) % ny, (face // (ny * nc)) * nc + face % nc, turn]
    return found


def oriented(block, turn):
    n, rows, width = block.shape
    i = lax.broadcasted_iota(jnp.int32, (width, width), 0)
    j = lax.broadcasted_iota(jnp.int32, (width, width), 1)
    source = jnp.where(turn == 1, width - 1 - j, j)
    matrix = jnp.where(i == source, 1.0, 0.0).astype(BF16)
    out = jnp.dot(block.reshape(n * rows, width), matrix, preferred_element_type=F32)
    return out.reshape(n, rows, width)


def find_slots(levels, tiles, capacity, winds, found_out, found, sem, extras):
    block = winds.shape[0] // tiles
    extra = jnp.concatenate([winds[h * block + block - 1].astype(F32) for h in range(tiles)], axis=0)
    row = lax.broadcasted_iota(jnp.int32, extra.shape, 0)
    holder, at = lax.shift_right_logical(row, 3), row & 7
    lane = lanes(*extra.shape)
    here = (at < capacity) & (spread(extra, LABEL, extra.shape) == lane.astype(F32))
    there = (at < capacity) & (spread(extra, LABEL_EAST, extra.shape) == lane.astype(F32))
    sides = (at - capacity == lane - HALF) & (at >= capacity) & (at < capacity + 2)
    there = there | (sides & (spread(extra, extra.shape[1] - 1, extra.shape) > 0.5))
    place = (holder * block + at * (2 * levels // 8)).astype(F32)
    index = jnp.sum(jnp.where(here, place, 0.0), axis=0, keepdims=True)
    found_out[...] = index.astype(jnp.int32)
    copy = pltpu.make_async_copy(found_out, found, sem)
    copy.start()
    extras[...] = lax.dot_general(
        extra.astype(BF16), jnp.where(there, 1.0, 0.0).astype(BF16), (((0,), (0,)), ((), ())), preferred_element_type=F32
    )
    copy.wait()


def wind(levels, winds, found, unit, i):
    whole = levels // 8 * 8
    base = found[0, unit]
    rest = winds[base + 2 * whole // 8].astype(F32)
    if i == 1:
        rest = pltpu.roll(rest, 8 - (levels - whole), 0)
    main = winds[pl.ds(base + i * (whole // 8), whole // 8)].astype(F32).reshape(whole, rest.shape[1])
    return jnp.concatenate([main, rest], axis=0)


def advance(step, rows, levels, winds, found, east_wind, row, upper, lower, south_end, halo, put):
    row_count, width = ROWS, winds.shape[2]
    lane = lanes(PAD, width)
    base = step * row_count

    def of(r, i):
        return wind(levels, winds, found, base + r, i)

    south_wind, at = None, None
    for r in rows:
        west_wind = of(r, 0)
        north_wind = south_wind if at == r - 1 else of(r, 1)
        south_wind, at = (of(r + 1, 1) if r + 1 < row_count else south_end), r
        eastern_wind = jnp.where(
            lane == width - 1, spread(east_wind, base + r, lane.shape), pltpu.roll(west_wind, width - 1, 1)
        )
        cw = COURANT * jnp.minimum(west_wind, 0.0)
        ce = COURANT * jnp.maximum(eastern_wind, 0.0)
        cn = COURANT * jnp.minimum(north_wind, 0.0)
        if south_wind is not None:
            cs = COURANT * jnp.maximum(south_wind, 0.0)
        for f in range(2):
            q = r * 2 + f
            a = row(r, f)
            beside = pltpu.roll(halo, width - 1 - 2 * q, 1)
            west = jnp.where(lane == 0, beside, pltpu.roll(a, 1, 1))
            east = jnp.where(lane == width - 1, beside, pltpu.roll(a, width - 1, 1))
            v = a + cw * (a - west)
            v = v + ce * (east - a)
            v = v + cn * (a - (row(r - 1, f) if r > 0 else upper[f]))
            if south_wind is not None:
                v = v + cs * ((row(r + 1, f) if r + 1 < row_count else lower[f]) - a)
            put(r, f, v)


def prepare_kernel(sizes, code, inverse, where, own, edge, ends):
    mates = sizes[0] * sizes[2]
    north, north_mate, turn_north, south, _, turn_south = neighbours(sizes, code, inverse, where)
    y, c, ny = where[0, 1], where[0, 2], sizes[1]
    half = ny // 2

    def arrived(plane, row):
        d = lax.rem(y - plane + ny, ny)
        i = jnp.where(d <= half, jnp.maximum(d - 1, 0), half + ny - d - 1)
        both = own[pl.ds(row, 2)].astype(F32), edge[i, pl.ds(row, 2)].astype(F32)
        return jnp.where(d == 0, *both).astype(BF16)

    ends[0:2] = oriented(arrived(north, 2 * north_mate), turn_north)
    ends[2:4] = oriented(arrived(south, 2 * (mates + c)), turn_south)


def first_kernel(
    step, levels, tiles,
    winds, adj, ends, from_west, from_east,
    item, kept, found_out, east_wind,
    found, sem, extras,
):
    end, width = adj.shape[0] - 1, adj.shape[3]
    find_slots(levels, tiles, CAPACITY, winds, found_out, found, sem, extras)
    east_wind[...] = extras[0:PAD, :]
    halo = joined(from_west, from_east)
    upper = (ends[0], ends[1])

    def put(r, f, v):
        item[f if r == 0 else 4 + f] = v.astype(BF16)
        kept[(7 if r == 0 else 5) + f] = v

    def row(r, f):
        return adj[r, f]

    advance(step, (0, end), levels, winds, found, east_wind, row, upper, None, None, halo, put)
    edge_wind = wind(levels, winds, found, step * ROWS, 1)
    item[2] = edge_wind.astype(BF16)
    item[3] = wind(levels, winds, found, (step - 1) * ROWS, 1).astype(BF16)
    for f in range(2):
        kept[f] = ends[2 + f] - adj[end, f]
        kept[2 + f] = adj[0, f].astype(BF16).astype(F32) - upper[f]
    kept[4] = edge_wind

    shape = (PAD, width)
    lane, level = lanes(*shape), lax.broadcasted_iota(jnp.int32, shape, 0)
    head, last = extras[0:PAD, :], extras[HALF : HALF + PAD, :]
    turned_west = spread(from_west, TURN, shape) > 0.5
    turned_east = spread(from_east, TURN, shape) > 0.5
    west = jnp.where(turned_west, spread(head, HALF + 1, shape), spread(last, HALF + 1, shape))
    east = jnp.where(turned_east, spread(last, HALF, shape), spread(head, HALF, shape))
    v = jnp.where(lane == 0, west, jnp.where(lane == 1, east, 0.0))
    v = jnp.where(level == levels, spread(from_west, MATCH, shape), v)
    v = jnp.where(level == levels + 1, spread(from_east, MATCH, shape), v)
    item[6] = v.astype(BF16)


def inner_kernel(
    step, levels, opening, found, winds, adj, ends, from_west, from_east, east_wind, out, sides
):
    row_count, width = adj.shape[0], adj.shape[3]
    columns = Columns(width)
    first_at, last_at = (7, 5) if opening else (2, 4)

    def put(r, f, v):
        out[r, f] = v
        columns.add(2 * r + f, v)

    def row(r, f):
        return ends[f] if r == row_count - 1 and not opening else adj[r, f]

    rows = range(1, row_count - 1)
    advance(step, rows, levels, winds, found, east_wind, row, None, None, None, joined(from_west, from_east), put)
    for f in range(2):
        put(0, f, ends[first_at + f])
        put(row_count - 1, f, ends[last_at + f])
    if opening:
        for f in range(2):
            columns.add(EDGE_COLUMN + f, ends[f])
    sides[...] = columns.held


def middle_kernel(
    step, levels, sizes,
    code, inverse, where, found, winds, adj, edge, kept, from_west, from_east, east_wind,
    item, both,
):
    end = adj.shape[0] - 1
    north, _, turn_north, south, _, turn_south = neighbours(sizes, code, inverse, where)
    lower = oriented(edge[south, 0:4], turn_south)
    upper = oriented(edge[north, 4:6], turn_north)
    cs = COURANT * jnp.maximum(lower[2], 0.0)
    final = [kept[5 + f] + cs * kept[f] for f in range(2)]
    cs = COURANT * jnp.maximum(kept[4], 0.0)
    northern = []
    for f in range(2):
        v = upper[f] + cs * kept[2 + f]
        northern.append(v.astype(BF16).astype(F32))
    shape = final[0].shape
    lane = lanes(*shape)
    sides = []
    for i, columns in enumerate((from_west[...], from_east[...])):
        corner = jnp.zeros(shape, F32)
        for d in range(sizes[1]):
            k = edge[d, 6].astype(F32)
            corner = jnp.where(spread(k, 2 + i, shape) > 0.5, spread(k, i, shape), corner)
        cs = COURANT * jnp.maximum(corner, 0.0)
        mended = columns
        for f in range(2):
            change = cs * spread(columns, 2 * (EDGE_COLUMN + f) + i, shape)
            mended = jnp.where(lane == 2 * (2 * end + f) + i, columns + change, mended)
        sides.append(mended)

    def put(r, f, v):
        item[f if r == 0 else 3 + f] = v.astype(BF16)
        both[(2 if r == 0 else 4) + f] = v

    def row(r, f):
        return final[f] if r == end else adj[r, f]

    advance(step, (0, end), levels, winds, found, east_wind, row, northern, lower, lower[3], joined(*sides), put)
    both[0] = final[0]
    both[1] = final[1]
    item[2] = wind(levels, winds, found, (step - 1) * ROWS, 1).astype(BF16)


def last_kernel(
    step, levels, sizes, code, inverse, where, found, winds, adj, edge, from_east, from_west, east_wind, out
):
    north, _, turn_north, south, _, turn_south = neighbours(sizes, code, inverse, where)
    upper = oriented(edge[north, 3:5], turn_north)
    lower = oriented(edge[south, 0:3], turn_south)

    def put(r, f, v):
        for l0 in range(0, levels, 8):
            n = min(8, levels - l0)
            out[pl.ds((f * levels + l0) * ROWS + r, n, stride=ROWS), :] = v[l0 : l0 + n]

    def row(r, f):
        return adj[r, f]

    halo = joined(from_west, from_east)
    advance(step, range(ROWS), levels, winds, found, east_wind, row, upper, lower, lower[2], halo, put)


def shards(sizes, tile_sizes, adjoint_end, stored_rows, stored_owner, stored_unit, stored_valid, edge_match, edge_turn):
    face, tile, group = ("zl", "y", "c"), ("x", "zh"), ("zl", "c")
    faces = sizes[0] * sizes[1] * sizes[2]
    tiles = tile_sizes[0] * tile_sizes[1]
    levels, row_count, width = adjoint_end.shape[1:]
    slots = stored_rows.shape[1]
    sds = jax.ShapeDtypeStruct
    side = sds((PAD, width), F32)

    where = jnp.stack([lax.axis_index(a) for a in face]).astype(jnp.int32).reshape(1, 3)
    block = CAPACITY * 2 * levels // 8 + 1
    payload = call(
        functools.partial(pack_kernel, levels, tiles, (STEPS - 1) * row_count),
        sds((tiles * block, 8, width), BF16),
        [SM, SM, SM, HBM],
        HBM,
        [
            pltpu.SMEM((tiles,), jnp.int32),
            pltpu.SMEM((slots + 1,), jnp.int32),
            pltpu.SMEM((slots + 1,), jnp.int32),
            pltpu.SMEM((tiles + 1,), jnp.int32),
            pltpu.VMEM((width, width), F32),
            pltpu.VMEM((width, width), F32),
            pltpu.VMEM(stored_rows.shape[1:], BF16),
            pltpu.VMEM((tiles * block, 8, width), BF16),
            pltpu.SemaphoreType.DMA,
            pltpu.SemaphoreType.DMA((CHUNKS,)),
        ],
        61 << 20,
    )(stored_owner, stored_unit, stored_valid, stored_rows[0])

    turned, item, sides = call(
        functools.partial(edges_kernel, levels, row_count),
        (sds((row_count, 2, PAD, width), F32), sds((4, PAD, width), BF16), side),
        [SM, SM, VM],
        (VM,) * 3,
    )(edge_match, edge_turn, adjoint_end.reshape(2 * levels * row_count, width))

    planes, mates = sizes[1], sizes[0] * sizes[2]

    def to_sides(sides):
        ahead = [(i, (i + 1) % tiles) for i in range(tiles)]
        back = [((i + 1) % tiles, i) for i in range(tiles)]
        return lax.ppermute(sides, tile, ahead), lax.ppermute(sides, tile, back)

    def exchange(item, north_from, rows):
        gathered = lax.all_gather(item, group, axis=0, tiled=False)
        chosen = call(
            functools.partial(choose_kernel, sizes, levels, north_from, rows),
            sds((planes,) + item.shape, BF16),
            [SM, SM, SM, VM],
            VM,
        )(code, inverse, where, gathered)
        return lax.all_to_all(chosen, "y", 0, 0, tiled=True)

    other = lax.ppermute(item, "zl", [(i, (i + 1) % sizes[0]) for i in range(sizes[0])])
    payload, other = lax.optimization_barrier((payload, other))
    winds = lax.all_to_all(payload, tile, 0, 0, tiled=True)
    from_west, from_east = to_sides(sides)
    near = lax.all_gather(jnp.stack([item, other]), "c", axis=0, tiled=False)
    half, cores = planes // 2, sizes[2]
    own, *parts = call(
        functools.partial(first_send_kernel, sizes, levels),
        (sds((2 * (mates + cores), PAD, width), BF16),) * (half + 1),
        [SM, VM],
        (VM,) * (half + 1),
    )(where, near)
    moved = []
    for d, part in enumerate(parts, 1):
        ways = [(c, d if c == 0 else -d) for c in range(cores) if c == 0 or d < half]
        route = [(y * cores + c, (y + way) % planes * cores + c) for y in range(planes) for c, way in ways]
        moved.append(lax.ppermute(part, ("y", "c"), route))
    edge = lax.all_gather(jnp.stack(moved), "c", axis=0, tiled=True)
    table = sds((1, width), jnp.int32)
    code, inverse = call(
        functools.partial(code_kernel, sizes, levels), (table, table), [SM, VM, VM], (VM, VM)
    )(where, own, edge)

    ends = call(
        functools.partial(prepare_kernel, sizes), sds((4, PAD, width), F32), [SM, SM, SM, VM, VM], VM
    )(code, inverse, where, own, edge)

    item, kept, found, east_wind = call(
        functools.partial(first_kernel, STEPS - 1, levels, tiles),
        (sds((7, PAD, width), BF16), sds((9, PAD, width), F32), table, side),
        [VM] * 5,
        (VM,) * 4,
        [pltpu.SMEM((1, width), jnp.int32), pltpu.SemaphoreType.DMA, pltpu.VMEM((width, width), F32)],
    )(winds, turned, ends, from_west, from_east)
    edge = exchange(item, 4, 6)

    def inner(step, opening, adj, ends):
        return call(
            functools.partial(inner_kernel, step, levels, opening),
            (sds(turned.shape, F32), side),
            [SM] + [VM] * 6,
            (VM,) * 2,
        )(found, winds, adj, ends, from_west, from_east, east_wind)

    adj, sides = inner(STEPS - 1, True, turned, kept)
    from_west, from_east = to_sides(sides)
    item, both = call(
        functools.partial(middle_kernel, STEPS - 2, levels, sizes),
        (sds((5, PAD, width), BF16), sds((6, PAD, width), F32)),
        [SM] * 4 + [VM] * 7,
        (VM,) * 2,
    )(code, inverse, where, found, winds, adj, edge, kept, from_west, from_east, east_wind)
    edge = exchange(item, 3, 5)
    adj, sides = inner(STEPS - 2, False, adj, both)

    from_west, from_east = to_sides(sides)
    out = call(
        functools.partial(last_kernel, STEPS - 3, levels, sizes),
        sds((2 * levels * row_count, width), F32),
        [SM] * 4 + [VM] * 6,
        VM,
    )(code, inverse, where, found, winds, adj, edge, from_east, from_west, east_wind)
    return out.reshape(adjoint_end.shape)


def solution(mesh, sizes=(2, 8, 2), tile_sizes=(8, 4)):
    fine = Mesh(mesh.devices.reshape(sizes + tile_sizes), ("zl", "y", "c", "x", "zh"))
    face, tile = ("zl", "y", "c"), ("x", "zh")
    placed = (
        P(None, None, face, tile),
        P(face, tile, None, None, None),
        P(face, tile),
        P(face, tile),
        P(face, tile),
        P(face, tile),
        P(face, tile),
    )
    return jax.shard_map(
        functools.partial(shards, sizes, tile_sizes),
        mesh=fine,
        in_specs=placed,
        out_specs=P(None, None, face, tile),
        check_vma=False,
    )
```
